32 devices in a mesh: section: 2 (over y), dp: 16 (over z, x, core).
Axes of the slice: x: 2, y: 2, z: 4, core: 2. Of those that a mesh axis runs over, the one named last changes fastest.
Arguments:
- inputs: bfloat16 [256, 64, 768], P('dp'), may hold values from -6 to 6
- cotangent: bfloat16 [2, 256, 64, 768], P('section', 'dp'), may hold values from -6 to 6
- images: bfloat16 [16, 576, 768], P('dp', 'section'), may hold values from -6 to 6
- seg_ids: int32 [256, 64], P('dp'), may hold values from 0 to 1, as said below
- row_block: int32 [256], P('dp'), may hold values from 0 to 15, as said below
- seg_image: int32 [256, 2], P('dp'), may hold values from 0 to 1, as said below
- ln1_gain: float32 [2, 768], P('section'), may hold values from 0.5 to 1.5
- ln1_bias: float32 [2, 768], P('section'), may hold values from -3 to 3
- w_qkv: bfloat16 [2, 768, 2304], P('section'), may hold values from -0.21875 to 0.21875
- w_out: bfloat16 [2, 768, 768], P('section'), may hold values from -0.875 to 0.875
- ln2_gain: float32 [2, 768], P('section'), may hold values from 0.5 to 1.5
- ln2_bias: float32 [2, 768], P('section'), may hold values from -3 to 3
- w_up: bfloat16 [2, 768, 3072], P('section'), may hold values from -0.21875 to 0.21875
- b_up: float32 [2, 3072], P('section'), may hold values from -3 to 3
- w_down: bfloat16 [2, 3072, 768], P('section'), may hold values from -0.109375 to 0.109375
- b_down: float32 [2, 768], P('section'), may hold values from -3 to 3
- lnc_gain: float32 [768], replicated, may hold values from 0.5 to 1.5
- lnc_bias: float32 [768], replicated, may hold values from -3 to 3
- wq_cross: bfloat16 [768, 768], replicated, may hold values from -0.21875 to 0.21875
- wkv_cross: bfloat16 [768, 1536], replicated, may hold values from -0.21875 to 0.21875
- wo_cross: bfloat16 [768, 768], replicated, may hold values from -3 to 3
Outputs:
- activations: float32 [2, 256, 64, 768], P('section', 'dp')
- back_grads: float32 [2, 256, 64, 768], P('section', 'dp')
- image_grad: float32 [16, 576, 768], P('dp', 'section')
- grad_ln1_gain: float32 [2, 768], P('section', 'dp')
- grad_ln1_bias: float32 [2, 768], P('section', 'dp')
- grad_w_qkv: float32 [2, 768, 2304], P('section', 'dp')
- grad_w_out: float32 [2, 768, 768], P('section', 'dp')
- grad_ln2_gain: float32 [2, 768], P('section', 'dp')
- grad_ln2_bias: float32 [2, 768], P('section', 'dp')
- grad_w_up: float32 [2, 768, 3072], P('section', 'dp')
- grad_b_up: float32 [2, 3072], P('section', 'dp')
- grad_w_down: float32 [2, 3072, 768], P('section', 'dp')
- grad_b_down: float32 [2, 768], P('section', 'dp')
- grad_lnc_gain: float32 [768], P('dp')
- grad_lnc_bias: float32 [768], P('dp')
- grad_wq_cross: float32 [768, 768], P('dp')
- grad_wkv_cross: float32 [768, 1536], P('dp')
- grad_wo_cross: float32 [768, 768], P('dp')
The draws below stay inside these ranges and needn't reach their ends.
Inputs may be any that keep to these rules, and one draw needn't show every extreme that they name: `seg_ids`: in every row caption 0 holds the first positions and caption 1 the rest; each caption has 16 to 48 positions, and row 0's first caption has exactly 48. `row_block`: for row r it is r // 16 - 1 or that number itself, modulo 16; the first row of each group of 16 rows takes the former, the last row the latter. Caption j of row r describes image (row_block[r] + seg_image[r, j]) modulo 16; in the first row of each group of 16 rows caption 0 takes 0, in the last row caption 1 takes 1.
All inputs are finite; a program needn't handle non-finite values.
Results may differ from the reference program's by a relative error of at most 0.025.
Values may be sent and summed in bfloat16 or wider, within the bound.
A program may use at most 640 MiB of HBM per device.

```python
import jax
import jax.numpy as jnp
from jax import lax

D = 768
H = 12
HD = 64
FF = 3072
IMG_TOK = 576
SEQ = 64
SEGS = 2
MICRO = 2
ROWS_MB = 8
ROWS = 256
IMAGES = 16
N_DP = 16


def draw_row_block(key, part):
    row_index = jnp.arange(ROWS, dtype=jnp.int32)
    group_len = MICRO * ROWS_MB
    home = row_index // group_len
    inner = row_index % group_len
    shifted = jax.random.randint(key, (ROWS,), 0, 2, dtype=jnp.int32)
    shifted = jnp.where(inner == 0, jnp.int32(0), shifted)
    shifted = jnp.where(inner == group_len - 1, jnp.int32(1), shifted)
    return ((home - 1 + shifted + IMAGES) % IMAGES).astype(jnp.int32)


def draw_seg_image(key, part):
    group_len = MICRO * ROWS_MB
    picks = jax.random.randint(jax.random.fold_in(key, 23), (ROWS, SEGS), 0, 2, dtype=jnp.int32)
    inner = (jnp.arange(ROWS, dtype=jnp.int32) % group_len)[:, None]
    column = jnp.arange(SEGS, dtype=jnp.int32)[None, :]
    picks = jnp.where((inner == 0) & (column == 0), jnp.int32(0), picks)
    picks = jnp.where((inner == group_len - 1) & (column == 1), jnp.int32(1), picks)
    return picks.astype(jnp.int32)


def draw_seg_ids(key, part):
    fewest = SEQ // 4
    most_len = SEQ * 3 // 4
    cuts = jax.random.randint(jax.random.fold_in(key, 11), (ROWS, 1), fewest, most_len + 1, dtype=jnp.int32)
    row_index = jnp.arange(ROWS, dtype=jnp.int32)[:, None]
    cuts = jnp.where(row_index == 0, jnp.int32(most_len), cuts)
    positions = jnp.arange(SEQ, dtype=jnp.int32)[None, :]
    return (positions >= cuts).astype(jnp.int32)


def level_of(stream_key, shape, shards, least, largest):
    gain = 1.0
    for axis_at, blocks in shards:
        draws = jax.random.uniform(jax.random.fold_in(jax.random.fold_in(stream_key, 6), axis_at), (blocks,), jnp.float32, least / len(shards), largest / len(shards))
        gain = gain * jnp.repeat(jnp.exp(draws), shape[axis_at] // blocks).reshape((-1,) + (1,) * (len(shape) - 1 - axis_at))
    return gain


def bell_draw(rng, shape, deviation, most, shards=(), kind=jnp.bfloat16):
    loudness = level_of(rng, shape, shards, -0.22, 0.18) if shards else 1.0
    result = jax.random.normal(rng, shape, jnp.float32) * deviation * loudness
    return jnp.minimum(jnp.maximum(result, -most), most).astype(kind)


def setup_inputs(seed: int = 0) -> dict:
    keys = jax.random.split(jax.random.key(seed), 22)
    inputs = bell_draw(keys[0], (ROWS, SEQ, D), 1.0, 6.0, ((0, 16),))
    cotangent = bell_draw(keys[1], (2, ROWS, SEQ, D), 1.0, 6.0, ((0, 2), (1, 16)))
    images = bell_draw(keys[2], (IMAGES, IMG_TOK, D), 1.0, 6.0, ((0, 16), (1, 2)))
    seg_ids = draw_seg_ids(jax.random.fold_in(keys[21], 71), 0)
    row_block = draw_row_block(jax.random.fold_in(keys[21], 71), 0)
    seg_image = draw_seg_image(jax.random.fold_in(keys[21], 71), 0)
    ln1_gain = jnp.clip(1.0 + 0.1 * jax.random.normal(keys[6], (2, D), jnp.float32), 0.5, 1.5)
    ln1_bias = bell_draw(keys[7], (2, D), 0.3, 3.0, ((0, 2),), jnp.float32)
    w_qkv = bell_draw(keys[8], (2, D, 3 * D), D ** -0.5, 0.21875, ((0, 2),))
    w_out = bell_draw(keys[9], (2, D, D), (D // 16) ** -0.5, 0.875, ((0, 2),))
    ln2_gain = jnp.clip(1.0 + 0.1 * jax.random.normal(keys[10], (2, D), jnp.float32), 0.5, 1.5)
    ln2_bias = bell_draw(keys[11], (2, D), 0.3, 3.0, ((0, 2),), jnp.float32)
    w_up = bell_draw(keys[12], (2, D, FF), D ** -0.5, 0.21875, ((0, 2),))
    b_up = bell_draw(keys[13], (2, FF), 0.5, 3.0, ((0, 2),), jnp.float32)
    w_down = bell_draw(keys[14], (2, FF, D), FF ** -0.5, 0.109375, ((0, 2),))
    b_down = bell_draw(keys[15], (2, D), 0.3, 3.0, ((0, 2),), jnp.float32)
    lnc_gain = jnp.clip(1.0 + 0.1 * jax.random.normal(keys[16], (D,), jnp.float32), 0.5, 1.5)
    lnc_bias = bell_draw(keys[17], (D,), 0.3, 3.0, (), jnp.float32)
    wq_cross = bell_draw(keys[18], (D, D), D ** -0.5, 0.21875)
    wkv_cross = bell_draw(keys[19], (D, 2 * D), D ** -0.5, 0.21875)
    wo_cross = bell_draw(keys[20], (D, D), (max(D // 192, 1)) ** -0.5, 3.0)
    return dict(inputs=inputs, cotangent=cotangent, images=images, seg_ids=seg_ids, row_block=row_block, seg_image=seg_image, ln1_gain=ln1_gain, ln1_bias=ln1_bias, w_qkv=w_qkv, w_out=w_out, ln2_gain=ln2_gain, ln2_bias=ln2_bias, w_up=w_up, b_up=b_up, w_down=w_down, b_down=b_down, lnc_gain=lnc_gain, lnc_bias=lnc_bias, wq_cross=wq_cross, wkv_cross=wkv_cross, wo_cross=wo_cross)


EPS = 1e-05
HIGH = lax.Precision.HIGHEST

@jax.custom_vjp
def low(v):
    return lax.optimization_barrier(v.astype(jnp.bfloat16)).astype(jnp.float32)

@jax.custom_vjp
def low_back(v):
    return v

def low_keep(v):
    return (low(v), None)

def low_pass(kept, grad):
    return (grad,)

def back_keep(v):
    return (v, None)

def back_low(kept, grad):
    return (low(grad),)
low.defvjp(low_keep, low_pass)
low_back.defvjp(back_keep, back_low)

def layer_norm(stream, gain_vec, bias_vec):
    middle = lax.optimization_barrier(jnp.mean(stream, -1, keepdims=True))
    centred = stream - middle
    spread = lax.optimization_barrier(jnp.mean(centred * centred, -1, keepdims=True))
    return centred * lax.rsqrt(spread + EPS) * gain_vec + bias_vec

def project(stream, weight):
    return jnp.einsum('...d,de->...e', stream, weight, precision=HIGH)

def attention(queries, key_rows, value_rows, allowed):
    factor = HD ** (-0.5)
    scores = low_back(jnp.einsum('rqhd,rkhd->rhqk', queries, key_rows, precision=HIGH) * factor)
    scores = jnp.where(allowed[:, None], scores, -1e+30)
    attn_probs = jax.nn.softmax(scores, axis=-1)
    return jnp.einsum('rhqk,rkhd->rqhd', low(attn_probs), value_rows, precision=HIGH)

def self_block(hidden, seg_rows, gain_vec, bias_vec, w_triple, w_mix):
    row_count, seq_len = seg_rows.shape
    normed = low(layer_norm(hidden, gain_vec, bias_vec))
    triple = low(low_back(project(normed, w_triple))).reshape(row_count, seq_len, 3, H, HD)
    positions = jnp.arange(seq_len)
    allowed = (seg_rows[:, :, None] == seg_rows[:, None, :]) & (positions[:, None] >= positions[None, :])[None]
    mixed_out = attention(triple[:, :, 0], triple[:, :, 1], triple[:, :, 2], allowed)
    mixed_out = low(low_back(mixed_out.reshape(row_count, seq_len, H * HD)))
    return low_back(project(mixed_out, w_mix))

def cross_block(hidden, seg_rows, image_pool, slot_ids, gain_vec, bias_vec, w_query, w_back):
    row_count, seq_len = seg_rows.shape
    normed = low(layer_norm(hidden, gain_vec, bias_vec))
    queries = low(low_back(project(normed, w_query))).reshape(row_count, seq_len, H, HD)
    chosen = image_pool[slot_ids].reshape(row_count, SEGS * IMG_TOK, 2, H, HD)
    owners = jnp.arange(SEGS * IMG_TOK) // IMG_TOK
    allowed = seg_rows[:, :, None] == owners[None, None, :]
    mixed_out = attention(queries, chosen[:, :, 0], chosen[:, :, 1], allowed)
    mixed_out = low(low_back(mixed_out.reshape(row_count, seq_len, H * HD)))
    return low_back(project(mixed_out, w_back))

def feed_forward(hidden, gain_vec, bias_vec, w_expand, b_expand, w_reduce, b_reduce):
    normed = low(layer_norm(hidden, gain_vec, bias_vec))
    pre_act = low_back(project(normed, w_expand) + b_expand)
    active = low(jax.nn.gelu(pre_act, approximate=False))
    return low_back(project(active, w_reduce) + b_reduce)

def forward(start, extra, pictures, seg_ids, row_block, seg_image, params):
    ln1_gain, ln1_bias, w_qkv, w_out, ln2_gain, ln2_bias, w_up, b_up, w_down, b_down, lnc_gain, lnc_bias, wq_cross, wkv_cross, wo_cross = params
    group_rows = ROWS // N_DP
    key_pairs = low(low_back(project(pictures, wkv_cross)))

    def lower_layer(unused, portion):
        hidden, seg_rows = portion
        hidden = hidden + self_block(hidden, seg_rows, ln1_gain[0], ln1_bias[0], w_qkv[0], w_out[0])
        hidden = hidden + feed_forward(hidden, ln2_gain[0], ln2_bias[0], w_up[0], b_up[0], w_down[0], b_down[0])
        return (unused, hidden)
    unused = jnp.zeros((), jnp.float32)
    _, lower_out = lax.scan(jax.checkpoint(lower_layer), unused, (start.reshape(N_DP, group_rows, SEQ, D), seg_ids.reshape(N_DP, group_rows, SEQ)))
    lower_out = lower_out.reshape(ROWS, SEQ, D)
    sent_rows = low_back(low(lower_out)) + extra

    def upper_layer(unused, portion):
        hidden, seg_rows, starts, offsets, device = portion
        near_ids = (device - 1 + jnp.arange(3, dtype=jnp.int32)) % N_DP
        image_pool = low_back(key_pairs[near_ids])
        slot_ids = ((starts[:, None] + offsets - device + 1 + N_DP) % N_DP).astype(jnp.int32)
        hidden = hidden + self_block(hidden, seg_rows, ln1_gain[1], ln1_bias[1], w_qkv[1], w_out[1])
        hidden = hidden + cross_block(hidden, seg_rows, image_pool, slot_ids, lnc_gain, lnc_bias, wq_cross, wo_cross)
        hidden = hidden + feed_forward(hidden, ln2_gain[1], ln2_bias[1], w_up[1], b_up[1], w_down[1], b_down[1])
        return (unused, hidden)
    _, upper_out = lax.scan(jax.checkpoint(upper_layer), unused, (sent_rows.reshape(N_DP, group_rows, SEQ, D), seg_ids.reshape(N_DP, group_rows, SEQ), row_block.reshape(N_DP, group_rows), seg_image.reshape(N_DP, group_rows, SEGS), jnp.arange(N_DP, dtype=jnp.int32)))
    return (lower_out, upper_out.reshape(ROWS, SEQ, D))

def reference(inputs, cotangent, images, seg_ids, row_block, seg_image, ln1_gain, ln1_bias, w_qkv, w_out, ln2_gain, ln2_bias, w_up, b_up, w_down, b_down, lnc_gain, lnc_bias, wq_cross, wkv_cross, wo_cross):
    params = tuple((weight.astype(jnp.float32) for weight in (ln1_gain, ln1_bias, w_qkv, w_out, ln2_gain, ln2_bias, w_up, b_up, w_down, b_down, lnc_gain, lnc_bias, wq_cross, wkv_cross, wo_cross)))
    start = inputs.astype(jnp.float32)
    extra = jnp.zeros_like(start)
    pictures = images.astype(jnp.float32)

    def whole_run(start, extra, pictures, params):
        return forward(start, extra, pictures, seg_ids, row_block, seg_image, params)
    (lower_out, upper_out), pullback = jax.vjp(whole_run, start, extra, pictures, params)
    grad_start, grad_extra, grad_pictures, grad_params = pullback((cotangent[0].astype(jnp.float32), cotangent[1].astype(jnp.float32)))
    return (jnp.stack([lower_out, upper_out]), jnp.stack([grad_start, grad_extra]), grad_pictures, grad_params[0], grad_params[1], grad_params[2], grad_params[3], grad_params[4], grad_params[5], grad_params[6], grad_params[7], grad_params[8], grad_params[9], grad_params[10], grad_params[11], grad_params[12], grad_params[13], grad_params[14])
```

```python
from functools import partial

import jax
import jax.numpy as jnp
from jax import lax
from jax.sharding import PartitionSpec as P

H = 12
HD = 64
MICRO = 2

EPS = 1e-05
MASKED = -1e30
SCALE = HD ** (-0.5)
F32 = jnp.float32
BF16 = jnp.bfloat16


def bf(x):
    return x.astype(BF16)


def run_on(flag, fn, *args):
    shapes = jax.eval_shape(fn, *args)

    def idle(*unused):
        return jax.tree.map(lambda s: jnp.zeros(s.shape, s.dtype), shapes)

    return lax.cond(flag, fn, idle, *args)


def norm_fwd(x, gain, bias):
    mean = jnp.mean(x, -1, keepdims=True)
    centred = x - mean
    var = jnp.mean(centred * centred, -1, keepdims=True)
    rstd = lax.rsqrt(var + EPS)
    xhat = centred * rstd
    return xhat * gain + bias, (xhat, rstd)


def norm_bwd(dy, saved, gain):
    xhat, rstd = saved
    lead = tuple(range(dy.ndim - 1))
    d_gain = jnp.sum(dy * xhat, lead)
    d_bias = jnp.sum(dy, lead)
    dxh = dy * gain
    dx = rstd * (
        dxh
        - jnp.mean(dxh, -1, keepdims=True)
        - xhat * jnp.mean(dxh * xhat, -1, keepdims=True)
    )
    return dx, d_gain, d_bias


def mm(a, w):
    return jnp.einsum("...d,de->...e", a, w, preferred_element_type=F32)


def mm_t(g, w):
    return jnp.einsum("...e,de->...d", g, w, preferred_element_type=F32)


def outer(a, b):
    return jnp.einsum("rtd,rte->de", a, b, preferred_element_type=F32)


def softmax_rows(s, axes):
    top = jnp.max(s, axes, keepdims=True)
    e = jnp.exp(s - top)
    return e / jnp.sum(e, axes, keepdims=True)


def self_fwd(h, seg, gain, bias, w_qkv, w_out):
    r, t = seg.shape
    y, nsave = norm_fwd(h, gain, bias)
    n = bf(y)
    trip = bf(mm(n, w_qkv)).reshape(r, t, 3, H, HD)
    q, k, v = trip[:, :, 0], trip[:, :, 1], trip[:, :, 2]
    pos = jnp.arange(t)
    allowed = (seg[:, :, None] == seg[:, None, :]) & (pos[:, None] >= pos[None, :])[None]
    s = jnp.einsum("rqhd,rkhd->rhqk", q, k, preferred_element_type=F32) * SCALE
    s = jnp.where(allowed[:, None], s, MASKED)
    p = softmax_rows(s, -1)
    o = bf(jnp.einsum("rhqk,rkhd->rqhd", bf(p), v, preferred_element_type=F32))
    o = o.reshape(r, t, H * HD)
    h2 = h + mm(o, w_out)
    saved = dict(nsave=nsave, n=n, q=q, k=k, v=v, p=p, o=o)
    return h2, saved


def self_bwd(dh2, sv, gain, w_qkv, w_out):
    r, t = dh2.shape[:2]
    g2 = bf(dh2)
    do = bf(mm_t(g2, w_out)).reshape(r, t, H, HD)
    p, q, k, v = sv["p"], sv["q"], sv["k"], sv["v"]
    dp = jnp.einsum("rqhd,rkhd->rhqk", do, v, preferred_element_type=F32)
    ds = bf(p * (dp - jnp.sum(p * dp, -1, keepdims=True)))
    dq = jnp.einsum("rhqk,rkhd->rqhd", ds, k, preferred_element_type=F32) * SCALE
    dk = jnp.einsum("rhqk,rqhd->rkhd", ds, q, preferred_element_type=F32) * SCALE
    dv = jnp.einsum("rhqk,rqhd->rkhd", bf(p), do, preferred_element_type=F32)
    dt = bf(jnp.stack([dq, dk, dv], 2)).reshape(r, t, 3 * H * HD)
    dn = mm_t(dt, w_qkv)
    dx, d_gain, d_bias = norm_bwd(dn, sv["nsave"], gain)
    pairs = dict(o=sv["o"], g2=g2, n=sv["n"], dt=dt)
    return dh2 + dx, (d_gain, d_bias), pairs


def cross_core_fwd(qc, pool_k, pool_v, pick):
    s = jnp.einsum("rqhd,pkhd->rhqpk", qc, pool_k, preferred_element_type=F32) * SCALE
    allowed = pick[:, :, None] == jnp.arange(pool_k.shape[0])[None, None, :]
    s = jnp.where(allowed[:, None, :, :, None], s, MASKED)
    p = softmax_rows(s, (-2, -1))
    oc = jnp.einsum("rhqpk,pkhd->rqhd", bf(p), pool_v, preferred_element_type=F32)
    return bf(oc), p


def cross_core_bwd(doc, qc, pool_k, pool_v, p):
    dp = jnp.einsum("rqhd,pkhd->rhqpk", doc, pool_v, preferred_element_type=F32)
    ds = bf(p * (dp - jnp.sum(p * dp, (-2, -1), keepdims=True)))
    dqc = jnp.einsum("rhqpk,pkhd->rqhd", ds, pool_k, preferred_element_type=F32) * SCALE
    dk = jnp.einsum("rhqpk,rqhd->pkhd", ds, qc, preferred_element_type=F32) * SCALE
    dv = jnp.einsum("rhqpk,rqhd->pkhd", bf(p), doc, preferred_element_type=F32)
    return dqc, dk, dv


def cross_fwd(h2, pick, pool_k, pool_v, gain, bias, wq, wo):
    r, t = pick.shape
    y, csave = norm_fwd(h2, gain, bias)
    c = bf(y)
    qc = bf(mm(c, wq)).reshape(r, t, H, HD)
    oc, p = cross_core_fwd(qc, pool_k, pool_v, pick)
    oc = oc.reshape(r, t, H * HD)
    h3 = h2 + mm(oc, wo)
    return h3, dict(csave=csave, c=c, qc=qc, p=p, oc=oc)


def cross_bwd(dh3, sv, pool_k, pool_v, gain, wq, wo):
    r, t = dh3.shape[:2]
    g3 = bf(dh3)
    doc = bf(mm_t(g3, wo)).reshape(r, t, H, HD)
    dqc, dk, dv = cross_core_bwd(doc, sv["qc"], pool_k, pool_v, sv["p"])
    dqc = bf(dqc.reshape(r, t, H * HD))
    dc = mm_t(dqc, wq)
    dx, d_gain, d_bias = norm_bwd(dc, sv["csave"], gain)
    pairs = dict(oc=sv["oc"], g3=g3, c=sv["c"], dqc=dqc)
    return dh3 + dx, (d_gain, d_bias), pairs, dk, dv


def gelu(z):
    return jax.nn.gelu(z, approximate=False)


def ffn_fwd(h3, gain, bias, w_up, b_up, w_down, b_down):
    y, usave = norm_fwd(h3, gain, bias)
    u = bf(y)
    z = mm(u, w_up) + b_up
    f = bf(gelu(z))
    out = h3 + (mm(f, w_down) + b_down)
    return out, dict(usave=usave, u=u, z=z, f=f)


def ffn_bwd(gout, sv, gain, w_up, w_down):
    gb = bf(gout)
    df = mm_t(gb, w_down)
    _, pull = jax.vjp(gelu, sv["z"])
    dz = bf(pull(df)[0])
    du = mm_t(dz, w_up)
    dx, d_gain, d_bias = norm_bwd(du, sv["usave"], gain)
    pairs = dict(f=sv["f"], gb=gb, u=sv["u"], dz=dz)
    return gout + dx, (d_gain, d_bias), pairs


def per_device(
    inputs,
    cotangent,
    images,
    seg_ids,
    row_block,
    seg_image,
    ln1_gain,
    ln1_bias,
    w_qkv,
    w_out,
    ln2_gain,
    ln2_bias,
    w_up,
    b_up,
    w_down,
    b_down,
    lnc_gain,
    lnc_bias,
    wq_cross,
    wkv_cross,
    wo_cross,
):
    up = lax.axis_index("section") == 1
    low = jnp.logical_not(up)
    dp_index = lax.axis_index("dp")
    n_dp = lax.axis_size("dp")
    rows = inputs.shape[0]
    rc = rows // MICRO
    g1, b1, wqkv, wout = ln1_gain[0], ln1_bias[0], w_qkv[0], w_out[0]
    g2, b2, wup, bup, wdown, bdown = ln2_gain[0], ln2_bias[0], w_up[0], b_up[0], w_down[0], b_down[0]
    n_img = n_dp * images.shape[0]

    first_half = lax.ppermute(images[0], "section", [(0, 1)])
    full_image = jnp.concatenate([first_half, images[0]], 0)

    def make_kv(img):
        return bf(mm(img, wkv_cross))

    kv_own = run_on(up, make_kv, full_image)
    ring_up = [(i, (i + 1) % n_dp) for i in range(n_dp)]
    ring_down = [((i + 1) % n_dp, i) for i in range(n_dp)]
    kv_prev = lax.ppermute(kv_own, "dp", ring_up)
    kv_next = lax.ppermute(kv_own, "dp", ring_down)
    pool = jnp.stack([kv_prev, kv_own, kv_next], 0)
    img_tok = pool.shape[1]
    pool = pool.reshape(3, img_tok, 2, H, HD)
    pool_k, pool_v = pool[:, :, 0], pool[:, :, 1]

    first_img = (row_block[:, None] + seg_image) % n_img
    slot = (first_img - dp_index + 1 + n_img) % n_img
    pick_all = jnp.where(seg_ids == 0, slot[:, :1], slot[:, 1:2])

    def chunk(a, m):
        return a[m * rc : (m + 1) * rc]

    x = inputs.astype(F32)

    def lower_fwd(hid, seg):
        h2, s_self = self_fwd(hid, seg, g1, b1, wqkv, wout)
        out, s_ffn = ffn_fwd(h2, g2, b2, wup, bup, wdown, bdown)
        return out, (s_self, s_ffn)

    def upper_fwd(sent, seg, pick, pk, pv):
        hid = sent.astype(F32)
        h2, s_self = self_fwd(hid, seg, g1, b1, wqkv, wout)
        h3, s_cross = cross_fwd(h2, pick, pk, pv, lnc_gain, lnc_bias, wq_cross, wo_cross)
        out, s_ffn = ffn_fwd(h3, g2, b2, wup, bup, wdown, bdown)
        return out, (s_self, s_cross, s_ffn)

    low_out, low_saved, sent = [], [], []
    for m in range(MICRO):
        out, saved = run_on(low, lower_fwd, chunk(x, m), chunk(seg_ids, m))
        low_out.append(out)
        low_saved.append(saved)
        sent.append(lax.ppermute(bf(out), "section", [(0, 1)]))
    up_out, up_saved = [], []
    for m in range(MICRO):
        out, saved = run_on(
            up, upper_fwd, sent[m], chunk(seg_ids, m), chunk(pick_all, m), pool_k, pool_v
        )
        up_out.append(out)
        up_saved.append(saved)

    cot = cotangent[0].astype(F32)

    def upper_bwd(gout, saved, pk, pv):
        s_self, s_cross, s_ffn = saved
        dh3, ln2g, pf = ffn_bwd(gout, s_ffn, g2, wup, wdown)
        dh2, lncg, pc, dk, dv = cross_bwd(dh3, s_cross, pk, pv, lnc_gain, wq_cross, wo_cross)
        dh, ln1g, ps = self_bwd(dh2, s_self, g1, wqkv, wout)
        return dh, (ln1g, ln2g, lncg), (ps, pf, pc), dk, dv

    up_grad, up_small, up_pairs = [], [], []
    returned = []
    pool_dk = pool_dv = None
    for m in range(MICRO):
        dh, small, pairs, dk, dv = run_on(up, upper_bwd, chunk(cot, m), up_saved[m], pool_k, pool_v)
        up_grad.append(dh)
        up_small.append(small)
        up_pairs.append(pairs)
        pool_dk = dk if pool_dk is None else pool_dk + dk
        pool_dv = dv if pool_dv is None else pool_dv + dv
        returned.append(lax.ppermute(bf(dh), "section", [(1, 0)]))

    def cat(name_path, pairs_list):
        return jnp.concatenate([name_path(p) for p in pairs_list], 0)

    def layer_weight_grads(pairs_list):
        ps = lambda i, k: cat(lambda p: p[i][k], pairs_list)
        d_wqkv = outer(ps(0, "n"), ps(0, "dt"))
        d_wout = outer(ps(0, "o"), ps(0, "g2"))
        d_wup = outer(ps(1, "u"), ps(1, "dz"))
        d_wdown = outer(ps(1, "f"), ps(1, "gb"))
        d_bup = jnp.sum(ps(1, "dz").astype(F32), (0, 1))
        d_bdown = jnp.sum(ps(1, "gb").astype(F32), (0, 1))
        return d_wqkv, d_wout, d_wup, d_bup, d_wdown, d_bdown

    def upper_wgrads(pairs_list):
        layer = layer_weight_grads(pairs_list)
        ps = lambda k: cat(lambda p: p[2][k], pairs_list)
        d_wq = outer(ps("c"), ps("dqc"))
        d_wo = outer(ps("oc"), ps("g3"))
        return layer, (d_wq, d_wo)

    up_w, cross_w = run_on(up, upper_wgrads, up_pairs)

    parts = bf(
        jnp.concatenate(
            [pool_dk.reshape(3, img_tok, H * HD), pool_dv.reshape(3, img_tok, H * HD)], -1
        )
    )
    from_next = lax.ppermute(parts[0], "dp", ring_down)
    from_prev = lax.ppermute(parts[2], "dp", ring_up)
    kv_grad = bf(parts[1].astype(F32) + from_next.astype(F32) + from_prev.astype(F32))

    def image_side(kvg, img):
        ig = jnp.einsum("te,de->td", kvg, wkv_cross, preferred_element_type=F32)
        dw = jnp.einsum("td,te->de", img, kvg, preferred_element_type=F32)
        return ig, dw

    image_grad_full, d_wkv = run_on(up, image_side, kv_grad, full_image)
    half = images.shape[1]
    ig_first = lax.ppermute(image_grad_full[:half], "section", [(1, 0)])
    image_grad = jnp.where(up, image_grad_full[half:], ig_first)[None]

    def lower_bwd(gout, saved):
        s_self, s_ffn = saved
        dh3, ln2g, pf = ffn_bwd(gout, s_ffn, g2, wup, wdown)
        dh, ln1g, ps = self_bwd(dh3, s_self, g1, wqkv, wout)
        return dh, (ln1g, ln2g), (ps, pf)

    low_grad, low_small, low_pairs = [], [], []
    for m in range(MICRO):
        gout = chunk(cot, m) + returned[m].astype(F32)
        dh, small, pairs = run_on(low, lower_bwd, gout, low_saved[m])
        low_grad.append(dh)
        low_small.append(small)
        low_pairs.append(pairs)

    low_w = run_on(low, layer_weight_grads, low_pairs)

    activations = jnp.where(
        up, jnp.concatenate(up_out, 0), jnp.concatenate(low_out, 0)
    )[None]
    back_grads = jnp.where(
        up, jnp.concatenate(up_grad, 0), jnp.concatenate(low_grad, 0)
    )[None]

    def tree_sum(xs):
        total = xs[0]
        for v in xs[1:]:
            total = jax.tree.map(jnp.add, total, v)
        return total

    up_sm = tree_sum(up_small)
    low_sm = tree_sum(low_small)
    ln1g = jax.tree.map(lambda a, b: jnp.where(up, a, b), up_sm[0], low_sm[0])
    ln2g = jax.tree.map(lambda a, b: jnp.where(up, a, b), up_sm[1], low_sm[1])
    lncg = up_sm[2]
    lw = jax.tree.map(lambda a, b: jnp.where(up, a, b), up_w, low_w)
    d_wqkv, d_wout, d_wup, d_bup, d_wdown, d_bdown = lw

    def rs(a, dim=0):
        return lax.psum_scatter(a, "dp", scatter_dimension=dim, tiled=True)

    def rs_cross(a):
        return lax.psum(jnp.where(up, rs(a), 0.0), "section")

    return (
        activations,
        back_grads,
        image_grad,
        rs(ln1g[0])[None],
        rs(ln1g[1])[None],
        rs(d_wqkv)[None],
        rs(d_wout)[None],
        rs(ln2g[0])[None],
        rs(ln2g[1])[None],
        rs(d_wup)[None],
        rs(d_bup)[None],
        rs(d_wdown)[None],
        rs(d_bdown)[None],
        rs_cross(lncg[0]),
        rs_cross(lncg[1]),
        rs_cross(cross_w[0]),
        rs_cross(d_wkv),
        rs_cross(cross_w[1]),
    )


def solution(mesh):
    placed = (
        P("dp", None, None),
        P("section", "dp", None, None),
        P("dp", "section", None),
        P("dp", None),
        P("dp"),
        P("dp", None),
        P("section", None),
        P("section", None),
        P("section", None, None),
        P("section", None, None),
        P("section", None),
        P("section", None),
        P("section", None, None),
        P("section", None),
        P("section", None, None),
        P("section", None),
        P(),
        P(),
        P(),
        P(),
        P(),
    )
    return jax.shard_map(
        per_device,
        mesh=mesh,
        in_specs=placed,
        out_specs=(
            P("section", "dp", None, None),
            P("section", "dp", None, None),
            P("dp", "section", None),
            P("section", "dp"),
            P("section", "dp"),
            P("section", "dp", None),
            P("section", "dp", None),
            P("section", "dp"),
            P("section", "dp"),
            P("section", "dp", None),
            P("section", "dp"),
            P("section", "dp", None),
            P("section", "dp"),
            P("dp"),
            P("dp"),
            P("dp", None),
            P("dp", None),
            P("dp", None),
        ),
        check_vma=False,
    )
```

```python
from functools import partial

import jax
import jax.numpy as jnp
from jax import lax
from jax.experimental import pallas as pl
from jax.experimental.pallas import tpu as pltpu
from jax.sharding import PartitionSpec as P

H = 12
HD = 64
MICRO = 2

EPS = 1e-05
MASKED = -1e30
SCALE = HD ** (-0.5)
F32 = jnp.float32
BF16 = jnp.bfloat16


def bf(x):
    return x.astype(BF16)


def run_on(flag, fn, *args):
    shapes = jax.eval_shape(fn, *args)

    def idle(*unused):
        return jax.tree.map(lambda s: jnp.zeros(s.shape, s.dtype), shapes)

    return lax.cond(flag, fn, idle, *args)


def norm_fwd(x, gain, bias):
    mean = jnp.mean(x, -1, keepdims=True)
    centred = x - mean
    var = jnp.mean(centred * centred, -1, keepdims=True)
    rstd = lax.rsqrt(var + EPS)
    xhat = centred * rstd
    return xhat * gain + bias, (xhat, rstd)


def norm_bwd(dy, saved, gain):
    xhat, rstd = saved
    lead = tuple(range(dy.ndim - 1))
    d_gain = jnp.sum(dy * xhat, lead)
    d_bias = jnp.sum(dy, lead)
    dxh = dy * gain
    dx = rstd * (
        dxh
        - jnp.mean(dxh, -1, keepdims=True)
        - xhat * jnp.mean(dxh * xhat, -1, keepdims=True)
    )
    return dx, d_gain, d_bias


def mm(a, w):
    return jnp.einsum("...d,de->...e", a, w, preferred_element_type=F32)


def mm_t(g, w):
    return jnp.einsum("...e,de->...d", g, w, preferred_element_type=F32)


def outer(a, b):
    return jnp.einsum("rtd,rte->de", a, b, preferred_element_type=F32)


def softmax_rows(s, axes):
    top = jnp.max(s, axes, keepdims=True)
    e = jnp.exp(s - top)
    return e / jnp.sum(e, axes, keepdims=True)


def self_fwd(h, seg, gain, bias, w_qkv, w_out):
    r, t = seg.shape
    y, nsave = norm_fwd(h, gain, bias)
    n = bf(y)
    trip = bf(mm(n, w_qkv)).reshape(r, t, 3, H, HD)
    q, k, v = trip[:, :, 0], trip[:, :, 1], trip[:, :, 2]
    pos = jnp.arange(t)
    allowed = (seg[:, :, None] == seg[:, None, :]) & (pos[:, None] >= pos[None, :])[None]
    s = jnp.einsum("rqhd,rkhd->rhqk", q, k, preferred_element_type=F32) * SCALE
    s = jnp.where(allowed[:, None], s, MASKED)
    p = softmax_rows(s, -1)
    o = bf(jnp.einsum("rhqk,rkhd->rqhd", bf(p), v, preferred_element_type=F32))
    o = o.reshape(r, t, H * HD)
    h2 = h + mm(o, w_out)
    saved = dict(nsave=nsave, n=n, q=q, k=k, v=v, p=p, o=o)
    return h2, saved


def self_bwd(dh2, sv, gain, w_qkv, w_out):
    r, t = dh2.shape[:2]
    g2 = bf(dh2)
    do = bf(mm_t(g2, w_out)).reshape(r, t, H, HD)
    p, q, k, v = sv["p"], sv["q"], sv["k"], sv["v"]
    dp = jnp.einsum("rqhd,rkhd->rhqk", do, v, preferred_element_type=F32)
    ds = bf(p * (dp - jnp.sum(p * dp, -1, keepdims=True)))
    dq = jnp.einsum("rhqk,rkhd->rqhd", ds, k, preferred_element_type=F32) * SCALE
    dk = jnp.einsum("rhqk,rqhd->rkhd", ds, q, preferred_element_type=F32) * SCALE
    dv = jnp.einsum("rhqk,rqhd->rkhd", bf(p), do, preferred_element_type=F32)
    dt = bf(jnp.stack([dq, dk, dv], 2)).reshape(r, t, 3 * H * HD)
    dn = mm_t(dt, w_qkv)
    dx, d_gain, d_bias = norm_bwd(dn, sv["nsave"], gain)
    pairs = dict(o=sv["o"], g2=g2, n=sv["n"], dt=dt)
    return dh2 + dx, (d_gain, d_bias), pairs


RB = 2


def _dot_nt(a, b):
    return lax.dot_general(a, b, (((1,), (1,)), ((), ())), preferred_element_type=F32)


def _dot_tn(a, b):
    return lax.dot_general(a, b, (((0,), (0,)), ((), ())), preferred_element_type=F32)


def _dot(a, b):
    return lax.dot_general(a, b, (((1,), (0,)), ((), ())), preferred_element_type=F32)


def _probs(q, ka, kb, first):
    sa = _dot_nt(q, ka) * SCALE
    sb = _dot_nt(q, kb) * SCALE
    s = jnp.where(first, sa, sb)
    top = jnp.max(s, -1, keepdims=True)
    e = jnp.exp(s - top)
    return e / jnp.sum(e, -1, keepdims=True)


def _fwd_kernel(slot_ref, cut_ref, q_ref, pool_ref, o_ref):
    i = pl.program_id(0)
    t = q_ref.shape[1]
    d = H * HD
    for j in range(RB):
        r = i * RB + j
        a = slot_ref[2 * r]
        b = slot_ref[2 * r + 1]
        first = lax.broadcasted_iota(jnp.int32, (t, 1), 0) < cut_ref[r]
        for h in range(H):
            cols = pl.ds(h * HD, HD)
            vcols = pl.ds(d + h * HD, HD)
            q = q_ref[j, :, cols]
            p = _probs(q, pool_ref[a, :, cols], pool_ref[b, :, cols], first).astype(BF16)
            zero = jnp.zeros_like(p)
            o = _dot(jnp.where(first, p, zero), pool_ref[a, :, vcols]) + _dot(
                jnp.where(first, zero, p), pool_ref[b, :, vcols]
            )
            o_ref[j, :, cols] = o.astype(o_ref.dtype)


def _bwd_kernel(slot_ref, cut_ref, q_ref, do_ref, pool_ref, dq_ref, dpool_ref):
    i = pl.program_id(0)
    t = q_ref.shape[1]
    d = H * HD

    @pl.when(i == 0)
    def _():
        dpool_ref[...] = jnp.zeros_like(dpool_ref)

    for j in range(RB):
        r = i * RB + j
        a = slot_ref[2 * r]
        b = slot_ref[2 * r + 1]
        first = lax.broadcasted_iota(jnp.int32, (t, 1), 0) < cut_ref[r]
        for h in range(H):
            cols = pl.ds(h * HD, HD)
            vcols = pl.ds(d + h * HD, HD)
            q = q_ref[j, :, cols]
            do = do_ref[j, :, cols]
            ka = pool_ref[a, :, cols]
            kb = pool_ref[b, :, cols]
            va = pool_ref[a, :, vcols]
            vb = pool_ref[b, :, vcols]
            p = _probs(q, ka, kb, first)
            dp = jnp.where(first, _dot_nt(do, va), _dot_nt(do, vb))
            ds = (p * (dp - jnp.sum(p * dp, -1, keepdims=True))).astype(BF16)
            zero = jnp.zeros_like(ds)
            dsa = jnp.where(first, ds, zero)
            dsb = jnp.where(first, zero, ds)
            dq = (_dot(dsa, ka) + _dot(dsb, kb)) * SCALE
            dq_ref[j, :, cols] = dq.astype(dq_ref.dtype)
            pb = p.astype(BF16)
            pa_ = jnp.where(first, pb, zero)
            pb_ = jnp.where(first, zero, pb)
            dpool_ref[a, :, cols] += _dot_tn(dsa, q) * SCALE
            dpool_ref[a, :, vcols] += _dot_tn(pa_, do)
            dpool_ref[b, :, cols] += _dot_tn(dsb, q) * SCALE
            dpool_ref[b, :, vcols] += _dot_tn(pb_, do)


def cross_attention_fwd(qc, pool, slots, cuts):
    r, t, d = qc.shape
    spec = pltpu.PrefetchScalarGridSpec(
        num_scalar_prefetch=2,
        grid=(r // RB,),
        in_specs=[
            pl.BlockSpec((RB, t, d), lambda i, s, c: (i, 0, 0)),
            pl.BlockSpec(pool.shape, lambda i, s, c: (0, 0, 0)),
        ],
        out_specs=pl.BlockSpec((RB, t, d), lambda i, s, c: (i, 0, 0)),
    )
    flops = r * H * 4 * 2 * t * pool.shape[1] * HD
    return pl.pallas_call(
        _fwd_kernel,
        grid_spec=spec,
        out_shape=jax.ShapeDtypeStruct((r, t, d), BF16),
        compiler_params=pltpu.CompilerParams(
            dimension_semantics=("arbitrary",), vmem_limit_bytes=48 * 1024 * 1024
        ),
        cost_estimate=pl.CostEstimate(
            flops=flops,
            transcendentals=r * H * t * 2 * pool.shape[1],
            bytes_accessed=2 * qc.size * 2 + pool.size * 2,
        ),
    )(slots.reshape(-1), cuts, qc, pool)


def cross_attention_bwd(qc, doc, pool, slots, cuts):
    r, t, d = qc.shape
    spec = pltpu.PrefetchScalarGridSpec(
        num_scalar_prefetch=2,
        grid=(r // RB,),
        in_specs=[
            pl.BlockSpec((RB, t, d), lambda i, s, c: (i, 0, 0)),
            pl.BlockSpec((RB, t, d), lambda i, s, c: (i, 0, 0)),
            pl.BlockSpec(pool.shape, lambda i, s, c: (0, 0, 0)),
        ],
        out_specs=[
            pl.BlockSpec((RB, t, d), lambda i, s, c: (i, 0, 0)),
            pl.BlockSpec(pool.shape, lambda i, s, c: (0, 0, 0)),
        ],
    )
    flops = r * H * 10 * 2 * t * pool.shape[1] * HD
    return pl.pallas_call(
        _bwd_kernel,
        grid_spec=spec,
        out_shape=(
            jax.ShapeDtypeStruct((r, t, d), BF16),
            jax.ShapeDtypeStruct(pool.shape, F32),
        ),
        compiler_params=pltpu.CompilerParams(
            dimension_semantics=("arbitrary",), vmem_limit_bytes=60 * 1024 * 1024
        ),
        cost_estimate=pl.CostEstimate(
            flops=flops,
            transcendentals=r * H * t * 2 * pool.shape[1],
            bytes_accessed=3 * qc.size * 2 + pool.size * 2 + pool.size * 4,
        ),
    )(slots.reshape(-1), cuts, qc, doc, pool)


def cross_fwd(h2, slots, cuts, pool, gain, bias, wq, wo):
    y, csave = norm_fwd(h2, gain, bias)
    c = bf(y)
    qc = bf(mm(c, wq))
    oc = cross_attention_fwd(qc, pool, slots, cuts)
    h3 = h2 + mm(oc, wo)
    return h3, dict(csave=csave, c=c, qc=qc, oc=oc)


def cross_bwd(dh3, sv, slots, cuts, pool, gain, wq, wo):
    g3 = bf(dh3)
    doc = bf(mm_t(g3, wo))
    dqc, dpool = cross_attention_bwd(sv["qc"], doc, pool, slots, cuts)
    dc = mm_t(dqc, wq)
    dx, d_gain, d_bias = norm_bwd(dc, sv["csave"], gain)
    pairs = dict(oc=sv["oc"], g3=g3, c=sv["c"], dqc=dqc)
    return dh3 + dx, (d_gain, d_bias), pairs, dpool


def gelu(z):
    return jax.nn.gelu(z, approximate=False)


def ffn_fwd(h3, gain, bias, w_up, b_up, w_down, b_down):
    y, usave = norm_fwd(h3, gain, bias)
    u = bf(y)
    z = mm(u, w_up) + b_up
    f = bf(gelu(z))
    out = h3 + (mm(f, w_down) + b_down)
    return out, dict(usave=usave, u=u, z=z, f=f)


def ffn_bwd(gout, sv, gain, w_up, w_down):
    gb = bf(gout)
    df = mm_t(gb, w_down)
    _, pull = jax.vjp(gelu, sv["z"])
    dz = bf(pull(df)[0])
    du = mm_t(dz, w_up)
    dx, d_gain, d_bias = norm_bwd(du, sv["usave"], gain)
    pairs = dict(f=sv["f"], gb=gb, u=sv["u"], dz=dz)
    return gout + dx, (d_gain, d_bias), pairs


def per_device(
    inputs,
    cotangent,
    images,
    seg_ids,
    row_block,
    seg_image,
    ln1_gain,
    ln1_bias,
    w_qkv,
    w_out,
    ln2_gain,
    ln2_bias,
    w_up,
    b_up,
    w_down,
    b_down,
    lnc_gain,
    lnc_bias,
    wq_cross,
    wkv_cross,
    wo_cross,
):
    up = lax.axis_index("section") == 1
    low = jnp.logical_not(up)
    dp_index = lax.axis_index("dp")
    n_dp = lax.axis_size("dp")
    rows = inputs.shape[0]
    rc = rows // MICRO
    g1, b1, wqkv, wout = ln1_gain[0], ln1_bias[0], w_qkv[0], w_out[0]
    g2, b2, wup, bup, wdown, bdown = ln2_gain[0], ln2_bias[0], w_up[0], b_up[0], w_down[0], b_down[0]
    n_img = n_dp * images.shape[0]

    first_half = lax.ppermute(images[0], "section", [(0, 1)])
    full_image = jnp.concatenate([first_half, images[0]], 0)

    def make_kv(img):
        return bf(mm(img, wkv_cross))

    kv_own = run_on(up, make_kv, full_image)
    ring_up = [(i, (i + 1) % n_dp) for i in range(n_dp)]
    ring_down = [((i + 1) % n_dp, i) for i in range(n_dp)]
    kv_prev = lax.ppermute(kv_own, "dp", ring_up)
    kv_next = lax.ppermute(kv_own, "dp", ring_down)
    pool = jnp.stack([kv_prev, kv_own, kv_next], 0)
    img_tok = pool.shape[1]

    first_img = (row_block[:, None] + seg_image) % n_img
    slot = (first_img - dp_index + 1 + n_img) % n_img
    cut_all = jnp.sum((seg_ids == 0).astype(jnp.int32), 1)

    def chunk(a, m):
        return a[m * rc : (m + 1) * rc]

    x = inputs.astype(F32)

    def lower_fwd(hid, seg):
        h2, s_self = self_fwd(hid, seg, g1, b1, wqkv, wout)
        out, s_ffn = ffn_fwd(h2, g2, b2, wup, bup, wdown, bdown)
        return out, (s_self, s_ffn)

    def upper_fwd(sent, seg, slots, cuts, pool):
        hid = sent.astype(F32)
        h2, s_self = self_fwd(hid, seg, g1, b1, wqkv, wout)
        h3, s_cross = cross_fwd(h2, slots, cuts, pool, lnc_gain, lnc_bias, wq_cross, wo_cross)
        out, s_ffn = ffn_fwd(h3, g2, b2, wup, bup, wdown, bdown)
        return out, (s_self, s_cross, s_ffn)

    low_out, low_saved, sent = [], [], []
    for m in range(MICRO):
        out, saved = run_on(low, lower_fwd, chunk(x, m), chunk(seg_ids, m))
        low_out.append(out)
        low_saved.append(saved)
        sent.append(lax.ppermute(bf(out), "section", [(0, 1)]))
    up_out, up_saved = [], []
    for m in range(MICRO):
        out, saved = run_on(
            up, upper_fwd, sent[m], chunk(seg_ids, m), chunk(slot, m), chunk(cut_all, m), pool
        )
        up_out.append(out)
        up_saved.append(saved)

    cot = cotangent[0].astype(F32)

    def upper_bwd(gout, saved, slots, cuts, pool):
        s_self, s_cross, s_ffn = saved
        dh3, ln2g, pf = ffn_bwd(gout, s_ffn, g2, wup, wdown)
        dh2, lncg, pc, dpool = cross_bwd(dh3, s_cross, slots, cuts, pool, lnc_gain, wq_cross, wo_cross)
        dh, ln1g, ps = self_bwd(dh2, s_self, g1, wqkv, wout)
        return dh, (ln1g, ln2g, lncg), (ps, pf, pc), dpool

    up_grad, up_small, up_pairs = [], [], []
    returned = []
    pool_grad = None
    for m in range(MICRO):
        dh, small, pairs, dpool = run_on(
            up, upper_bwd, chunk(cot, m), up_saved[m], chunk(slot, m), chunk(cut_all, m), pool
        )
        up_grad.append(dh)
        up_small.append(small)
        up_pairs.append(pairs)
        pool_grad = dpool if pool_grad is None else pool_grad + dpool
        returned.append(lax.ppermute(bf(dh), "section", [(1, 0)]))

    def cat(name_path, pairs_list):
        return jnp.concatenate([name_path(p) for p in pairs_list], 0)

    def layer_weight_grads(pairs_list):
        ps = lambda i, k: cat(lambda p: p[i][k], pairs_list)
        d_wqkv = outer(ps(0, "n"), ps(0, "dt"))
        d_wout = outer(ps(0, "o"), ps(0, "g2"))
        d_wup = outer(ps(1, "u"), ps(1, "dz"))
        d_wdown = outer(ps(1, "f"), ps(1, "gb"))
        d_bup = jnp.sum(ps(1, "dz").astype(F32), (0, 1))
        d_bdown = jnp.sum(ps(1, "gb").astype(F32), (0, 1))
        return d_wqkv, d_wout, d_wup, d_bup, d_wdown, d_bdown

    def upper_wgrads(pairs_list):
        layer = layer_weight_grads(pairs_list)
        ps = lambda k: cat(lambda p: p[2][k], pairs_list)
        d_wq = outer(ps("c"), ps("dqc"))
        d_wo = outer(ps("oc"), ps("g3"))
        return layer, (d_wq, d_wo)

    up_w, cross_w = run_on(up, upper_wgrads, up_pairs)

    parts = bf(pool_grad)
    from_next = lax.ppermute(parts[0], "dp", ring_down)
    from_prev = lax.ppermute(parts[2], "dp", ring_up)
    kv_grad = bf(parts[1].astype(F32) + from_next.astype(F32) + from_prev.astype(F32))

    def image_side(kvg, img):
        ig = jnp.einsum("te,de->td", kvg, wkv_cross, preferred_element_type=F32)
        dw = jnp.einsum("td,te->de", img, kvg, preferred_element_type=F32)
        return ig, dw

    image_grad_full, d_wkv = run_on(up, image_side, kv_grad, full_image)
    half = images.shape[1]
    ig_first = lax.ppermute(image_grad_full[:half], "section", [(1, 0)])
    image_grad = jnp.where(up, image_grad_full[half:], ig_first)[None]

    def lower_bwd(gout, saved):
        s_self, s_ffn = saved
        dh3, ln2g, pf = ffn_bwd(gout, s_ffn, g2, wup, wdown)
        dh, ln1g, ps = self_bwd(dh3, s_self, g1, wqkv, wout)
        return dh, (ln1g, ln2g), (ps, pf)

    low_grad, low_small, low_pairs = [], [], []
    for m in range(MICRO):
        gout = chunk(cot, m) + returned[m].astype(F32)
        dh, small, pairs = run_on(low, lower_bwd, gout, low_saved[m])
        low_grad.append(dh)
        low_small.append(small)
        low_pairs.append(pairs)

    low_w = run_on(low, layer_weight_grads, low_pairs)

    activations = jnp.where(
        up, jnp.concatenate(up_out, 0), jnp.concatenate(low_out, 0)
    )[None]
    back_grads = jnp.where(
        up, jnp.concatenate(up_grad, 0), jnp.concatenate(low_grad, 0)
    )[None]

    def tree_sum(xs):
        total = xs[0]
        for v in xs[1:]:
            total = jax.tree.map(jnp.add, total, v)
        return total

    up_sm = tree_sum(up_small)
    low_sm = tree_sum(low_small)
    ln1g = jax.tree.map(lambda a, b: jnp.where(up, a, b), up_sm[0], low_sm[0])
    ln2g = jax.tree.map(lambda a, b: jnp.where(up, a, b), up_sm[1], low_sm[1])
    lncg = up_sm[2]
    lw = jax.tree.map(lambda a, b: jnp.where(up, a, b), up_w, low_w)
    d_wqkv, d_wout, d_wup, d_bup, d_wdown, d_bdown = lw

    def rs(a, dim=0):
        return lax.psum_scatter(a, "dp", scatter_dimension=dim, tiled=True)

    def rs_cross(a):
        return lax.psum(jnp.where(up, rs(a), 0.0), "section")

    return (
        activations,
        back_grads,
        image_grad,
        rs(ln1g[0])[None],
        rs(ln1g[1])[None],
        rs(d_wqkv)[None],
        rs(d_wout)[None],
        rs(ln2g[0])[None],
        rs(ln2g[1])[None],
        rs(d_wup)[None],
        rs(d_bup)[None],
        rs(d_wdown)[None],
        rs(d_bdown)[None],
        rs_cross(lncg[0]),
        rs_cross(lncg[1]),
        rs_cross(cross_w[0]),
        rs_cross(d_wkv),
        rs_cross(cross_w[1]),
    )


def solution(mesh):
    placed = (
        P("dp", None, None),
        P("section", "dp", None, None),
        P("dp", "section", None),
        P("dp", None),
        P("dp"),
        P("dp", None),
        P("section", None),
        P("section", None),
        P("section", None, None),
        P("section", None, None),
        P("section", None),
        P("section", None),
        P("section", None, None),
        P("section", None),
        P("section", None, None),
        P("section", None),
        P(),
        P(),
        P(),
        P(),
        P(),
    )
    return jax.shard_map(
        per_device,
        mesh=mesh,
        in_specs=placed,
        out_specs=(
            P("section", "dp", None, None),
            P("section", "dp", None, None),
            P("dp", "section", None),
            P("section", "dp"),
            P("section", "dp"),
            P("section", "dp", None),
            P("section", "dp", None),
            P("section", "dp"),
            P("section", "dp"),
            P("section", "dp", None),
            P("section", "dp"),
            P("section", "dp", None),
            P("section", "dp"),
            P("dp"),
            P("dp"),
            P("dp", None),
            P("dp", None),
            P("dp", None),
        ),
        check_vma=False,
    )
```

```python
from functools import partial

import jax
import jax.numpy as jnp
from jax import lax
from jax.experimental import pallas as pl
from jax.experimental.pallas import tpu as pltpu
from jax.sharding import PartitionSpec as P

H = 12
HD = 64
MICRO = 2

EPS = 1e-05
MASKED = -1e30
SCALE = HD ** (-0.5)
F32 = jnp.float32
BF16 = jnp.bfloat16


def bf(x):
    return x.astype(BF16)


def run_on(flag, fn, *args):
    shapes = jax.eval_shape(fn, *args)

    def idle(*unused):
        return jax.tree.map(lambda s: jnp.zeros(s.shape, s.dtype), shapes)

    return lax.cond(flag, fn, idle, *args)


def norm_fwd(x, gain, bias):
    mean = jnp.mean(x, -1, keepdims=True)
    centred = x - mean
    var = jnp.mean(centred * centred, -1, keepdims=True)
    rstd = lax.rsqrt(var + EPS)
    xhat = centred * rstd
    return xhat * gain + bias, (xhat, rstd)


def norm_bwd(dy, saved, gain):
    xhat, rstd = saved
    lead = tuple(range(dy.ndim - 1))
    d_gain = jnp.sum(dy * xhat, lead)
    d_bias = jnp.sum(dy, lead)
    dxh = dy * gain
    dx = rstd * (
        dxh
        - jnp.mean(dxh, -1, keepdims=True)
        - xhat * jnp.mean(dxh * xhat, -1, keepdims=True)
    )
    return dx, d_gain, d_bias


def mm(a, w):
    return jnp.einsum("...d,de->...e", a, w, preferred_element_type=F32)


def mm_t(g, w):
    return jnp.einsum("...e,de->...d", g, w, preferred_element_type=F32)


def outer(a, b):
    return jnp.einsum("rtd,rte->de", a, b, preferred_element_type=F32)


def softmax_rows(s, axes):
    top = jnp.max(s, axes, keepdims=True)
    e = jnp.exp(s - top)
    return e / jnp.sum(e, axes, keepdims=True)


def self_fwd(h, seg, gain, bias, w_qkv, w_out):
    r, t = seg.shape
    y, nsave = norm_fwd(h, gain, bias)
    n = bf(y)
    trip = bf(mm(n, w_qkv)).reshape(r, t, 3, H, HD)
    q, k, v = trip[:, :, 0], trip[:, :, 1], trip[:, :, 2]
    pos = jnp.arange(t)
    allowed = (seg[:, :, None] == seg[:, None, :]) & (pos[:, None] >= pos[None, :])[None]
    s = jnp.einsum("rqhd,rkhd->rhqk", q, k, preferred_element_type=F32) * SCALE
    s = jnp.where(allowed[:, None], s, MASKED)
    p = softmax_rows(s, -1)
    o = bf(jnp.einsum("rhqk,rkhd->rqhd", bf(p), v, preferred_element_type=F32))
    o = o.reshape(r, t, H * HD)
    h2 = h + mm(o, w_out)
    saved = dict(nsave=nsave, n=n, q=q, k=k, v=v, p=p, o=o)
    return h2, saved


def self_bwd(dh2, sv, gain, w_qkv, w_out):
    r, t = dh2.shape[:2]
    g2 = bf(dh2)
    do = bf(mm_t(g2, w_out)).reshape(r, t, H, HD)
    p, q, k, v = sv["p"], sv["q"], sv["k"], sv["v"]
    dp = jnp.einsum("rqhd,rkhd->rhqk", do, v, preferred_element_type=F32)
    ds = bf(p * (dp - jnp.sum(p * dp, -1, keepdims=True)))
    dq = jnp.einsum("rhqk,rkhd->rqhd", ds, k, preferred_element_type=F32) * SCALE
    dk = jnp.einsum("rhqk,rqhd->rkhd", ds, q, preferred_element_type=F32) * SCALE
    dv = jnp.einsum("rhqk,rqhd->rkhd", bf(p), do, preferred_element_type=F32)
    dt = bf(jnp.stack([dq, dk, dv], 2)).reshape(r, t, 3 * H * HD)
    dn = mm_t(dt, w_qkv)
    dx, d_gain, d_bias = norm_bwd(dn, sv["nsave"], gain)
    pairs = dict(o=sv["o"], g2=g2, n=sv["n"], dt=dt)
    return dh2 + dx, (d_gain, d_bias), pairs


RB = 2


def _dot_nt(a, b):
    return lax.dot_general(a, b, (((1,), (1,)), ((), ())), preferred_element_type=F32)


def _dot_tn(a, b):
    return lax.dot_general(a, b, (((0,), (0,)), ((), ())), preferred_element_type=F32)


def _dot(a, b):
    return lax.dot_general(a, b, (((1,), (0,)), ((), ())), preferred_element_type=F32)


def _probs(q, ka, kb, first):
    sa = _dot_nt(q, ka) * SCALE
    sb = _dot_nt(q, kb) * SCALE
    s = jnp.where(first, sa, sb)
    top = jnp.max(s, -1, keepdims=True)
    e = jnp.exp(s - top)
    return e / jnp.sum(e, -1, keepdims=True)


def _fwd_kernel(slot_ref, cut_ref, q_ref, pool_ref, o_ref):
    i = pl.program_id(0)
    t = q_ref.shape[1]
    d = H * HD
    for j in range(RB):
        r = i * RB + j
        a = slot_ref[2 * r]
        b = slot_ref[2 * r + 1]
        first = lax.broadcasted_iota(jnp.int32, (t, 1), 0) < cut_ref[r]
        for h in range(H):
            cols = pl.ds(h * HD, HD)
            vcols = pl.ds(d + h * HD, HD)
            q = q_ref[j, :, cols]
            p = _probs(q, pool_ref[a, :, cols], pool_ref[b, :, cols], first).astype(BF16)
            zero = jnp.zeros_like(p)
            o = _dot(jnp.where(first, p, zero), pool_ref[a, :, vcols]) + _dot(
                jnp.where(first, zero, p), pool_ref[b, :, vcols]
            )
            o_ref[j, :, cols] = o.astype(o_ref.dtype)


def _bwd_kernel(slot_ref, cut_ref, q_ref, do_ref, pool_ref, dq_ref, dpool_ref):
    i = pl.program_id(0)
    t = q_ref.shape[1]
    d = H * HD

    @pl.when(i == 0)
    def _():
        dpool_ref[...] = jnp.zeros_like(dpool_ref)

    for j in range(RB):
        r = i * RB + j
        a = slot_ref[2 * r]
        b = slot_ref[2 * r + 1]
        first = lax.broadcasted_iota(jnp.int32, (t, 1), 0) < cut_ref[r]
        for h in range(H):
            cols = pl.ds(h * HD, HD)
            vcols = pl.ds(d + h * HD, HD)
            q = q_ref[j, :, cols]
            do = do_ref[j, :, cols]
            ka = pool_ref[a, :, cols]
            kb = pool_ref[b, :, cols]
            va = pool_ref[a, :, vcols]
            vb = pool_ref[b, :, vcols]
            p = _probs(q, ka, kb, first)
            dp = jnp.where(first, _dot_nt(do, va), _dot_nt(do, vb))
            ds = (p * (dp - jnp.sum(p * dp, -1, keepdims=True))).astype(BF16)
            zero = jnp.zeros_like(ds)
            dsa = jnp.where(first, ds, zero)
            dsb = jnp.where(first, zero, ds)
            dq = (_dot(dsa, ka) + _dot(dsb, kb)) * SCALE
            dq_ref[j, :, cols] = dq.astype(dq_ref.dtype)
            pb = p.astype(BF16)
            pa_ = jnp.where(first, pb, zero)
            pb_ = jnp.where(first, zero, pb)
            dpool_ref[a, :, cols] += _dot_tn(dsa, q) * SCALE
            dpool_ref[a, :, vcols] += _dot_tn(pa_, do)
            dpool_ref[b, :, cols] += _dot_tn(dsb, q) * SCALE
            dpool_ref[b, :, vcols] += _dot_tn(pb_, do)


def cross_attention_fwd(qc, pool, slots, cuts):
    r, t, d = qc.shape
    spec = pltpu.PrefetchScalarGridSpec(
        num_scalar_prefetch=2,
        grid=(r // RB,),
        in_specs=[
            pl.BlockSpec((RB, t, d), lambda i, s, c: (i, 0, 0)),
            pl.BlockSpec(pool.shape, lambda i, s, c: (0, 0, 0)),
        ],
        out_specs=pl.BlockSpec((RB, t, d), lambda i, s, c: (i, 0, 0)),
    )
    flops = r * H * 4 * 2 * t * pool.shape[1] * HD
    return pl.pallas_call(
        _fwd_kernel,
        grid_spec=spec,
        out_shape=jax.ShapeDtypeStruct((r, t, d), BF16),
        compiler_params=pltpu.CompilerParams(
            dimension_semantics=("arbitrary",), vmem_limit_bytes=48 * 1024 * 1024
        ),
        cost_estimate=pl.CostEstimate(
            flops=flops,
            transcendentals=r * H * t * 2 * pool.shape[1],
            bytes_accessed=2 * qc.size * 2 + pool.size * 2,
        ),
    )(slots.reshape(-1), cuts, qc, pool)


def cross_attention_bwd(qc, doc, pool, slots, cuts):
    r, t, d = qc.shape
    spec = pltpu.PrefetchScalarGridSpec(
        num_scalar_prefetch=2,
        grid=(r // RB,),
        in_specs=[
            pl.BlockSpec((RB, t, d), lambda i, s, c: (i, 0, 0)),
            pl.BlockSpec((RB, t, d), lambda i, s, c: (i, 0, 0)),
            pl.BlockSpec(pool.shape, lambda i, s, c: (0, 0, 0)),
        ],
        out_specs=[
            pl.BlockSpec((RB, t, d), lambda i, s, c: (i, 0, 0)),
            pl.BlockSpec(pool.shape, lambda i, s, c: (0, 0, 0)),
        ],
    )
    flops = r * H * 10 * 2 * t * pool.shape[1] * HD
    return pl.pallas_call(
        _bwd_kernel,
        grid_spec=spec,
        out_shape=(
            jax.ShapeDtypeStruct((r, t, d), BF16),
            jax.ShapeDtypeStruct(pool.shape, F32),
        ),
        compiler_params=pltpu.CompilerParams(
            dimension_semantics=("arbitrary",), vmem_limit_bytes=60 * 1024 * 1024
        ),
        cost_estimate=pl.CostEstimate(
            flops=flops,
            transcendentals=r * H * t * 2 * pool.shape[1],
            bytes_accessed=3 * qc.size * 2 + pool.size * 2 + pool.size * 4,
        ),
    )(slots.reshape(-1), cuts, qc, doc, pool)


def cross_fwd(h2, slots, cuts, pool, gain, bias, wq, wo):
    y, csave = norm_fwd(h2, gain, bias)
    c = bf(y)
    qc = bf(mm(c, wq))
    oc = cross_attention_fwd(qc, pool, slots, cuts)
    h3 = h2 + mm(oc, wo)
    return h3, dict(csave=csave, c=c, qc=qc, oc=oc)


def cross_bwd(dh3, sv, slots, cuts, pool, gain, wq, wo):
    g3 = bf(dh3)
    doc = bf(mm_t(g3, wo))
    dqc, dpool = cross_attention_bwd(sv["qc"], doc, pool, slots, cuts)
    dc = mm_t(dqc, wq)
    dx, d_gain, d_bias = norm_bwd(dc, sv["csave"], gain)
    pairs = dict(oc=sv["oc"], g3=g3, c=sv["c"], dqc=dqc)
    return dh3 + dx, (d_gain, d_bias), pairs, dpool


def gelu(z):
    return jax.nn.gelu(z, approximate=False)


def ffn_fwd(h3, gain, bias, w_up, b_up, w_down, b_down):
    y, usave = norm_fwd(h3, gain, bias)
    u = bf(y)
    z = mm(u, w_up) + b_up
    f = bf(gelu(z))
    out = h3 + (mm(f, w_down) + b_down)
    return out, dict(usave=usave, u=u, z=z, f=f)


def ffn_bwd(gout, sv, gain, w_up, w_down):
    gb = bf(gout)
    df = mm_t(gb, w_down)
    _, pull = jax.vjp(gelu, sv["z"])
    dz = bf(pull(df)[0])
    du = mm_t(dz, w_up)
    dx, d_gain, d_bias = norm_bwd(du, sv["usave"], gain)
    pairs = dict(f=sv["f"], gb=gb, u=sv["u"], dz=dz)
    return gout + dx, (d_gain, d_bias), pairs


def per_device(
    inputs,
    cotangent,
    images,
    seg_ids,
    row_block,
    seg_image,
    ln1_gain,
    ln1_bias,
    w_qkv,
    w_out,
    ln2_gain,
    ln2_bias,
    w_up,
    b_up,
    w_down,
    b_down,
    lnc_gain,
    lnc_bias,
    wq_cross,
    wkv_cross,
    wo_cross,
):
    up = lax.axis_index("section") == 1
    low = jnp.logical_not(up)
    dp_index = lax.axis_index("dp")
    n_dp = lax.axis_size("dp")
    rows = inputs.shape[0]
    rc = rows // MICRO
    g1, b1, wqkv, wout = ln1_gain[0], ln1_bias[0], w_qkv[0], w_out[0]
    g2, b2, wup, bup, wdown, bdown = ln2_gain[0], ln2_bias[0], w_up[0], b_up[0], w_down[0], b_down[0]
    n_img = n_dp * images.shape[0]

    first_half = lax.ppermute(images[0], "section", [(0, 1)])
    full_image = jnp.concatenate([first_half, images[0]], 0)

    def make_kv(img):
        return bf(mm(img, wkv_cross))

    kv_own = run_on(up, make_kv, full_image)
    ring_up = [(i, (i + 1) % n_dp) for i in range(n_dp)]
    ring_down = [((i + 1) % n_dp, i) for i in range(n_dp)]
    kv_prev = lax.ppermute(kv_own, "dp", ring_up)
    kv_next = lax.ppermute(kv_own, "dp", ring_down)
    pool = jnp.stack([kv_prev, kv_own, kv_next], 0)
    img_tok = pool.shape[1]

    first_img = (row_block[:, None] + seg_image) % n_img
    slot = (first_img - dp_index + 1 + n_img) % n_img
    cut_all = jnp.sum((seg_ids == 0).astype(jnp.int32), 1)

    def chunk(a, m):
        return a[m * rc : (m + 1) * rc]

    x = inputs.astype(F32)

    def lower_fwd(hid, seg):
        h2, s_self = self_fwd(hid, seg, g1, b1, wqkv, wout)
        out, s_ffn = ffn_fwd(h2, g2, b2, wup, bup, wdown, bdown)
        return out, (s_self, s_ffn)

    def upper_fwd(sent, seg, slots, cuts, pool):
        hid = sent.astype(F32)
        h2, s_self = self_fwd(hid, seg, g1, b1, wqkv, wout)
        h3, s_cross = cross_fwd(h2, slots, cuts, pool, lnc_gain, lnc_bias, wq_cross, wo_cross)
        out, s_ffn = ffn_fwd(h3, g2, b2, wup, bup, wdown, bdown)
        return out, (s_self, s_cross, s_ffn)

    low_out, low_saved, sent = [], [], []
    for m in range(MICRO):
        x_m = chunk(x, m)
        if m > 0:
            x_m, low_out[-1] = lax.optimization_barrier((x_m, low_out[-1]))
        out, saved = run_on(low, lower_fwd, x_m, chunk(seg_ids, m))
        low_out.append(out)
        low_saved.append(saved)
        sent.append(lax.ppermute(bf(out), "section", [(0, 1)]))
    up_out, up_saved = [], []
    for m in range(MICRO):
        arriving = sent[m]
        if m > 0:
            arriving, up_out[-1] = lax.optimization_barrier((arriving, up_out[-1]))
        out, saved = run_on(
            up, upper_fwd, arriving, chunk(seg_ids, m), chunk(slot, m), chunk(cut_all, m), pool
        )
        up_out.append(out)
        up_saved.append(saved)

    cot = cotangent[0].astype(F32)

    def upper_bwd(gout, saved, slots, cuts, pool):
        s_self, s_cross, s_ffn = saved
        dh3, ln2g, pf = ffn_bwd(gout, s_ffn, g2, wup, wdown)
        dh2, lncg, pc, dpool = cross_bwd(dh3, s_cross, slots, cuts, pool, lnc_gain, wq_cross, wo_cross)
        dh, ln1g, ps = self_bwd(dh2, s_self, g1, wqkv, wout)
        return dh, (ln1g, ln2g, lncg), (ps, pf, pc), dpool

    up_grad, up_small, up_pairs = [], [], []
    returned = []
    pool_grad = None
    for m in range(MICRO):
        cot_m = chunk(cot, m)
        if m > 0:
            cot_m, up_grad[-1] = lax.optimization_barrier((cot_m, up_grad[-1]))
        dh, small, pairs, dpool = run_on(
            up, upper_bwd, cot_m, up_saved[m], chunk(slot, m), chunk(cut_all, m), pool
        )
        up_grad.append(dh)
        up_small.append(small)
        up_pairs.append(pairs)
        pool_grad = dpool if pool_grad is None else pool_grad + dpool
        returned.append(lax.ppermute(bf(dh), "section", [(1, 0)]))

    def cat(name_path, pairs_list):
        return jnp.concatenate([name_path(p) for p in pairs_list], 0)

    def layer_weight_grads(pairs_list):
        ps = lambda i, k: cat(lambda p: p[i][k], pairs_list)
        d_wqkv = outer(ps(0, "n"), ps(0, "dt"))
        d_wout = outer(ps(0, "o"), ps(0, "g2"))
        d_wup = outer(ps(1, "u"), ps(1, "dz"))
        d_wdown = outer(ps(1, "f"), ps(1, "gb"))
        d_bup = jnp.sum(ps(1, "dz").astype(F32), (0, 1))
        d_bdown = jnp.sum(ps(1, "gb").astype(F32), (0, 1))
        return d_wqkv, d_wout, d_wup, d_bup, d_wdown, d_bdown

    def upper_wgrads(pairs_list):
        layer = layer_weight_grads(pairs_list)
        ps = lambda k: cat(lambda p: p[2][k], pairs_list)
        d_wq = outer(ps("c"), ps("dqc"))
        d_wo = outer(ps("oc"), ps("g3"))
        return layer, (d_wq, d_wo)

    up_w, cross_w = run_on(up, upper_wgrads, up_pairs)

    parts = bf(pool_grad)
    from_next = lax.ppermute(parts[0], "dp", ring_down)
    from_prev = lax.ppermute(parts[2], "dp", ring_up)
    kv_grad = bf(parts[1].astype(F32) + from_next.astype(F32) + from_prev.astype(F32))

    def image_side(kvg, img):
        ig = jnp.einsum("te,de->td", kvg, wkv_cross, preferred_element_type=F32)
        dw = jnp.einsum("td,te->de", img, kvg, preferred_element_type=F32)
        return ig, dw

    image_grad_full, d_wkv = run_on(up, image_side, kv_grad, full_image)
    half = images.shape[1]
    ig_first = lax.ppermute(image_grad_full[:half], "section", [(1, 0)])
    image_grad = jnp.where(up, image_grad_full[half:], ig_first)[None]

    def tree_sum(xs):
        total = xs[0]
        for v in xs[1:]:
            total = jax.tree.map(jnp.add, total, v)
        return total

    def rs(a, dim=0):
        return lax.psum_scatter(a, "dp", scatter_dimension=dim, tiled=True)

    def rs_bf(a, dim=0):
        return rs(bf(a), dim).astype(F32)

    def pack(vs):
        return jnp.concatenate([v.reshape(n_dp, -1) for v in vs], 1)

    def unpack(row, vs):
        out, at = [], 0
        for v in vs:
            width = v.size // n_dp
            out.append(row[:, at : at + width])
            at += width
        return out

    def reduce_layer(lw, sm):
        d_wqkv, d_wout, d_wup, d_bup, d_wdown, d_bdown = lw
        big = [rs_bf(d_wqkv), rs_bf(d_wout), rs_bf(d_wup), rs_bf(d_wdown)]
        vecs = [sm[0][0], sm[0][1], sm[1][0], sm[1][1], d_bup, d_bdown]
        return big, vecs

    up_sm = tree_sum(up_small)
    a_big, a_vecs = reduce_layer(up_w, up_sm)
    a_cross = [rs_bf(cross_w[0]), rs_bf(cross_w[1]), rs_bf(d_wkv)]
    a_vecs = a_vecs + [up_sm[2][0], up_sm[2][1]]
    a_small = unpack(rs(pack(a_vecs)), a_vecs)

    def lower_bwd(gout, saved):
        s_self, s_ffn = saved
        dh3, ln2g, pf = ffn_bwd(gout, s_ffn, g2, wup, wdown)
        dh, ln1g, ps = self_bwd(dh3, s_self, g1, wqkv, wout)
        return dh, (ln1g, ln2g), (ps, pf)

    low_grad, low_small, low_pairs = [], [], []
    for m in range(MICRO):
        gout = chunk(cot, m) + returned[m].astype(F32)
        if m == 0:
            gout, (a_big, a_small, a_cross) = lax.optimization_barrier(
                (gout, (a_big, a_small, a_cross))
            )
        else:
            gout, low_grad[-1] = lax.optimization_barrier((gout, low_grad[-1]))
        dh, small, pairs = run_on(low, lower_bwd, gout, low_saved[m])
        low_grad.append(dh)
        low_small.append(small)
        low_pairs.append(pairs)

    low_w = run_on(low, layer_weight_grads, low_pairs)
    low_sm = tree_sum(low_small)
    low_w, low_sm, (a_big, a_small, a_cross) = lax.optimization_barrier(
        (low_w, low_sm, (a_big, a_small, a_cross))
    )
    b_big, b_vecs = reduce_layer(low_w, low_sm)
    b_small = unpack(rs(pack(b_vecs)), b_vecs)

    cross_out = a_cross + a_small[6:]
    cross_out, (b_big, b_small) = lax.optimization_barrier((cross_out, (b_big, b_small)))
    cross_copy = lax.ppermute(cross_out, "section", [(1, 0)])
    cross_out = [jnp.where(up, a, c) for a, c in zip(cross_out, cross_copy)]

    activations = jnp.where(
        up, jnp.concatenate(up_out, 0), jnp.concatenate(low_out, 0)
    )[None]
    back_grads = jnp.where(
        up, jnp.concatenate(up_grad, 0), jnp.concatenate(low_grad, 0)
    )[None]
    big = [jnp.where(up, a, b)[None] for a, b in zip(a_big, b_big)]
    small = [jnp.where(up, a, b) for a, b in zip(a_small[:6], b_small)]
    d_wq, d_wo, d_wkv_sh, lnc_g, lnc_b = cross_out

    return (
        activations,
        back_grads,
        image_grad,
        small[0],
        small[1],
        big[0],
        big[1],
        small[2],
        small[3],
        big[2],
        small[4],
        big[3],
        small[5],
        lnc_g[0],
        lnc_b[0],
        d_wq,
        d_wkv_sh,
        d_wo,
    )


def solution(mesh):
    placed = (
        P("dp", None, None),
        P("section", "dp", None, None),
        P("dp", "section", None),
        P("dp", None),
        P("dp"),
        P("dp", None),
        P("section", None),
        P("section", None),
        P("section", None, None),
        P("section", None, None),
        P("section", None),
        P("section", None),
        P("section", None, None),
        P("section", None),
        P("section", None, None),
        P("section", None),
        P(),
        P(),
        P(),
        P(),
        P(),
    )
    return jax.shard_map(
        per_device,
        mesh=mesh,
        in_specs=placed,
        out_specs=(
            P("section", "dp", None, None),
            P("section", "dp", None, None),
            P("dp", "section", None),
            P("section", "dp"),
            P("section", "dp"),
            P("section", "dp", None),
            P("section", "dp", None),
            P("section", "dp"),
            P("section", "dp"),
            P("section", "dp", None),
            P("section", "dp"),
            P("section", "dp", None),
            P("section", "dp"),
            P("dp"),
            P("dp"),
            P("dp", None),
            P("dp", None),
            P("dp", None),
        ),
        check_vma=False,
    )
```

```python
from functools import partial

import jax
import jax.numpy as jnp
from jax import lax
from jax.experimental import pallas as pl
from jax.experimental.pallas import tpu as pltpu
from jax.sharding import PartitionSpec as P

H = 12
HD = 64
MICRO = 2

EPS = 1e-05
MASKED = -1e30
SCALE = HD ** (-0.5)
F32 = jnp.float32
BF16 = jnp.bfloat16


def bf(x):
    return x.astype(BF16)


def run_on(flag, fn, *args):
    shapes = jax.eval_shape(fn, *args)

    def idle(*unused):
        return jax.tree.map(lambda s: jnp.zeros(s.shape, s.dtype), shapes)

    return lax.cond(flag, fn, idle, *args)


def norm_fwd(x, gain, bias):
    mean = jnp.mean(x, -1, keepdims=True)
    centred = x - mean
    var = jnp.mean(centred * centred, -1, keepdims=True)
    rstd = lax.rsqrt(var + EPS)
    xhat = centred * rstd
    return xhat * gain + bias, (xhat, rstd)


def norm_bwd(dy, saved, gain):
    xhat, rstd = saved
    lead = tuple(range(dy.ndim - 1))
    d_gain = jnp.sum(dy * xhat, lead)
    d_bias = jnp.sum(dy, lead)
    dxh = dy * gain
    dx = rstd * (
        dxh
        - jnp.mean(dxh, -1, keepdims=True)
        - xhat * jnp.mean(dxh * xhat, -1, keepdims=True)
    )
    return dx, d_gain, d_bias


def mm(a, w):
    return jnp.einsum("...d,de->...e", a, w, preferred_element_type=F32)


def mm_t(g, w):
    return jnp.einsum("...e,de->...d", g, w, preferred_element_type=F32)


def outer(a, b):
    return jnp.einsum("rtd,rte->de", a, b, preferred_element_type=F32)


def softmax_rows(s, axes):
    top = jnp.max(s, axes, keepdims=True)
    e = jnp.exp(s - top)
    return e / jnp.sum(e, axes, keepdims=True)


def self_fwd(h, seg, gain, bias, w_qkv, w_out):
    r, t = seg.shape
    y, nsave = norm_fwd(h, gain, bias)
    n = bf(y)
    trip = bf(mm(n, w_qkv)).reshape(r, t, 3, H, HD)
    q, k, v = trip[:, :, 0], trip[:, :, 1], trip[:, :, 2]
    pos = jnp.arange(t)
    allowed = (seg[:, :, None] == seg[:, None, :]) & (pos[:, None] >= pos[None, :])[None]
    s = jnp.einsum("rqhd,rkhd->rhqk", q, k, preferred_element_type=F32) * SCALE
    s = jnp.where(allowed[:, None], s, MASKED)
    p = softmax_rows(s, -1)
    o = bf(jnp.einsum("rhqk,rkhd->rqhd", bf(p), v, preferred_element_type=F32))
    o = o.reshape(r, t, H * HD)
    h2 = h + mm(o, w_out)
    saved = dict(nsave=nsave, n=n, q=q, k=k, v=v, p=p, o=o)
    return h2, saved


def self_bwd(dh2, sv, gain, w_qkv, w_out):
    r, t = dh2.shape[:2]
    g2 = bf(dh2)
    do = bf(mm_t(g2, w_out)).reshape(r, t, H, HD)
    p, q, k, v = sv["p"], sv["q"], sv["k"], sv["v"]
    dp = jnp.einsum("rqhd,rkhd->rhqk", do, v, preferred_element_type=F32)
    ds = bf(p * (dp - jnp.sum(p * dp, -1, keepdims=True)))
    dq = jnp.einsum("rhqk,rkhd->rqhd", ds, k, preferred_element_type=F32) * SCALE
    dk = jnp.einsum("rhqk,rqhd->rkhd", ds, q, preferred_element_type=F32) * SCALE
    dv = jnp.einsum("rhqk,rqhd->rkhd", bf(p), do, preferred_element_type=F32)
    dt = bf(jnp.stack([dq, dk, dv], 2)).reshape(r, t, 3 * H * HD)
    dn = mm_t(dt, w_qkv)
    dx, d_gain, d_bias = norm_bwd(dn, sv["nsave"], gain)
    pairs = dict(o=sv["o"], g2=g2, n=sv["n"], dt=dt)
    return dh2 + dx, (d_gain, d_bias), pairs


RB = 2


def _dot_nt(a, b):
    return lax.dot_general(a, b, (((1,), (1,)), ((), ())), preferred_element_type=F32)


def _dot_tn(a, b):
    return lax.dot_general(a, b, (((0,), (0,)), ((), ())), preferred_element_type=F32)


def _dot(a, b):
    return lax.dot_general(a, b, (((1,), (0,)), ((), ())), preferred_element_type=F32)


def _probs(q, ka, kb, first):
    sa = _dot_nt(q, ka) * SCALE
    sb = _dot_nt(q, kb) * SCALE
    s = jnp.where(first, sa, sb)
    top = jnp.max(s, -1, keepdims=True)
    e = jnp.exp(s - top)
    return e / jnp.sum(e, -1, keepdims=True)


def _fwd_kernel(slot_ref, cut_ref, q_ref, pool_ref, o_ref):
    i = pl.program_id(0)
    t = q_ref.shape[1]
    d = H * HD
    for j in range(RB):
        r = i * RB + j
        a = slot_ref[2 * r]
        b = slot_ref[2 * r + 1]
        first = lax.broadcasted_iota(jnp.int32, (t, 1), 0) < cut_ref[r]
        for h in range(H):
            cols = pl.ds(h * HD, HD)
            vcols = pl.ds(d + h * HD, HD)
            q = q_ref[j, :, cols]
            p = _probs(q, pool_ref[a, :, cols], pool_ref[b, :, cols], first).astype(BF16)
            zero = jnp.zeros_like(p)
            o = _dot(jnp.where(first, p, zero), pool_ref[a, :, vcols]) + _dot(
                jnp.where(first, zero, p), pool_ref[b, :, vcols]
            )
            o_ref[j, :, cols] = o.astype(o_ref.dtype)


def _bwd_kernel(slot_ref, cut_ref, q_ref, do_ref, pool_ref, dq_ref, dpool_ref):
    i = pl.program_id(0)
    t = q_ref.shape[1]
    d = H * HD

    @pl.when(i == 0)
    def _():
        dpool_ref[...] = jnp.zeros_like(dpool_ref)

    for j in range(RB):
        r = i * RB + j
        a = slot_ref[2 * r]
        b = slot_ref[2 * r + 1]
        first = lax.broadcasted_iota(jnp.int32, (t, 1), 0) < cut_ref[r]
        for h in range(H):
            cols = pl.ds(h * HD, HD)
            vcols = pl.ds(d + h * HD, HD)
            q = q_ref[j, :, cols]
            do = do_ref[j, :, cols]
            ka = pool_ref[a, :, cols]
            kb = pool_ref[b, :, cols]
            va = pool_ref[a, :, vcols]
            vb = pool_ref[b, :, vcols]
            p = _probs(q, ka, kb, first)
            dp = jnp.where(first, _dot_nt(do, va), _dot_nt(do, vb))
            ds = (p * (dp - jnp.sum(p * dp, -1, keepdims=True))).astype(BF16)
            zero = jnp.zeros_like(ds)
            dsa = jnp.where(first, ds, zero)
            dsb = jnp.where(first, zero, ds)
            dq = (_dot(dsa, ka) + _dot(dsb, kb)) * SCALE
            dq_ref[j, :, cols] = dq.astype(dq_ref.dtype)
            pb = p.astype(BF16)
            pa_ = jnp.where(first, pb, zero)
            pb_ = jnp.where(first, zero, pb)
            dpool_ref[a, :, cols] += _dot_tn(dsa, q) * SCALE
            dpool_ref[a, :, vcols] += _dot_tn(pa_, do)
            dpool_ref[b, :, cols] += _dot_tn(dsb, q) * SCALE
            dpool_ref[b, :, vcols] += _dot_tn(pb_, do)


def cross_attention_fwd(qc, pool, slots, cuts):
    r, t, d = qc.shape
    spec = pltpu.PrefetchScalarGridSpec(
        num_scalar_prefetch=2,
        grid=(r // RB,),
        in_specs=[
            pl.BlockSpec((RB, t, d), lambda i, s, c: (i, 0, 0)),
            pl.BlockSpec(pool.shape, lambda i, s, c: (0, 0, 0)),
        ],
        out_specs=pl.BlockSpec((RB, t, d), lambda i, s, c: (i, 0, 0)),
    )
    flops = r * H * 4 * 2 * t * pool.shape[1] * HD
    return pl.pallas_call(
        _fwd_kernel,
        grid_spec=spec,
        out_shape=jax.ShapeDtypeStruct((r, t, d), BF16),
        compiler_params=pltpu.CompilerParams(
            dimension_semantics=("arbitrary",), vmem_limit_bytes=48 * 1024 * 1024
        ),
        cost_estimate=pl.CostEstimate(
            flops=flops,
            transcendentals=r * H * t * 2 * pool.shape[1],
            bytes_accessed=2 * qc.size * 2 + pool.size * 2,
        ),
    )(slots.reshape(-1), cuts, qc, pool)


def cross_attention_bwd(qc, doc, pool, slots, cuts):
    r, t, d = qc.shape
    spec = pltpu.PrefetchScalarGridSpec(
        num_scalar_prefetch=2,
        grid=(r // RB,),
        in_specs=[
            pl.BlockSpec((RB, t, d), lambda i, s, c: (i, 0, 0)),
            pl.BlockSpec((RB, t, d), lambda i, s, c: (i, 0, 0)),
            pl.BlockSpec(pool.shape, lambda i, s, c: (0, 0, 0)),
        ],
        out_specs=[
            pl.BlockSpec((RB, t, d), lambda i, s, c: (i, 0, 0)),
            pl.BlockSpec(pool.shape, lambda i, s, c: (0, 0, 0)),
        ],
    )
    flops = r * H * 10 * 2 * t * pool.shape[1] * HD
    return pl.pallas_call(
        _bwd_kernel,
        grid_spec=spec,
        out_shape=(
            jax.ShapeDtypeStruct((r, t, d), BF16),
            jax.ShapeDtypeStruct(pool.shape, F32),
        ),
        compiler_params=pltpu.CompilerParams(
            dimension_semantics=("arbitrary",), vmem_limit_bytes=60 * 1024 * 1024
        ),
        cost_estimate=pl.CostEstimate(
            flops=flops,
            transcendentals=r * H * t * 2 * pool.shape[1],
            bytes_accessed=3 * qc.size * 2 + pool.size * 2 + pool.size * 4,
        ),
    )(slots.reshape(-1), cuts, qc, doc, pool)


def cross_fwd(h2, slots, cuts, pool, gain, bias, wq, wo):
    y, csave = norm_fwd(h2, gain, bias)
    c = bf(y)
    qc = bf(mm(c, wq))
    oc = cross_attention_fwd(qc, pool, slots, cuts)
    h3 = h2 + mm(oc, wo)
    return h3, dict(csave=csave, c=c, qc=qc, oc=oc)


def cross_bwd(dh3, sv, slots, cuts, pool, gain, wq, wo):
    g3 = bf(dh3)
    doc = bf(mm_t(g3, wo))
    dqc, dpool = cross_attention_bwd(sv["qc"], doc, pool, slots, cuts)
    dc = mm_t(dqc, wq)
    dx, d_gain, d_bias = norm_bwd(dc, sv["csave"], gain)
    pairs = dict(oc=sv["oc"], g3=g3, c=sv["c"], dqc=dqc)
    return dh3 + dx, (d_gain, d_bias), pairs, dpool


def gelu(z):
    return jax.nn.gelu(z, approximate=False)


def ffn_fwd(h3, gain, bias, w_up, b_up, w_down, b_down):
    y, usave = norm_fwd(h3, gain, bias)
    u = bf(y)
    z = mm(u, w_up) + b_up
    f = bf(gelu(z))
    out = h3 + (mm(f, w_down) + b_down)
    return out, dict(usave=usave, u=u, z=z, f=f)


def ffn_bwd(gout, sv, gain, w_up, w_down):
    gb = bf(gout)
    df = mm_t(gb, w_down)
    _, pull = jax.vjp(gelu, sv["z"])
    dz = bf(pull(df)[0])
    du = mm_t(dz, w_up)
    dx, d_gain, d_bias = norm_bwd(du, sv["usave"], gain)
    pairs = dict(f=sv["f"], gb=gb, u=sv["u"], dz=dz)
    return gout + dx, (d_gain, d_bias), pairs


def chip_cycle(mesh):
    n_dp = mesh.shape["dp"]
    plane = mesh.devices.reshape(-1, n_dp)[0]
    try:
        chips = {}
        for i, dev in enumerate(plane):
            chips.setdefault(tuple(dev.coords), []).append(i)
    except AttributeError:
        return list(range(n_dp))
    keys = sorted(chips)
    if len(keys) < 3:
        return [i for k in keys for i in sorted(chips[k])]
    near = {
        k: [j for j in keys if sum(abs(a - b) for a, b in zip(k, j)) == 1] for k in keys
    }
    path, seen, budget = [keys[0]], {keys[0]}, [200000]

    def walk():
        budget[0] -= 1
        if budget[0] < 0:
            return False
        if len(path) == len(keys):
            return keys[0] in near[path[-1]]
        options = sorted(
            (j for j in near[path[-1]] if j not in seen),
            key=lambda j: sum(1 for n in near[j] if n not in seen),
        )
        for j in options:
            path.append(j)
            seen.add(j)
            if walk():
                return True
            path.pop()
            seen.discard(j)
        return False

    if not walk():
        return list(range(n_dp))
    return [i for k in path for i in sorted(chips[k])]


def ring_reduce_scatter(packed, plane, cycle, dp_index):
    n = len(cycle)
    n_dp = packed.shape[0]
    axes = ("section", "dp")
    fwd = [(plane * n_dp + cycle[i], plane * n_dp + cycle[(i + 1) % n]) for i in range(n)]
    bwd = [(b, a) for a, b in fwd]
    where_in = [0] * n
    for i, d in enumerate(cycle):
        where_in[d] = i
    rows = packed[jnp.array(cycle, jnp.int32)]
    half = rows.shape[1] // 2
    cw, ccw = rows[:, :half], rows[:, half:]
    p = jnp.array(where_in, jnp.int32)[dp_index]

    def take(a, idx):
        return lax.dynamic_index_in_dim(a, idx % n, 0, keepdims=False)

    send_c, send_w = take(cw, p - 1), take(ccw, p + 1)
    for step in range(n - 1):
        got_c = lax.ppermute(send_c, axes, fwd)
        got_w = lax.ppermute(send_w, axes, bwd)
        acc_c = got_c.astype(F32) + take(cw, p - step - 2).astype(F32)
        acc_w = got_w.astype(F32) + take(ccw, p + step + 2).astype(F32)
        send_c, send_w = bf(acc_c), bf(acc_w)
    return jnp.concatenate([acc_c, acc_w], 0)


def pack_rows(arrays, n):
    flat = [bf(a).reshape(n, -1) for a in arrays]
    width = sum(f.shape[1] for f in flat)
    if width % 2:
        flat.append(jnp.zeros((n, 1), BF16))
    return jnp.concatenate(flat, 1)


def unpack_row(row, arrays, n):
    out, at = [], 0
    for a in arrays:
        size = a.size // n
        out.append(row[at : at + size].reshape((a.shape[0] // n,) + a.shape[1:]))
        at += size
    return out


def per_device(
    cycle,
    inputs,
    cotangent,
    images,
    seg_ids,
    row_block,
    seg_image,
    ln1_gain,
    ln1_bias,
    w_qkv,
    w_out,
    ln2_gain,
    ln2_bias,
    w_up,
    b_up,
    w_down,
    b_down,
    lnc_gain,
    lnc_bias,
    wq_cross,
    wkv_cross,
    wo_cross,
):
    up = lax.axis_index("section") == 1
    low = jnp.logical_not(up)
    dp_index = lax.axis_index("dp")
    n_dp = lax.axis_size("dp")
    rows = inputs.shape[0]
    rc = rows // MICRO
    g1, b1, wqkv, wout = ln1_gain[0], ln1_bias[0], w_qkv[0], w_out[0]
    g2, b2, wup, bup, wdown, bdown = ln2_gain[0], ln2_bias[0], w_up[0], b_up[0], w_down[0], b_down[0]
    n_img = n_dp * images.shape[0]

    first_half = lax.ppermute(images[0], "section", [(0, 1)])
    full_image = jnp.concatenate([first_half, images[0]], 0)

    def make_kv(img):
        return bf(mm(img, wkv_cross))

    kv_own = run_on(up, make_kv, full_image)
    ring_up = [(i, (i + 1) % n_dp) for i in range(n_dp)]
    ring_down = [((i + 1) % n_dp, i) for i in range(n_dp)]
    kv_prev = lax.ppermute(kv_own, "dp", ring_up)
    kv_next = lax.ppermute(kv_own, "dp", ring_down)
    pool = jnp.stack([kv_prev, kv_own, kv_next], 0)
    img_tok = pool.shape[1]

    first_img = (row_block[:, None] + seg_image) % n_img
    slot = (first_img - dp_index + 1 + n_img) % n_img
    cut_all = jnp.sum((seg_ids == 0).astype(jnp.int32), 1)

    def chunk(a, m):
        return a[m * rc : (m + 1) * rc]

    x = inputs.astype(F32)

    def lower_fwd(hid, seg):
        h2, s_self = self_fwd(hid, seg, g1, b1, wqkv, wout)
        out, s_ffn = ffn_fwd(h2, g2, b2, wup, bup, wdown, bdown)
        return out, (s_self, s_ffn)

    def upper_fwd(sent, seg, slots, cuts, pool):
        hid = sent.astype(F32)
        h2, s_self = self_fwd(hid, seg, g1, b1, wqkv, wout)
        h3, s_cross = cross_fwd(h2, slots, cuts, pool, lnc_gain, lnc_bias, wq_cross, wo_cross)
        out, s_ffn = ffn_fwd(h3, g2, b2, wup, bup, wdown, bdown)
        return out, (s_self, s_cross, s_ffn)

    low_out, low_saved, sent = [], [], []
    for m in range(MICRO):
        x_m = chunk(x, m)
        if m > 0:
            x_m, low_out[-1] = lax.optimization_barrier((x_m, low_out[-1]))
        out, saved = run_on(low, lower_fwd, x_m, chunk(seg_ids, m))
        low_out.append(out)
        low_saved.append(saved)
        sent.append(lax.ppermute(bf(out), "section", [(0, 1)]))
    up_out, up_saved = [], []
    for m in range(MICRO):
        arriving = sent[m]
        if m > 0:
            arriving, up_out[-1] = lax.optimization_barrier((arriving, up_out[-1]))
        out, saved = run_on(
            up, upper_fwd, arriving, chunk(seg_ids, m), chunk(slot, m), chunk(cut_all, m), pool
        )
        up_out.append(out)
        up_saved.append(saved)

    cot = cotangent[0].astype(F32)

    def upper_bwd(gout, saved, slots, cuts, pool):
        s_self, s_cross, s_ffn = saved
        dh3, ln2g, pf = ffn_bwd(gout, s_ffn, g2, wup, wdown)
        dh2, lncg, pc, dpool = cross_bwd(dh3, s_cross, slots, cuts, pool, lnc_gain, wq_cross, wo_cross)
        dh, ln1g, ps = self_bwd(dh2, s_self, g1, wqkv, wout)
        return dh, (ln1g, ln2g, lncg), (ps, pf, pc), dpool

    up_grad, up_small, up_pairs = [], [], []
    returned = []
    pool_grad = None
    for m in range(MICRO):
        cot_m = chunk(cot, m)
        if m > 0:
            cot_m, up_grad[-1] = lax.optimization_barrier((cot_m, up_grad[-1]))
        dh, small, pairs, dpool = run_on(
            up, upper_bwd, cot_m, up_saved[m], chunk(slot, m), chunk(cut_all, m), pool
        )
        up_grad.append(dh)
        up_small.append(small)
        up_pairs.append(pairs)
        pool_grad = dpool if pool_grad is None else pool_grad + dpool
        returned.append(lax.ppermute(bf(dh), "section", [(1, 0)]))

    def cat(name_path, pairs_list):
        return jnp.concatenate([name_path(p) for p in pairs_list], 0)

    def layer_weight_grads(pairs_list):
        ps = lambda i, k: cat(lambda p: p[i][k], pairs_list)
        d_wqkv = outer(ps(0, "n"), ps(0, "dt"))
        d_wout = outer(ps(0, "o"), ps(0, "g2"))
        d_wup = outer(ps(1, "u"), ps(1, "dz"))
        d_wdown = outer(ps(1, "f"), ps(1, "gb"))
        d_bup = jnp.sum(ps(1, "dz").astype(F32), (0, 1))
        d_bdown = jnp.sum(ps(1, "gb").astype(F32), (0, 1))
        return d_wqkv, d_wout, d_wup, d_bup, d_wdown, d_bdown

    def upper_wgrads(pairs_list):
        layer = layer_weight_grads(pairs_list)
        ps = lambda k: cat(lambda p: p[2][k], pairs_list)
        d_wq = outer(ps("c"), ps("dqc"))
        d_wo = outer(ps("oc"), ps("g3"))
        return layer, (d_wq, d_wo)

    up_w, cross_w = run_on(up, upper_wgrads, up_pairs)

    parts = bf(pool_grad)
    from_next = lax.ppermute(parts[0], "dp", ring_down)
    from_prev = lax.ppermute(parts[2], "dp", ring_up)
    kv_grad = bf(parts[1].astype(F32) + from_next.astype(F32) + from_prev.astype(F32))

    def image_side(kvg, img):
        ig = jnp.einsum("te,de->td", kvg, wkv_cross, preferred_element_type=F32)
        dw = jnp.einsum("td,te->de", img, kvg, preferred_element_type=F32)
        return ig, dw

    image_grad_full, d_wkv = run_on(up, image_side, kv_grad, full_image)
    half = images.shape[1]
    ig_first = lax.ppermute(image_grad_full[:half], "section", [(1, 0)])
    image_grad = jnp.where(up, image_grad_full[half:], ig_first)[None]

    def tree_sum(xs):
        total = xs[0]
        for v in xs[1:]:
            total = jax.tree.map(jnp.add, total, v)
        return total

    def layer_list(lw, sm):
        d_wqkv, d_wout, d_wup, d_bup, d_wdown, d_bdown = lw
        return [d_wqkv, d_wout, d_wup, d_wdown, sm[0][0], sm[0][1], sm[1][0], sm[1][1], d_bup, d_bdown]

    up_sm = tree_sum(up_small)
    a_list = layer_list(up_w, up_sm) + [cross_w[0], cross_w[1], d_wkv, up_sm[2][0], up_sm[2][1]]
    a_row = ring_reduce_scatter(pack_rows(a_list, n_dp), 1, cycle, dp_index)

    def lower_bwd(gout, saved):
        s_self, s_ffn = saved
        dh3, ln2g, pf = ffn_bwd(gout, s_ffn, g2, wup, wdown)
        dh, ln1g, ps = self_bwd(dh3, s_self, g1, wqkv, wout)
        return dh, (ln1g, ln2g), (ps, pf)

    low_grad, low_small, low_pairs = [], [], []
    for m in range(MICRO):
        gout = chunk(cot, m) + returned[m].astype(F32)
        if m == 0:
            gout, a_row = lax.optimization_barrier((gout, a_row))
        else:
            gout, low_grad[-1] = lax.optimization_barrier((gout, low_grad[-1]))
        dh, small, pairs = run_on(low, lower_bwd, gout, low_saved[m])
        low_grad.append(dh)
        low_small.append(small)
        low_pairs.append(pairs)

    low_w = run_on(low, layer_weight_grads, low_pairs)
    low_sm = tree_sum(low_small)
    b_list = layer_list(low_w, low_sm)
    b_row = ring_reduce_scatter(pack_rows(b_list, n_dp), 0, cycle, dp_index)
    a_got = unpack_row(a_row, a_list, n_dp)
    b_got = unpack_row(b_row, b_list, n_dp)

    cross_out = a_got[10:]
    cross_copy = lax.ppermute(cross_out, "section", [(1, 0)])
    cross_out = [jnp.where(up, a, c) for a, c in zip(cross_out, cross_copy)]

    activations = jnp.where(
        up, jnp.concatenate(up_out, 0), jnp.concatenate(low_out, 0)
    )[None]
    back_grads = jnp.where(
        up, jnp.concatenate(up_grad, 0), jnp.concatenate(low_grad, 0)
    )[None]
    layer = [jnp.where(up, a, b)[None] for a, b in zip(a_got[:10], b_got)]
    big, small = layer[:4], [v.reshape(1, -1) for v in layer[4:]]
    d_wq, d_wo, d_wkv_sh, lnc_g, lnc_b = cross_out

    return (
        activations,
        back_grads,
        image_grad,
        small[0],
        small[1],
        big[0],
        big[1],
        small[2],
        small[3],
        big[2],
        small[4],
        big[3],
        small[5],
        lnc_g,
        lnc_b,
        d_wq,
        d_wkv_sh,
        d_wo,
    )


def solution(mesh):
    placed = (
        P("dp", None, None),
        P("section", "dp", None, None),
        P("dp", "section", None),
        P("dp", None),
        P("dp"),
        P("dp", None),
        P("section", None),
        P("section", None),
        P("section", None, None),
        P("section", None, None),
        P("section", None),
        P("section", None),
        P("section", None, None),
        P("section", None),
        P("section", None, None),
        P("section", None),
        P(),
        P(),
        P(),
        P(),
        P(),
    )
    return jax.shard_map(
        partial(per_device, chip_cycle(mesh)),
        mesh=mesh,
        in_specs=placed,
        out_specs=(
            P("section", "dp", None, None),
            P("section", "dp", None, None),
            P("dp", "section", None),
            P("section", "dp"),
            P("section", "dp"),
            P("section", "dp", None),
            P("section", "dp", None),
            P("section", "dp"),
            P("section", "dp"),
            P("section", "dp", None),
            P("section", "dp"),
            P("section", "dp", None),
            P("section", "dp"),
            P("dp"),
            P("dp"),
            P("dp", None),
            P("dp", None),
            P("dp", None),
        ),
        check_vma=False,
    )
```

```python
from functools import partial

import jax
import jax.numpy as jnp
from jax import lax
from jax.experimental import pallas as pl
from jax.experimental.pallas import tpu as pltpu
from jax.sharding import PartitionSpec as P

H = 12
HD = 64
MICRO = 2

EPS = 1e-05
MASKED = -1e30
SCALE = HD ** (-0.5)
F32 = jnp.float32
BF16 = jnp.bfloat16


def bf(x):
    return x.astype(BF16)


def run_on(flag, fn, *args):
    shapes = jax.eval_shape(fn, *args)

    def idle(*unused):
        return jax.tree.map(lambda s: jnp.zeros(s.shape, s.dtype), shapes)

    return lax.cond(flag, fn, idle, *args)


def norm_fwd(x, gain, bias):
    mean = jnp.mean(x, -1, keepdims=True)
    centred = x - mean
    var = jnp.mean(centred * centred, -1, keepdims=True)
    rstd = lax.rsqrt(var + EPS)
    xhat = centred * rstd
    return xhat * gain + bias, (xhat, rstd)


def norm_bwd(dy, saved, gain):
    xhat, rstd = saved
    lead = tuple(range(dy.ndim - 1))
    d_gain = jnp.sum(dy * xhat, lead)
    d_bias = jnp.sum(dy, lead)
    dxh = dy * gain
    dx = rstd * (
        dxh
        - jnp.mean(dxh, -1, keepdims=True)
        - xhat * jnp.mean(dxh * xhat, -1, keepdims=True)
    )
    return dx, d_gain, d_bias


def mm(a, w):
    return jnp.einsum("...d,de->...e", a, w, preferred_element_type=F32)


def mm_t(g, w):
    return jnp.einsum("...e,de->...d", g, w, preferred_element_type=F32)


def outer(a, b):
    return jnp.einsum("rtd,rte->de", a, b, preferred_element_type=F32)


def softmax_rows(s, axes):
    top = jnp.max(s, axes, keepdims=True)
    e = jnp.exp(s - top)
    return e / jnp.sum(e, axes, keepdims=True)


def self_fwd(h, seg, gain, bias, w_qkv, w_out):
    r, t = seg.shape
    y, nsave = norm_fwd(h, gain, bias)
    n = bf(y)
    trip = bf(mm(n, w_qkv)).reshape(r, t, 3, H, HD)
    q, k, v = trip[:, :, 0], trip[:, :, 1], trip[:, :, 2]
    pos = jnp.arange(t)
    allowed = (seg[:, :, None] == seg[:, None, :]) & (pos[:, None] >= pos[None, :])[None]
    s = jnp.einsum("rqhd,rkhd->rhqk", q, k, preferred_element_type=F32) * SCALE
    s = jnp.where(allowed[:, None], s, MASKED)
    p = softmax_rows(s, -1)
    o = bf(jnp.einsum("rhqk,rkhd->rqhd", bf(p), v, preferred_element_type=F32))
    o = o.reshape(r, t, H * HD)
    h2 = h + mm(o, w_out)
    saved = dict(nsave=nsave, n=n, q=q, k=k, v=v, p=p, o=o)
    return h2, saved


def self_bwd(dh2, sv, gain, w_qkv, w_out):
    r, t = dh2.shape[:2]
    g2 = bf(dh2)
    do = bf(mm_t(g2, w_out)).reshape(r, t, H, HD)
    p, q, k, v = sv["p"], sv["q"], sv["k"], sv["v"]
    dp = jnp.einsum("rqhd,rkhd->rhqk", do, v, preferred_element_type=F32)
    ds = bf(p * (dp - jnp.sum(p * dp, -1, keepdims=True)))
    dq = jnp.einsum("rhqk,rkhd->rqhd", ds, k, preferred_element_type=F32) * SCALE
    dk = jnp.einsum("rhqk,rqhd->rkhd", ds, q, preferred_element_type=F32) * SCALE
    dv = jnp.einsum("rhqk,rqhd->rkhd", bf(p), do, preferred_element_type=F32)
    dt = bf(jnp.stack([dq, dk, dv], 2)).reshape(r, t, 3 * H * HD)
    dn = mm_t(dt, w_qkv)
    dx, d_gain, d_bias = norm_bwd(dn, sv["nsave"], gain)
    pairs = dict(o=sv["o"], g2=g2, n=sv["n"], dt=dt)
    return dh2 + dx, (d_gain, d_bias), pairs


RB = 2


def _dot_nt(a, b):
    return lax.dot_general(a, b, (((1,), (1,)), ((), ())), preferred_element_type=F32)


def _dot_tn(a, b):
    return lax.dot_general(a, b, (((0,), (0,)), ((), ())), preferred_element_type=F32)


def _dot(a, b):
    return lax.dot_general(a, b, (((1,), (0,)), ((), ())), preferred_element_type=F32)


def _probs(q, ka, kb, first):
    sa = _dot_nt(q, ka) * SCALE
    sb = _dot_nt(q, kb) * SCALE
    s = jnp.where(first, sa, sb)
    top = jnp.max(s, -1, keepdims=True)
    e = jnp.exp(s - top)
    return e / jnp.sum(e, -1, keepdims=True)


def _fwd_kernel(slot_ref, cut_ref, q_ref, pool_ref, o_ref):
    i = pl.program_id(0)
    t = q_ref.shape[1]
    d = H * HD
    for j in range(RB):
        r = i * RB + j
        a = slot_ref[2 * r]
        b = slot_ref[2 * r + 1]
        first = lax.broadcasted_iota(jnp.int32, (t, 1), 0) < cut_ref[r]
        for h in range(H):
            cols = pl.ds(h * HD, HD)
            vcols = pl.ds(d + h * HD, HD)
            q = q_ref[j, :, cols]
            p = _probs(q, pool_ref[a, :, cols], pool_ref[b, :, cols], first).astype(BF16)
            zero = jnp.zeros_like(p)
            o = _dot(jnp.where(first, p, zero), pool_ref[a, :, vcols]) + _dot(
                jnp.where(first, zero, p), pool_ref[b, :, vcols]
            )
            o_ref[j, :, cols] = o.astype(o_ref.dtype)


def _bwd_kernel(slot_ref, cut_ref, q_ref, do_ref, pool_ref, dq_ref, dpool_ref):
    i = pl.program_id(0)
    t = q_ref.shape[1]
    d = H * HD

    @pl.when(i == 0)
    def _():
        dpool_ref[...] = jnp.zeros_like(dpool_ref)

    for j in range(RB):
        r = i * RB + j
        a = slot_ref[2 * r]
        b = slot_ref[2 * r + 1]
        first = lax.broadcasted_iota(jnp.int32, (t, 1), 0) < cut_ref[r]
        for h in range(H):
            cols = pl.ds(h * HD, HD)
            vcols = pl.ds(d + h * HD, HD)
            q = q_ref[j, :, cols]
            do = do_ref[j, :, cols]
            ka = pool_ref[a, :, cols]
            kb = pool_ref[b, :, cols]
            va = pool_ref[a, :, vcols]
            vb = pool_ref[b, :, vcols]
            p = _probs(q, ka, kb, first)
            dp = jnp.where(first, _dot_nt(do, va), _dot_nt(do, vb))
            ds = (p * (dp - jnp.sum(p * dp, -1, keepdims=True))).astype(BF16)
            zero = jnp.zeros_like(ds)
            dsa = jnp.where(first, ds, zero)
            dsb = jnp.where(first, zero, ds)
            dq = (_dot(dsa, ka) + _dot(dsb, kb)) * SCALE
            dq_ref[j, :, cols] = dq.astype(dq_ref.dtype)
            pb = p.astype(BF16)
            pa_ = jnp.where(first, pb, zero)
            pb_ = jnp.where(first, zero, pb)
            dpool_ref[a, :, cols] += _dot_tn(dsa, q) * SCALE
            dpool_ref[a, :, vcols] += _dot_tn(pa_, do)
            dpool_ref[b, :, cols] += _dot_tn(dsb, q) * SCALE
            dpool_ref[b, :, vcols] += _dot_tn(pb_, do)


def cross_attention_fwd(qc, pool, slots, cuts):
    r, t, d = qc.shape
    spec = pltpu.PrefetchScalarGridSpec(
        num_scalar_prefetch=2,
        grid=(r // RB,),
        in_specs=[
            pl.BlockSpec((RB, t, d), lambda i, s, c: (i, 0, 0)),
            pl.BlockSpec(pool.shape, lambda i, s, c: (0, 0, 0)),
        ],
        out_specs=pl.BlockSpec((RB, t, d), lambda i, s, c: (i, 0, 0)),
    )
    flops = r * H * 4 * 2 * t * pool.shape[1] * HD
    return pl.pallas_call(
        _fwd_kernel,
        grid_spec=spec,
        out_shape=jax.ShapeDtypeStruct((r, t, d), BF16),
        compiler_params=pltpu.CompilerParams(
            dimension_semantics=("arbitrary",), vmem_limit_bytes=48 * 1024 * 1024
        ),
        cost_estimate=pl.CostEstimate(
            flops=flops,
            transcendentals=r * H * t * 2 * pool.shape[1],
            bytes_accessed=2 * qc.size * 2 + pool.size * 2,
        ),
    )(slots.reshape(-1), cuts, qc, pool)


def cross_attention_bwd(qc, doc, pool, slots, cuts):
    r, t, d = qc.shape
    spec = pltpu.PrefetchScalarGridSpec(
        num_scalar_prefetch=2,
        grid=(r // RB,),
        in_specs=[
            pl.BlockSpec((RB, t, d), lambda i, s, c: (i, 0, 0)),
            pl.BlockSpec((RB, t, d), lambda i, s, c: (i, 0, 0)),
            pl.BlockSpec(pool.shape, lambda i, s, c: (0, 0, 0)),
        ],
        out_specs=[
            pl.BlockSpec((RB, t, d), lambda i, s, c: (i, 0, 0)),
            pl.BlockSpec(pool.shape, lambda i, s, c: (0, 0, 0)),
        ],
    )
    flops = r * H * 10 * 2 * t * pool.shape[1] * HD
    return pl.pallas_call(
        _bwd_kernel,
        grid_spec=spec,
        out_shape=(
            jax.ShapeDtypeStruct((r, t, d), BF16),
            jax.ShapeDtypeStruct(pool.shape, F32),
        ),
        compiler_params=pltpu.CompilerParams(
            dimension_semantics=("arbitrary",), vmem_limit_bytes=60 * 1024 * 1024
        ),
        cost_estimate=pl.CostEstimate(
            flops=flops,
            transcendentals=r * H * t * 2 * pool.shape[1],
            bytes_accessed=3 * qc.size * 2 + pool.size * 2 + pool.size * 4,
        ),
    )(slots.reshape(-1), cuts, qc, doc, pool)


def cross_fwd(h2, slots, cuts, pool, gain, bias, wq, wo):
    y, csave = norm_fwd(h2, gain, bias)
    c = bf(y)
    qc = bf(mm(c, wq))
    oc = cross_attention_fwd(qc, pool, slots, cuts)
    h3 = h2 + mm(oc, wo)
    return h3, dict(csave=csave, c=c, qc=qc, oc=oc)


def cross_bwd(dh3, sv, slots, cuts, pool, gain, wq, wo):
    g3 = bf(dh3)
    doc = bf(mm_t(g3, wo))
    dqc, dpool = cross_attention_bwd(sv["qc"], doc, pool, slots, cuts)
    dc = mm_t(dqc, wq)
    dx, d_gain, d_bias = norm_bwd(dc, sv["csave"], gain)
    pairs = dict(oc=sv["oc"], g3=g3, c=sv["c"], dqc=dqc)
    return dh3 + dx, (d_gain, d_bias), pairs, dpool


def gelu(z):
    return jax.nn.gelu(z, approximate=False)


def ffn_fwd(h3, gain, bias, w_up, b_up, w_down, b_down):
    y, usave = norm_fwd(h3, gain, bias)
    u = bf(y)
    z = mm(u, w_up) + b_up
    f = bf(gelu(z))
    out = h3 + (mm(f, w_down) + b_down)
    return out, dict(usave=usave, u=u, z=z, f=f)


def ffn_bwd(gout, sv, gain, w_up, w_down):
    gb = bf(gout)
    df = mm_t(gb, w_down)
    _, pull = jax.vjp(gelu, sv["z"])
    dz = bf(pull(df)[0])
    du = mm_t(dz, w_up)
    dx, d_gain, d_bias = norm_bwd(du, sv["usave"], gain)
    pairs = dict(f=sv["f"], gb=gb, u=sv["u"], dz=dz)
    return gout + dx, (d_gain, d_bias), pairs


def chip_cycle(mesh):
    n_dp = mesh.shape["dp"]
    plane = mesh.devices.reshape(-1, n_dp)[0]
    try:
        chips = {}
        for i, dev in enumerate(plane):
            chips.setdefault(tuple(dev.coords), []).append(i)
    except AttributeError:
        return list(range(n_dp))
    keys = sorted(chips)
    if len(keys) < 3:
        return [i for k in keys for i in sorted(chips[k])]
    near = {
        k: [j for j in keys if sum(abs(a - b) for a, b in zip(k, j)) == 1] for k in keys
    }
    path, seen, budget = [keys[0]], {keys[0]}, [200000]

    def walk():
        budget[0] -= 1
        if budget[0] < 0:
            return False
        if len(path) == len(keys):
            return keys[0] in near[path[-1]]
        options = sorted(
            (j for j in near[path[-1]] if j not in seen),
            key=lambda j: sum(1 for n in near[j] if n not in seen),
        )
        for j in options:
            path.append(j)
            seen.add(j)
            if walk():
                return True
            path.pop()
            seen.discard(j)
        return False

    if not walk():
        return list(range(n_dp))
    return [i for k in path for i in sorted(chips[k])]


def ring_reduce_scatter(blocks, plane, cycle, dp_index):
    n = len(cycle)
    n_dp = blocks[0].shape[0]
    axes = ("section", "dp")
    fwd = [(plane * n_dp + cycle[i], plane * n_dp + cycle[(i + 1) % n]) for i in range(n)]
    bwd = [(b, a) for a, b in fwd]
    where_in = [0] * n
    for i, d in enumerate(cycle):
        where_in[d] = i
    order = jnp.array(cycle * 2, jnp.int32)
    cw = [bf(x[..., : x.shape[-1] // 2]) for x in blocks]
    ccw = [bf(x[..., x.shape[-1] // 2 :]) for x in blocks]
    p = jnp.array(where_in, jnp.int32)[dp_index]

    def take(arrays, idx):
        at = order[idx % n]
        return [lax.dynamic_index_in_dim(x, at, 0, keepdims=False) for x in arrays]

    send_c, send_w = take(cw, p + n - 1), take(ccw, p + 1)
    for step in range(n - 1):
        got_c = lax.ppermute(send_c, axes, fwd)
        got_w = lax.ppermute(send_w, axes, bwd)
        own_c = take(cw, p + 2 * n - step - 2)
        own_w = take(ccw, p + step + 2)
        acc_c = [g.astype(F32) + o.astype(F32) for g, o in zip(got_c, own_c)]
        acc_w = [g.astype(F32) + o.astype(F32) for g, o in zip(got_w, own_w)]
        send_c, send_w = [bf(x) for x in acc_c], [bf(x) for x in acc_w]
    return [jnp.concatenate([c, w], -1) for c, w in zip(acc_c, acc_w)]


def as_blocks(arrays, n):
    big = [a.reshape((n, a.shape[0] // n) + a.shape[1:]) for a in arrays if a.ndim == 2]
    small = [a.reshape(n, -1) for a in arrays if a.ndim == 1]
    return big + [jnp.concatenate(small, 1)]


def from_blocks(got, arrays, n):
    big = iter(got[:-1])
    small, at, out = got[-1], 0, []
    for a in arrays:
        if a.ndim == 2:
            out.append(next(big))
        else:
            width = a.size // n
            out.append(small[at : at + width])
            at += width
    return out


def per_device(
    cycle,
    inputs,
    cotangent,
    images,
    seg_ids,
    row_block,
    seg_image,
    ln1_gain,
    ln1_bias,
    w_qkv,
    w_out,
    ln2_gain,
    ln2_bias,
    w_up,
    b_up,
    w_down,
    b_down,
    lnc_gain,
    lnc_bias,
    wq_cross,
    wkv_cross,
    wo_cross,
):
    up = lax.axis_index("section") == 1
    low = jnp.logical_not(up)
    dp_index = lax.axis_index("dp")
    n_dp = lax.axis_size("dp")
    rows = inputs.shape[0]
    rc = rows // MICRO
    g1, b1, wqkv, wout = ln1_gain[0], ln1_bias[0], w_qkv[0], w_out[0]
    g2, b2, wup, bup, wdown, bdown = ln2_gain[0], ln2_bias[0], w_up[0], b_up[0], w_down[0], b_down[0]
    n_img = n_dp * images.shape[0]

    first_half = lax.ppermute(images[0], "section", [(0, 1)])
    full_image = jnp.concatenate([first_half, images[0]], 0)

    def make_kv(img):
        return bf(mm(img, wkv_cross))

    kv_own = run_on(up, make_kv, full_image)
    ring_up = [(i, (i + 1) % n_dp) for i in range(n_dp)]
    ring_down = [((i + 1) % n_dp, i) for i in range(n_dp)]
    kv_prev = lax.ppermute(kv_own, "dp", ring_up)
    kv_next = lax.ppermute(kv_own, "dp", ring_down)
    pool = jnp.stack([kv_prev, kv_own, kv_next], 0)
    img_tok = pool.shape[1]

    first_img = (row_block[:, None] + seg_image) % n_img
    slot = (first_img - dp_index + 1 + n_img) % n_img
    cut_all = jnp.sum((seg_ids == 0).astype(jnp.int32), 1)

    def chunk(a, m):
        return a[m * rc : (m + 1) * rc]

    x = inputs.astype(F32)

    def lower_fwd(hid, seg):
        h2, s_self = self_fwd(hid, seg, g1, b1, wqkv, wout)
        out, s_ffn = ffn_fwd(h2, g2, b2, wup, bup, wdown, bdown)
        return out, (s_self, s_ffn)

    def upper_fwd(sent, seg, slots, cuts, pool):
        hid = sent.astype(F32)
        h2, s_self = self_fwd(hid, seg, g1, b1, wqkv, wout)
        h3, s_cross = cross_fwd(h2, slots, cuts, pool, lnc_gain, lnc_bias, wq_cross, wo_cross)
        out, s_ffn = ffn_fwd(h3, g2, b2, wup, bup, wdown, bdown)
        return out, (s_self, s_cross, s_ffn)

    low_out, low_saved, sent = [], [], []
    for m in range(MICRO):
        x_m = chunk(x, m)
        if m > 0:
            x_m, low_out[-1] = lax.optimization_barrier((x_m, low_out[-1]))
        out, saved = run_on(low, lower_fwd, x_m, chunk(seg_ids, m))
        low_out.append(out)
        low_saved.append(saved)
        sent.append(lax.ppermute(bf(out), "section", [(0, 1)]))
    up_out, up_saved = [], []
    for m in range(MICRO):
        arriving = sent[m]
        if m > 0:
            arriving, up_out[-1] = lax.optimization_barrier((arriving, up_out[-1]))
        out, saved = run_on(
            up, upper_fwd, arriving, chunk(seg_ids, m), chunk(slot, m), chunk(cut_all, m), pool
        )
        up_out.append(out)
        up_saved.append(saved)

    cot = cotangent[0].astype(F32)

    def upper_bwd(gout, saved, slots, cuts, pool):
        s_self, s_cross, s_ffn = saved
        dh3, ln2g, pf = ffn_bwd(gout, s_ffn, g2, wup, wdown)
        dh2, lncg, pc, dpool = cross_bwd(dh3, s_cross, slots, cuts, pool, lnc_gain, wq_cross, wo_cross)
        dh, ln1g, ps = self_bwd(dh2, s_self, g1, wqkv, wout)
        return dh, (ln1g, ln2g, lncg), (ps, pf, pc), dpool

    up_grad, up_small, up_pairs = [], [], []
    returned = []
    pool_grad = None
    for m in range(MICRO):
        cot_m = chunk(cot, m)
        if m > 0:
            cot_m, up_grad[-1] = lax.optimization_barrier((cot_m, up_grad[-1]))
        dh, small, pairs, dpool = run_on(
            up, upper_bwd, cot_m, up_saved[m], chunk(slot, m), chunk(cut_all, m), pool
        )
        up_grad.append(dh)
        up_small.append(small)
        up_pairs.append(pairs)
        pool_grad = dpool if pool_grad is None else pool_grad + dpool
        returned.append(lax.ppermute(bf(dh), "section", [(1, 0)]))

    def cat(name_path, pairs_list):
        return jnp.concatenate([name_path(p) for p in pairs_list], 0)

    def layer_weight_grads(pairs_list):
        ps = lambda i, k: cat(lambda p: p[i][k], pairs_list)
        d_wqkv = outer(ps(0, "n"), ps(0, "dt"))
        d_wout = outer(ps(0, "o"), ps(0, "g2"))
        d_wup = outer(ps(1, "u"), ps(1, "dz"))
        d_wdown = outer(ps(1, "f"), ps(1, "gb"))
        d_bup = jnp.sum(ps(1, "dz").astype(F32), (0, 1))
        d_bdown = jnp.sum(ps(1, "gb").astype(F32), (0, 1))
        return d_wqkv, d_wout, d_wup, d_bup, d_wdown, d_bdown

    def upper_wgrads(pairs_list):
        layer = layer_weight_grads(pairs_list)
        ps = lambda k: cat(lambda p: p[2][k], pairs_list)
        d_wq = outer(ps("c"), ps("dqc"))
        d_wo = outer(ps("oc"), ps("g3"))
        return layer, (d_wq, d_wo)

    up_w, cross_w = run_on(up, upper_wgrads, up_pairs)

    parts = bf(pool_grad)
    from_next = lax.ppermute(parts[0], "dp", ring_down)
    from_prev = lax.ppermute(parts[2], "dp", ring_up)
    kv_grad = bf(parts[1].astype(F32) + from_next.astype(F32) + from_prev.astype(F32))

    def image_side(kvg, img):
        ig = jnp.einsum("te,de->td", kvg, wkv_cross, preferred_element_type=F32)
        dw = jnp.einsum("td,te->de", img, kvg, preferred_element_type=F32)
        return ig, dw

    image_grad_full, d_wkv = run_on(up, image_side, kv_grad, full_image)
    half = images.shape[1]
    ig_first = lax.ppermute(image_grad_full[:half], "section", [(1, 0)])
    image_grad = jnp.where(up, image_grad_full[half:], ig_first)[None]

    def tree_sum(xs):
        total = xs[0]
        for v in xs[1:]:
            total = jax.tree.map(jnp.add, total, v)
        return total

    def layer_list(lw, sm):
        d_wqkv, d_wout, d_wup, d_bup, d_wdown, d_bdown = lw
        return [d_wqkv, d_wout, d_wup, d_wdown, sm[0][0], sm[0][1], sm[1][0], sm[1][1], d_bup, d_bdown]

    up_sm = tree_sum(up_small)
    a_list = layer_list(up_w, up_sm) + [cross_w[0], cross_w[1], d_wkv, up_sm[2][0], up_sm[2][1]]
    a_blocks = as_blocks(a_list, n_dp)

    def lower_bwd(gout, saved):
        s_self, s_ffn = saved
        dh3, ln2g, pf = ffn_bwd(gout, s_ffn, g2, wup, wdown)
        dh, ln1g, ps = self_bwd(dh3, s_self, g1, wqkv, wout)
        return dh, (ln1g, ln2g), (ps, pf)

    low_grad, low_small, low_pairs = [], [], []
    for m in range(MICRO):
        gout = chunk(cot, m) + returned[m].astype(F32)
        if m == 0:
            pass
        else:
            gout, low_grad[-1] = lax.optimization_barrier((gout, low_grad[-1]))
        dh, small, pairs = run_on(low, lower_bwd, gout, low_saved[m])
        low_grad.append(dh)
        low_small.append(small)
        low_pairs.append(pairs)

    low_w = run_on(low, layer_weight_grads, low_pairs)
    low_sm = tree_sum(low_small)
    b_list = layer_list(low_w, low_sm)
    b_blocks = as_blocks(b_list, n_dp)
    a_blocks, b_blocks = lax.optimization_barrier((a_blocks, b_blocks))
    a_got = from_blocks(ring_reduce_scatter(a_blocks, 1, cycle, dp_index), a_list, n_dp)
    b_got = from_blocks(ring_reduce_scatter(b_blocks, 0, cycle, dp_index), b_list, n_dp)

    cross_out = a_got[10:]
    cross_copy = lax.ppermute(cross_out, "section", [(1, 0)])
    cross_out = [jnp.where(up, a, c) for a, c in zip(cross_out, cross_copy)]

    activations = jnp.where(
        up, jnp.concatenate(up_out, 0), jnp.concatenate(low_out, 0)
    )[None]
    back_grads = jnp.where(
        up, jnp.concatenate(up_grad, 0), jnp.concatenate(low_grad, 0)
    )[None]
    layer = [jnp.where(up, a, b)[None] for a, b in zip(a_got[:10], b_got)]
    big, small = layer[:4], [v.reshape(1, -1) for v in layer[4:]]
    d_wq, d_wo, d_wkv_sh, lnc_g, lnc_b = cross_out

    return (
        activations,
        back_grads,
        image_grad,
        small[0],
        small[1],
        big[0],
        big[1],
        small[2],
        small[3],
        big[2],
        small[4],
        big[3],
        small[5],
        lnc_g,
        lnc_b,
        d_wq,
        d_wkv_sh,
        d_wo,
    )


def solution(mesh):
    placed = (
        P("dp", None, None),
        P("section", "dp", None, None),
        P("dp", "section", None),
        P("dp", None),
        P("dp"),
        P("dp", None),
        P("section", None),
        P("section", None),
        P("section", None, None),
        P("section", None, None),
        P("section", None),
        P("section", None),
        P("section", None, None),
        P("section", None),
        P("section", None, None),
        P("section", None),
        P(),
        P(),
        P(),
        P(),
        P(),
    )
    return jax.shard_map(
        partial(per_device, chip_cycle(mesh)),
        mesh=mesh,
        in_specs=placed,
        out_specs=(
            P("section", "dp", None, None),
            P("section", "dp", None, None),
            P("dp", "section", None),
            P("section", "dp"),
            P("section", "dp"),
            P("section", "dp", None),
            P("section", "dp", None),
            P("section", "dp"),
            P("section", "dp"),
            P("section", "dp", None),
            P("section", "dp"),
            P("section", "dp", None),
            P("section", "dp"),
            P("dp"),
            P("dp"),
            P("dp", None),
            P("dp", None),
            P("dp", None),
        ),
        check_vma=False,
    )
```

```python
from functools import partial

import jax
import jax.numpy as jnp
from jax import lax
from jax.experimental import pallas as pl
from jax.experimental.pallas import tpu as pltpu
from jax.sharding import PartitionSpec as P

H = 12
HD = 64
MICRO = 2

EPS = 1e-05
MASKED = -1e30
SCALE = HD ** (-0.5)
F32 = jnp.float32
BF16 = jnp.bfloat16


def bf(x):
    return x.astype(BF16)


def run_on(flag, fn, *args):
    shapes = jax.eval_shape(fn, *args)

    def idle(*unused):
        return jax.tree.map(lambda s: jnp.zeros(s.shape, s.dtype), shapes)

    return lax.cond(flag, fn, idle, *args)


def norm_fwd(x, gain, bias):
    mean = jnp.mean(x, -1, keepdims=True)
    centred = x - mean
    var = jnp.mean(centred * centred, -1, keepdims=True)
    rstd = lax.rsqrt(var + EPS)
    xhat = centred * rstd
    return xhat * gain + bias, (xhat, rstd)


def norm_bwd(dy, saved, gain):
    xhat, rstd = saved
    lead = tuple(range(dy.ndim - 1))
    d_gain = jnp.sum(dy * xhat, lead)
    d_bias = jnp.sum(dy, lead)
    dxh = dy * gain
    dx = rstd * (
        dxh
        - jnp.mean(dxh, -1, keepdims=True)
        - xhat * jnp.mean(dxh * xhat, -1, keepdims=True)
    )
    return dx, d_gain, d_bias


def mm(a, w):
    return jnp.einsum("...d,de->...e", a, w, preferred_element_type=F32)


def mm_t(g, w):
    return jnp.einsum("...e,de->...d", g, w, preferred_element_type=F32)


def outer(a, b):
    return jnp.einsum("rtd,rte->de", a, b, preferred_element_type=F32)


def softmax_rows(s, axes):
    top = jnp.max(s, axes, keepdims=True)
    e = jnp.exp(s - top)
    return e / jnp.sum(e, axes, keepdims=True)


def self_fwd(h, seg, gain, bias, w_qkv, w_out):
    r, t = seg.shape
    y, nsave = norm_fwd(h, gain, bias)
    n = bf(y)
    trip = bf(mm(n, w_qkv)).reshape(r, t, 3, H, HD)
    q, k, v = trip[:, :, 0], trip[:, :, 1], trip[:, :, 2]
    pos = jnp.arange(t)
    allowed = (seg[:, :, None] == seg[:, None, :]) & (pos[:, None] >= pos[None, :])[None]
    s = jnp.einsum("rqhd,rkhd->rhqk", q, k, preferred_element_type=F32) * SCALE
    s = jnp.where(allowed[:, None], s, MASKED)
    p = softmax_rows(s, -1)
    o = bf(jnp.einsum("rhqk,rkhd->rqhd", bf(p), v, preferred_element_type=F32))
    o = o.reshape(r, t, H * HD)
    h2 = h + mm(o, w_out)
    saved = dict(nsave=nsave, n=n, q=q, k=k, v=v, p=p, o=o)
    return h2, saved


def self_bwd(dh2, sv, gain, w_qkv, w_out):
    r, t = dh2.shape[:2]
    g2 = bf(dh2)
    do = bf(mm_t(g2, w_out)).reshape(r, t, H, HD)
    p, q, k, v = sv["p"], sv["q"], sv["k"], sv["v"]
    dp = jnp.einsum("rqhd,rkhd->rhqk", do, v, preferred_element_type=F32)
    ds = bf(p * (dp - jnp.sum(p * dp, -1, keepdims=True)))
    dq = jnp.einsum("rhqk,rkhd->rqhd", ds, k, preferred_element_type=F32) * SCALE
    dk = jnp.einsum("rhqk,rqhd->rkhd", ds, q, preferred_element_type=F32) * SCALE
    dv = jnp.einsum("rhqk,rqhd->rkhd", bf(p), do, preferred_element_type=F32)
    dt = bf(jnp.stack([dq, dk, dv], 2)).reshape(r, t, 3 * H * HD)
    dn = mm_t(dt, w_qkv)
    dx, d_gain, d_bias = norm_bwd(dn, sv["nsave"], gain)
    pairs = dict(o=sv["o"], g2=g2, n=sv["n"], dt=dt)
    return dh2 + dx, (d_gain, d_bias), pairs


RB = 2


def _dot_nt(a, b):
    return lax.dot_general(a, b, (((1,), (1,)), ((), ())), preferred_element_type=F32)


def _dot_tn(a, b):
    return lax.dot_general(a, b, (((0,), (0,)), ((), ())), preferred_element_type=F32)


def _dot(a, b):
    return lax.dot_general(a, b, (((1,), (0,)), ((), ())), preferred_element_type=F32)


def _probs(q, ka, kb, first):
    sa = _dot_nt(q, ka) * SCALE
    sb = _dot_nt(q, kb) * SCALE
    s = jnp.where(first, sa, sb)
    top = jnp.max(s, -1, keepdims=True)
    e = jnp.exp(s - top)
    return e / jnp.sum(e, -1, keepdims=True)


def _fwd_kernel(slot_ref, cut_ref, q_ref, pool_ref, o_ref):
    i = pl.program_id(0)
    t = q_ref.shape[1]
    d = H * HD
    for j in range(RB):
        r = i * RB + j
        a = slot_ref[2 * r]
        b = slot_ref[2 * r + 1]
        first = lax.broadcasted_iota(jnp.int32, (t, 1), 0) < cut_ref[r]
        for h in range(H):
            cols = pl.ds(h * HD, HD)
            vcols = pl.ds(d + h * HD, HD)
            q = q_ref[j, :, cols]
            p = _probs(q, pool_ref[a, :, cols], pool_ref[b, :, cols], first).astype(BF16)
            zero = jnp.zeros_like(p)
            o = _dot(jnp.where(first, p, zero), pool_ref[a, :, vcols]) + _dot(
                jnp.where(first, zero, p), pool_ref[b, :, vcols]
            )
            o_ref[j, :, cols] = o.astype(o_ref.dtype)


def _bwd_kernel(slot_ref, cut_ref, q_ref, do_ref, pool_ref, dq_ref, dpool_ref):
    i = pl.program_id(0)
    t = q_ref.shape[1]
    d = H * HD

    @pl.when(i == 0)
    def _():
        dpool_ref[...] = jnp.zeros_like(dpool_ref)

    for j in range(RB):
        r = i * RB + j
        a = slot_ref[2 * r]
        b = slot_ref[2 * r + 1]
        first = lax.broadcasted_iota(jnp.int32, (t, 1), 0) < cut_ref[r]
        for h in range(H):
            cols = pl.ds(h * HD, HD)
            vcols = pl.ds(d + h * HD, HD)
            q = q_ref[j, :, cols]
            do = do_ref[j, :, cols]
            ka = pool_ref[a, :, cols]
            kb = pool_ref[b, :, cols]
            va = pool_ref[a, :, vcols]
            vb = pool_ref[b, :, vcols]
            p = _probs(q, ka, kb, first)
            dp = jnp.where(first, _dot_nt(do, va), _dot_nt(do, vb))
            ds = (p * (dp - jnp.sum(p * dp, -1, keepdims=True))).astype(BF16)
            zero = jnp.zeros_like(ds)
            dsa = jnp.where(first, ds, zero)
            dsb = jnp.where(first, zero, ds)
            dq = (_dot(dsa, ka) + _dot(dsb, kb)) * SCALE
            dq_ref[j, :, cols] = dq.astype(dq_ref.dtype)
            pb = p.astype(BF16)
            pa_ = jnp.where(first, pb, zero)
            pb_ = jnp.where(first, zero, pb)
            dpool_ref[a, :, cols] += _dot_tn(dsa, q) * SCALE
            dpool_ref[a, :, vcols] += _dot_tn(pa_, do)
            dpool_ref[b, :, cols] += _dot_tn(dsb, q) * SCALE
            dpool_ref[b, :, vcols] += _dot_tn(pb_, do)


def cross_attention_fwd(qc, pool, slots, cuts):
    r, t, d = qc.shape
    spec = pltpu.PrefetchScalarGridSpec(
        num_scalar_prefetch=2,
        grid=(r // RB,),
        in_specs=[
            pl.BlockSpec((RB, t, d), lambda i, s, c: (i, 0, 0)),
            pl.BlockSpec(pool.shape, lambda i, s, c: (0, 0, 0)),
        ],
        out_specs=pl.BlockSpec((RB, t, d), lambda i, s, c: (i, 0, 0)),
    )
    flops = r * H * 4 * 2 * t * pool.shape[1] * HD
    return pl.pallas_call(
        _fwd_kernel,
        grid_spec=spec,
        out_shape=jax.ShapeDtypeStruct((r, t, d), BF16),
        compiler_params=pltpu.CompilerParams(
            dimension_semantics=("arbitrary",), vmem_limit_bytes=48 * 1024 * 1024
        ),
        cost_estimate=pl.CostEstimate(
            flops=flops,
            transcendentals=r * H * t * 2 * pool.shape[1],
            bytes_accessed=2 * qc.size * 2 + pool.size * 2,
        ),
    )(slots.reshape(-1), cuts, qc, pool)


def cross_attention_bwd(qc, doc, pool, slots, cuts):
    r, t, d = qc.shape
    spec = pltpu.PrefetchScalarGridSpec(
        num_scalar_prefetch=2,
        grid=(r // RB,),
        in_specs=[
            pl.BlockSpec((RB, t, d), lambda i, s, c: (i, 0, 0)),
            pl.BlockSpec((RB, t, d), lambda i, s, c: (i, 0, 0)),
            pl.BlockSpec(pool.shape, lambda i, s, c: (0, 0, 0)),
        ],
        out_specs=[
            pl.BlockSpec((RB, t, d), lambda i, s, c: (i, 0, 0)),
            pl.BlockSpec(pool.shape, lambda i, s, c: (0, 0, 0)),
        ],
    )
    flops = r * H * 10 * 2 * t * pool.shape[1] * HD
    return pl.pallas_call(
        _bwd_kernel,
        grid_spec=spec,
        out_shape=(
            jax.ShapeDtypeStruct((r, t, d), BF16),
            jax.ShapeDtypeStruct(pool.shape, F32),
        ),
        compiler_params=pltpu.CompilerParams(
            dimension_semantics=("arbitrary",), vmem_limit_bytes=60 * 1024 * 1024
        ),
        cost_estimate=pl.CostEstimate(
            flops=flops,
            transcendentals=r * H * t * 2 * pool.shape[1],
            bytes_accessed=3 * qc.size * 2 + pool.size * 2 + pool.size * 4,
        ),
    )(slots.reshape(-1), cuts, qc, doc, pool)


def cross_fwd(h2, slots, cuts, pool, gain, bias, wq, wo):
    y, csave = norm_fwd(h2, gain, bias)
    c = bf(y)
    qc = bf(mm(c, wq))
    oc = cross_attention_fwd(qc, pool, slots, cuts)
    h3 = h2 + mm(oc, wo)
    return h3, dict(csave=csave, c=c, qc=qc, oc=oc)


def cross_bwd(dh3, sv, slots, cuts, pool, gain, wq, wo):
    g3 = bf(dh3)
    doc = bf(mm_t(g3, wo))
    dqc, dpool = cross_attention_bwd(sv["qc"], doc, pool, slots, cuts)
    dc = mm_t(dqc, wq)
    dx, d_gain, d_bias = norm_bwd(dc, sv["csave"], gain)
    pairs = dict(oc=sv["oc"], g3=g3, c=sv["c"], dqc=dqc)
    return dh3 + dx, (d_gain, d_bias), pairs, dpool


def gelu(z):
    return jax.nn.gelu(z, approximate=False)


def ffn_fwd(h3, gain, bias, w_up, b_up, w_down, b_down):
    y, usave = norm_fwd(h3, gain, bias)
    u = bf(y)
    z = mm(u, w_up) + b_up
    f = bf(gelu(z))
    out = h3 + (mm(f, w_down) + b_down)
    return out, dict(usave=usave, u=u, z=z, f=f)


def ffn_bwd(gout, sv, gain, w_up, w_down):
    gb = bf(gout)
    df = mm_t(gb, w_down)
    _, pull = jax.vjp(gelu, sv["z"])
    dz = bf(pull(df)[0])
    du = mm_t(dz, w_up)
    dx, d_gain, d_bias = norm_bwd(du, sv["usave"], gain)
    pairs = dict(f=sv["f"], gb=gb, u=sv["u"], dz=dz)
    return gout + dx, (d_gain, d_bias), pairs


def chip_cycle(mesh):
    n_dp = mesh.shape["dp"]
    plane = mesh.devices.reshape(-1, n_dp)[0]
    try:
        chips = {}
        for i, dev in enumerate(plane):
            chips.setdefault(tuple(dev.coords), []).append(i)
    except AttributeError:
        return list(range(n_dp))
    keys = sorted(chips)
    if len(keys) < 3:
        return [i for k in keys for i in sorted(chips[k])]
    near = {
        k: [j for j in keys if sum(abs(a - b) for a, b in zip(k, j)) == 1] for k in keys
    }
    path, seen, budget = [keys[0]], {keys[0]}, [200000]

    def walk():
        budget[0] -= 1
        if budget[0] < 0:
            return False
        if len(path) == len(keys):
            return keys[0] in near[path[-1]]
        options = sorted(
            (j for j in near[path[-1]] if j not in seen),
            key=lambda j: sum(1 for n in near[j] if n not in seen),
        )
        for j in options:
            path.append(j)
            seen.add(j)
            if walk():
                return True
            path.pop()
            seen.discard(j)
        return False

    if not walk():
        return list(range(n_dp))
    return [i for k in path for i in sorted(chips[k])]


def ring_reduce_scatter(packed, plane, cycle, dp_index):
    n = len(cycle)
    n_dp = packed.shape[0]
    axes = ("section", "dp")
    fwd = [(plane * n_dp + cycle[i], plane * n_dp + cycle[(i + 1) % n]) for i in range(n)]
    bwd = [(b, a) for a, b in fwd]
    where_in = [0] * n
    for i, d in enumerate(cycle):
        where_in[d] = i
    order = jnp.array(cycle * 2, jnp.int32)
    half = packed.shape[-1] // 2
    cw, ccw = packed[..., :half], packed[..., half:]
    p = jnp.array(where_in, jnp.int32)[dp_index]

    def take(a, idx):
        return lax.dynamic_index_in_dim(a, order[idx % n], 0, keepdims=False)

    send_c, send_w = take(cw, p + n - 1), take(ccw, p + 1)
    for step in range(n - 1):
        got_c = lax.ppermute(send_c, axes, fwd)
        got_w = lax.ppermute(send_w, axes, bwd)
        acc_c = got_c.astype(F32) + take(cw, p + 2 * n - step - 2).astype(F32)
        acc_w = got_w.astype(F32) + take(ccw, p + step + 2).astype(F32)
        send_c, send_w = bf(acc_c), bf(acc_w)
    return jnp.concatenate([acc_c, acc_w], -1)


def pack_rows(arrays, n, rows):
    pieces = [bf(a).reshape(n, rows, -1) for a in arrays if a.ndim == 2]
    vecs = jnp.concatenate([bf(a).reshape(n, -1) for a in arrays if a.ndim == 1], 1)
    width = -(-vecs.shape[1] // rows)
    vecs = jnp.pad(vecs, ((0, 0), (0, width * rows - vecs.shape[1]))).reshape(n, rows, width)
    pieces.append(vecs)
    cols = sum(x.shape[-1] for x in pieces)
    target = -(-cols // 256) * 256
    pieces.append(jnp.zeros((n, rows, target - cols), BF16))
    return jnp.concatenate(pieces, -1)


def unpack_row(block, arrays, n, rows):
    out, at = [], 0
    mats = {}
    for i, a in enumerate(arrays):
        if a.ndim == 2:
            width = a.size // n // rows
            mats[i] = block[:, at : at + width].reshape((a.shape[0] // n,) + a.shape[1:])
            at += width
    vec_total = sum(a.size // n for a in arrays if a.ndim == 1)
    width = -(-vec_total // rows)
    flat = block[:, at : at + width].reshape(-1)
    vat = 0
    for i, a in enumerate(arrays):
        if a.ndim == 2:
            out.append(mats[i])
        else:
            size = a.size // n
            out.append(flat[vat : vat + size])
            vat += size
    return out


def per_device(
    cycle,
    inputs,
    cotangent,
    images,
    seg_ids,
    row_block,
    seg_image,
    ln1_gain,
    ln1_bias,
    w_qkv,
    w_out,
    ln2_gain,
    ln2_bias,
    w_up,
    b_up,
    w_down,
    b_down,
    lnc_gain,
    lnc_bias,
    wq_cross,
    wkv_cross,
    wo_cross,
):
    up = lax.axis_index("section") == 1
    low = jnp.logical_not(up)
    dp_index = lax.axis_index("dp")
    n_dp = lax.axis_size("dp")
    rows = inputs.shape[0]
    rc = rows // MICRO
    g1, b1, wqkv, wout = ln1_gain[0], ln1_bias[0], w_qkv[0], w_out[0]
    g2, b2, wup, bup, wdown, bdown = ln2_gain[0], ln2_bias[0], w_up[0], b_up[0], w_down[0], b_down[0]
    n_img = n_dp * images.shape[0]

    first_half = lax.ppermute(images[0], "section", [(0, 1)])
    full_image = jnp.concatenate([first_half, images[0]], 0)

    def make_kv(img):
        return bf(mm(img, wkv_cross))

    kv_own = run_on(up, make_kv, full_image)
    ring_up = [(i, (i + 1) % n_dp) for i in range(n_dp)]
    ring_down = [((i + 1) % n_dp, i) for i in range(n_dp)]
    kv_prev = lax.ppermute(kv_own, "dp", ring_up)
    kv_next = lax.ppermute(kv_own, "dp", ring_down)
    pool = jnp.stack([kv_prev, kv_own, kv_next], 0)
    img_tok = pool.shape[1]

    first_img = (row_block[:, None] + seg_image) % n_img
    slot = (first_img - dp_index + 1 + n_img) % n_img
    cut_all = jnp.sum((seg_ids == 0).astype(jnp.int32), 1)

    def chunk(a, m):
        return a[m * rc : (m + 1) * rc]

    x = inputs.astype(F32)

    def lower_fwd(hid, seg):
        h2, s_self = self_fwd(hid, seg, g1, b1, wqkv, wout)
        out, s_ffn = ffn_fwd(h2, g2, b2, wup, bup, wdown, bdown)
        return out, (s_self, s_ffn)

    def upper_fwd(sent, seg, slots, cuts, pool):
        hid = sent.astype(F32)
        h2, s_self = self_fwd(hid, seg, g1, b1, wqkv, wout)
        h3, s_cross = cross_fwd(h2, slots, cuts, pool, lnc_gain, lnc_bias, wq_cross, wo_cross)
        out, s_ffn = ffn_fwd(h3, g2, b2, wup, bup, wdown, bdown)
        return out, (s_self, s_cross, s_ffn)

    low_out, low_saved, sent = [], [], []
    for m in range(MICRO):
        x_m = chunk(x, m)
        if m > 0:
            x_m, low_out[-1] = lax.optimization_barrier((x_m, low_out[-1]))
        out, saved = run_on(low, lower_fwd, x_m, chunk(seg_ids, m))
        low_out.append(out)
        low_saved.append(saved)
        sent.append(lax.ppermute(bf(out), "section", [(0, 1)]))
    up_out, up_saved = [], []
    for m in range(MICRO):
        arriving = sent[m]
        if m > 0:
            arriving, up_out[-1] = lax.optimization_barrier((arriving, up_out[-1]))
        out, saved = run_on(
            up, upper_fwd, arriving, chunk(seg_ids, m), chunk(slot, m), chunk(cut_all, m), pool
        )
        up_out.append(out)
        up_saved.append(saved)

    cot = cotangent[0].astype(F32)

    def upper_bwd(gout, saved, slots, cuts, pool):
        s_self, s_cross, s_ffn = saved
        dh3, ln2g, pf = ffn_bwd(gout, s_ffn, g2, wup, wdown)
        dh2, lncg, pc, dpool = cross_bwd(dh3, s_cross, slots, cuts, pool, lnc_gain, wq_cross, wo_cross)
        dh, ln1g, ps = self_bwd(dh2, s_self, g1, wqkv, wout)
        return dh, (ln1g, ln2g, lncg), (ps, pf, pc), dpool

    up_grad, up_small, up_pairs = [], [], []
    returned = []
    pool_grad = None
    for m in range(MICRO):
        cot_m = chunk(cot, m)
        if m > 0:
            cot_m, up_grad[-1] = lax.optimization_barrier((cot_m, up_grad[-1]))
        dh, small, pairs, dpool = run_on(
            up, upper_bwd, cot_m, up_saved[m], chunk(slot, m), chunk(cut_all, m), pool
        )
        up_grad.append(dh)
        up_small.append(small)
        up_pairs.append(pairs)
        pool_grad = dpool if pool_grad is None else pool_grad + dpool
        returned.append(lax.ppermute(bf(dh), "section", [(1, 0)]))

    def cat(name_path, pairs_list):
        return jnp.concatenate([name_path(p) for p in pairs_list], 0)

    def layer_weight_grads(pairs_list):
        ps = lambda i, k: cat(lambda p: p[i][k], pairs_list)
        d_wqkv = outer(ps(0, "n"), ps(0, "dt"))
        d_wout = outer(ps(0, "o"), ps(0, "g2"))
        d_wup = outer(ps(1, "u"), ps(1, "dz"))
        d_wdown = outer(ps(1, "f"), ps(1, "gb"))
        d_bup = jnp.sum(ps(1, "dz").astype(F32), (0, 1))
        d_bdown = jnp.sum(ps(1, "gb").astype(F32), (0, 1))
        return d_wqkv, d_wout, d_wup, d_bup, d_wdown, d_bdown

    def upper_wgrads(pairs_list):
        layer = layer_weight_grads(pairs_list)
        ps = lambda k: cat(lambda p: p[2][k], pairs_list)
        d_wq = outer(ps("c"), ps("dqc"))
        d_wo = outer(ps("oc"), ps("g3"))
        return layer, (d_wq, d_wo)

    up_w, cross_w = run_on(up, upper_wgrads, up_pairs)

    parts = bf(pool_grad)
    from_next = lax.ppermute(parts[0], "dp", ring_down)
    from_prev = lax.ppermute(parts[2], "dp", ring_up)
    kv_grad = bf(parts[1].astype(F32) + from_next.astype(F32) + from_prev.astype(F32))

    def image_side(kvg, img):
        ig = jnp.einsum("te,de->td", kvg, wkv_cross, preferred_element_type=F32)
        dw = jnp.einsum("td,te->de", img, kvg, preferred_element_type=F32)
        return ig, dw

    image_grad_full, d_wkv = run_on(up, image_side, kv_grad, full_image)
    half = images.shape[1]
    ig_first = lax.ppermute(image_grad_full[:half], "section", [(1, 0)])
    image_grad = jnp.where(up, image_grad_full[half:], ig_first)[None]

    def tree_sum(xs):
        total = xs[0]
        for v in xs[1:]:
            total = jax.tree.map(jnp.add, total, v)
        return total

    def layer_list(lw, sm):
        d_wqkv, d_wout, d_wup, d_bup, d_wdown, d_bdown = lw
        return [d_wqkv, d_wout, d_wup, d_wdown, sm[0][0], sm[0][1], sm[1][0], sm[1][1], d_bup, d_bdown]

    up_sm = tree_sum(up_small)
    a_list = layer_list(up_w, up_sm) + [cross_w[0], cross_w[1], d_wkv, up_sm[2][0], up_sm[2][1]]
    block_rows = wqkv.shape[0] // n_dp
    a_packed = pack_rows(a_list, n_dp, block_rows)

    def lower_bwd(gout, saved):
        s_self, s_ffn = saved
        dh3, ln2g, pf = ffn_bwd(gout, s_ffn, g2, wup, wdown)
        dh, ln1g, ps = self_bwd(dh3, s_self, g1, wqkv, wout)
        return dh, (ln1g, ln2g), (ps, pf)

    low_grad, low_small, low_pairs = [], [], []
    for m in range(MICRO):
        gout = chunk(cot, m) + returned[m].astype(F32)
        if m == 0:
            pass
        else:
            gout, low_grad[-1] = lax.optimization_barrier((gout, low_grad[-1]))
        dh, small, pairs = run_on(low, lower_bwd, gout, low_saved[m])
        low_grad.append(dh)
        low_small.append(small)
        low_pairs.append(pairs)

    low_w = run_on(low, layer_weight_grads, low_pairs)
    low_sm = tree_sum(low_small)
    b_list = layer_list(low_w, low_sm)
    b_packed = pack_rows(b_list, n_dp, block_rows)
    a_packed, b_packed = lax.optimization_barrier((a_packed, b_packed))
    a_row = ring_reduce_scatter(a_packed, 1, cycle, dp_index)
    b_row = ring_reduce_scatter(b_packed, 0, cycle, dp_index)
    a_got = unpack_row(a_row, a_list, n_dp, block_rows)
    b_got = unpack_row(b_row, b_list, n_dp, block_rows)

    cross_out = a_got[10:]
    cross_copy = lax.ppermute(cross_out, "section", [(1, 0)])
    cross_out = [jnp.where(up, a, c) for a, c in zip(cross_out, cross_copy)]

    activations = jnp.where(
        up, jnp.concatenate(up_out, 0), jnp.concatenate(low_out, 0)
    )[None]
    back_grads = jnp.where(
        up, jnp.concatenate(up_grad, 0), jnp.concatenate(low_grad, 0)
    )[None]
    layer = [jnp.where(up, a, b)[None] for a, b in zip(a_got[:10], b_got)]
    big, small = layer[:4], [v.reshape(1, -1) for v in layer[4:]]
    d_wq, d_wo, d_wkv_sh, lnc_g, lnc_b = cross_out

    return (
        activations,
        back_grads,
        image_grad,
        small[0],
        small[1],
        big[0],
        big[1],
        small[2],
        small[3],
        big[2],
        small[4],
        big[3],
        small[5],
        lnc_g,
        lnc_b,
        d_wq,
        d_wkv_sh,
        d_wo,
    )


def solution(mesh):
    placed = (
        P("dp", None, None),
        P("section", "dp", None, None),
        P("dp", "section", None),
        P("dp", None),
        P("dp"),
        P("dp", None),
        P("section", None),
        P("section", None),
        P("section", None, None),
        P("section", None, None),
        P("section", None),
        P("section", None),
        P("section", None, None),
        P("section", None),
        P("section", None, None),
        P("section", None),
        P(),
        P(),
        P(),
        P(),
        P(),
    )
    return jax.shard_map(
        partial(per_device, chip_cycle(mesh)),
        mesh=mesh,
        in_specs=placed,
        out_specs=(
            P("section", "dp", None, None),
            P("section", "dp", None, None),
            P("dp", "section", None),
            P("section", "dp"),
            P("section", "dp"),
            P("section", "dp", None),
            P("section", "dp", None),
            P("section", "dp"),
            P("section", "dp"),
            P("section", "dp", None),
            P("section", "dp"),
            P("section", "dp", None),
            P("section", "dp"),
            P("dp"),
            P("dp"),
            P("dp", None),
            P("dp", None),
            P("dp", None),
        ),
        check_vma=False,
    )
```

```python
from functools import partial

import jax
import jax.numpy as jnp
from jax import lax
from jax.experimental import pallas as pl
from jax.experimental.pallas import tpu as pltpu
from jax.sharding import PartitionSpec as P

H = 12
HD = 64
MICRO = 4

EPS = 1e-05
MASKED = -1e30
SCALE = HD ** (-0.5)
F32 = jnp.float32
BF16 = jnp.bfloat16


def bf(x):
    return x.astype(BF16)


def run_on(flag, fn, *args):
    shapes = jax.eval_shape(fn, *args)

    def idle(*unused):
        return jax.tree.map(lambda s: jnp.zeros(s.shape, s.dtype), shapes)

    return lax.cond(flag, fn, idle, *args)


def norm_fwd(x, gain, bias):
    mean = jnp.mean(x, -1, keepdims=True)
    centred = x - mean
    var = jnp.mean(centred * centred, -1, keepdims=True)
    rstd = lax.rsqrt(var + EPS)
    xhat = centred * rstd
    return xhat * gain + bias, (xhat, rstd)


def norm_bwd(dy, saved, gain):
    xhat, rstd = saved
    lead = tuple(range(dy.ndim - 1))
    d_gain = jnp.sum(dy * xhat, lead)
    d_bias = jnp.sum(dy, lead)
    dxh = dy * gain
    dx = rstd * (
        dxh
        - jnp.mean(dxh, -1, keepdims=True)
        - xhat * jnp.mean(dxh * xhat, -1, keepdims=True)
    )
    return dx, d_gain, d_bias


def mm(a, w):
    return jnp.einsum("...d,de->...e", a, w, preferred_element_type=F32)


def mm_t(g, w):
    return jnp.einsum("...e,de->...d", g, w, preferred_element_type=F32)


def outer(a, b):
    return jnp.einsum("rtd,rte->de", a, b, preferred_element_type=F32)


def softmax_rows(s, axes):
    top = jnp.max(s, axes, keepdims=True)
    e = jnp.exp(s - top)
    return e / jnp.sum(e, axes, keepdims=True)


def self_fwd(h, seg, gain, bias, w_qkv, w_out):
    r, t = seg.shape
    y, nsave = norm_fwd(h, gain, bias)
    n = bf(y)
    trip = bf(mm(n, w_qkv)).reshape(r, t, 3, H, HD)
    q, k, v = trip[:, :, 0], trip[:, :, 1], trip[:, :, 2]
    pos = jnp.arange(t)
    allowed = (seg[:, :, None] == seg[:, None, :]) & (pos[:, None] >= pos[None, :])[None]
    s = jnp.einsum("rqhd,rkhd->rhqk", q, k, preferred_element_type=F32) * SCALE
    s = jnp.where(allowed[:, None], s, MASKED)
    p = softmax_rows(s, -1)
    o = bf(jnp.einsum("rhqk,rkhd->rqhd", bf(p), v, preferred_element_type=F32))
    o = o.reshape(r, t, H * HD)
    h2 = h + mm(o, w_out)
    saved = dict(nsave=nsave, n=n, q=q, k=k, v=v, p=p, o=o)
    return h2, saved


def self_bwd(dh2, sv, gain, w_qkv, w_out):
    r, t = dh2.shape[:2]
    g2 = bf(dh2)
    do = bf(mm_t(g2, w_out)).reshape(r, t, H, HD)
    p, q, k, v = sv["p"], sv["q"], sv["k"], sv["v"]
    dp = jnp.einsum("rqhd,rkhd->rhqk", do, v, preferred_element_type=F32)
    ds = bf(p * (dp - jnp.sum(p * dp, -1, keepdims=True)))
    dq = jnp.einsum("rhqk,rkhd->rqhd", ds, k, preferred_element_type=F32) * SCALE
    dk = jnp.einsum("rhqk,rqhd->rkhd", ds, q, preferred_element_type=F32) * SCALE
    dv = jnp.einsum("rhqk,rqhd->rkhd", bf(p), do, preferred_element_type=F32)
    dt = bf(jnp.stack([dq, dk, dv], 2)).reshape(r, t, 3 * H * HD)
    dn = mm_t(dt, w_qkv)
    dx, d_gain, d_bias = norm_bwd(dn, sv["nsave"], gain)
    pairs = dict(o=sv["o"], g2=g2, n=sv["n"], dt=dt)
    return dh2 + dx, (d_gain, d_bias), pairs


RB = 2


def _dot_nt(a, b):
    return lax.dot_general(a, b, (((1,), (1,)), ((), ())), preferred_element_type=F32)


def _dot_tn(a, b):
    return lax.dot_general(a, b, (((0,), (0,)), ((), ())), preferred_element_type=F32)


def _dot(a, b):
    return lax.dot_general(a, b, (((1,), (0,)), ((), ())), preferred_element_type=F32)


def _probs(q, ka, kb, first):
    sa = _dot_nt(q, ka) * SCALE
    sb = _dot_nt(q, kb) * SCALE
    s = jnp.where(first, sa, sb)
    top = jnp.max(s, -1, keepdims=True)
    e = jnp.exp(s - top)
    return e / jnp.sum(e, -1, keepdims=True)


def _fwd_kernel(slot_ref, cut_ref, q_ref, pool_ref, o_ref):
    i = pl.program_id(0)
    t = q_ref.shape[1]
    d = H * HD
    for j in range(RB):
        r = i * RB + j
        a = slot_ref[2 * r]
        b = slot_ref[2 * r + 1]
        first = lax.broadcasted_iota(jnp.int32, (t, 1), 0) < cut_ref[r]
        for h in range(H):
            cols = pl.ds(h * HD, HD)
            vcols = pl.ds(d + h * HD, HD)
            q = q_ref[j, :, cols]
            p = _probs(q, pool_ref[a, :, cols], pool_ref[b, :, cols], first).astype(BF16)
            zero = jnp.zeros_like(p)
            o = _dot(jnp.where(first, p, zero), pool_ref[a, :, vcols]) + _dot(
                jnp.where(first, zero, p), pool_ref[b, :, vcols]
            )
            o_ref[j, :, cols] = o.astype(o_ref.dtype)


def _bwd_kernel(slot_ref, cut_ref, q_ref, do_ref, pool_ref, dq_ref, dpool_ref):
    i = pl.program_id(0)
    t = q_ref.shape[1]
    d = H * HD

    @pl.when(i == 0)
    def _():
        dpool_ref[...] = jnp.zeros_like(dpool_ref)

    for j in range(RB):
        r = i * RB + j
        a = slot_ref[2 * r]
        b = slot_ref[2 * r + 1]
        first = lax.broadcasted_iota(jnp.int32, (t, 1), 0) < cut_ref[r]
        for h in range(H):
            cols = pl.ds(h * HD, HD)
            vcols = pl.ds(d + h * HD, HD)
            q = q_ref[j, :, cols]
            do = do_ref[j, :, cols]
            ka = pool_ref[a, :, cols]
            kb = pool_ref[b, :, cols]
            va = pool_ref[a, :, vcols]
            vb = pool_ref[b, :, vcols]
            p = _probs(q, ka, kb, first)
            dp = jnp.where(first, _dot_nt(do, va), _dot_nt(do, vb))
            ds = (p * (dp - jnp.sum(p * dp, -1, keepdims=True))).astype(BF16)
            zero = jnp.zeros_like(ds)
            dsa = jnp.where(first, ds, zero)
            dsb = jnp.where(first, zero, ds)
            dq = (_dot(dsa, ka) + _dot(dsb, kb)) * SCALE
            dq_ref[j, :, cols] = dq.astype(dq_ref.dtype)
            pb = p.astype(BF16)
            pa_ = jnp.where(first, pb, zero)
            pb_ = jnp.where(first, zero, pb)
            dpool_ref[a, :, cols] += _dot_tn(dsa, q) * SCALE
            dpool_ref[a, :, vcols] += _dot_tn(pa_, do)
            dpool_ref[b, :, cols] += _dot_tn(dsb, q) * SCALE
            dpool_ref[b, :, vcols] += _dot_tn(pb_, do)


def cross_attention_fwd(qc, pool, slots, cuts):
    r, t, d = qc.shape
    spec = pltpu.PrefetchScalarGridSpec(
        num_scalar_prefetch=2,
        grid=(r // RB,),
        in_specs=[
            pl.BlockSpec((RB, t, d), lambda i, s, c: (i, 0, 0)),
            pl.BlockSpec(pool.shape, lambda i, s, c: (0, 0, 0)),
        ],
        out_specs=pl.BlockSpec((RB, t, d), lambda i, s, c: (i, 0, 0)),
    )
    flops = r * H * 4 * 2 * t * pool.shape[1] * HD
    return pl.pallas_call(
        _fwd_kernel,
        grid_spec=spec,
        out_shape=jax.ShapeDtypeStruct((r, t, d), BF16),
        compiler_params=pltpu.CompilerParams(
            dimension_semantics=("arbitrary",), vmem_limit_bytes=48 * 1024 * 1024
        ),
        cost_estimate=pl.CostEstimate(
            flops=flops,
            transcendentals=r * H * t * 2 * pool.shape[1],
            bytes_accessed=2 * qc.size * 2 + pool.size * 2,
        ),
    )(slots.reshape(-1), cuts, qc, pool)


def cross_attention_bwd(qc, doc, pool, slots, cuts):
    r, t, d = qc.shape
    spec = pltpu.PrefetchScalarGridSpec(
        num_scalar_prefetch=2,
        grid=(r // RB,),
        in_specs=[
            pl.BlockSpec((RB, t, d), lambda i, s, c: (i, 0, 0)),
            pl.BlockSpec((RB, t, d), lambda i, s, c: (i, 0, 0)),
            pl.BlockSpec(pool.shape, lambda i, s, c: (0, 0, 0)),
        ],
        out_specs=[
            pl.BlockSpec((RB, t, d), lambda i, s, c: (i, 0, 0)),
            pl.BlockSpec(pool.shape, lambda i, s, c: (0, 0, 0)),
        ],
    )
    flops = r * H * 10 * 2 * t * pool.shape[1] * HD
    return pl.pallas_call(
        _bwd_kernel,
        grid_spec=spec,
        out_shape=(
            jax.ShapeDtypeStruct((r, t, d), BF16),
            jax.ShapeDtypeStruct(pool.shape, F32),
        ),
        compiler_params=pltpu.CompilerParams(
            dimension_semantics=("arbitrary",), vmem_limit_bytes=60 * 1024 * 1024
        ),
        cost_estimate=pl.CostEstimate(
            flops=flops,
            transcendentals=r * H * t * 2 * pool.shape[1],
            bytes_accessed=3 * qc.size * 2 + pool.size * 2 + pool.size * 4,
        ),
    )(slots.reshape(-1), cuts, qc, doc, pool)


def cross_fwd(h2, slots, cuts, pool, gain, bias, wq, wo):
    y, csave = norm_fwd(h2, gain, bias)
    c = bf(y)
    qc = bf(mm(c, wq))
    oc = cross_attention_fwd(qc, pool, slots, cuts)
    h3 = h2 + mm(oc, wo)
    return h3, dict(csave=csave, c=c, qc=qc, oc=oc)


def cross_bwd(dh3, sv, slots, cuts, pool, gain, wq, wo):
    g3 = bf(dh3)
    doc = bf(mm_t(g3, wo))
    dqc, dpool = cross_attention_bwd(sv["qc"], doc, pool, slots, cuts)
    dc = mm_t(dqc, wq)
    dx, d_gain, d_bias = norm_bwd(dc, sv["csave"], gain)
    pairs = dict(oc=sv["oc"], g3=g3, c=sv["c"], dqc=dqc)
    return dh3 + dx, (d_gain, d_bias), pairs, dpool


def gelu(z):
    return jax.nn.gelu(z, approximate=False)


def ffn_fwd(h3, gain, bias, w_up, b_up, w_down, b_down):
    y, usave = norm_fwd(h3, gain, bias)
    u = bf(y)
    z = mm(u, w_up) + b_up
    f = bf(gelu(z))
    out = h3 + (mm(f, w_down) + b_down)
    return out, dict(usave=usave, u=u, z=z, f=f)


def ffn_bwd(gout, sv, gain, w_up, w_down):
    gb = bf(gout)
    df = mm_t(gb, w_down)
    _, pull = jax.vjp(gelu, sv["z"])
    dz = bf(pull(df)[0])
    du = mm_t(dz, w_up)
    dx, d_gain, d_bias = norm_bwd(du, sv["usave"], gain)
    pairs = dict(f=sv["f"], gb=gb, u=sv["u"], dz=dz)
    return gout + dx, (d_gain, d_bias), pairs


def chip_cycle(mesh):
    n_dp = mesh.shape["dp"]
    plane = mesh.devices.reshape(-1, n_dp)[0]
    try:
        chips = {}
        for i, dev in enumerate(plane):
            chips.setdefault(tuple(dev.coords), []).append(i)
    except AttributeError:
        return list(range(n_dp))
    keys = sorted(chips)
    if len(keys) < 3:
        return [i for k in keys for i in sorted(chips[k])]
    near = {
        k: [j for j in keys if sum(abs(a - b) for a, b in zip(k, j)) == 1] for k in keys
    }
    path, seen, budget = [keys[0]], {keys[0]}, [200000]

    def walk():
        budget[0] -= 1
        if budget[0] < 0:
            return False
        if len(path) == len(keys):
            return keys[0] in near[path[-1]]
        options = sorted(
            (j for j in near[path[-1]] if j not in seen),
            key=lambda j: sum(1 for n in near[j] if n not in seen),
        )
        for j in options:
            path.append(j)
            seen.add(j)
            if walk():
                return True
            path.pop()
            seen.discard(j)
        return False

    if not walk():
        return list(range(n_dp))
    return [i for k in path for i in sorted(chips[k])]


def ring_reduce_scatter(packed, plane, cycle, dp_index):
    n = len(cycle)
    n_dp = packed.shape[0]
    axes = ("section", "dp")
    fwd = [(plane * n_dp + cycle[i], plane * n_dp + cycle[(i + 1) % n]) for i in range(n)]
    bwd = [(b, a) for a, b in fwd]
    where_in = [0] * n
    for i, d in enumerate(cycle):
        where_in[d] = i
    order = jnp.array(cycle * 2, jnp.int32)
    half = packed.shape[-1] // 2
    cw, ccw = packed[..., :half], packed[..., half:]
    p = jnp.array(where_in, jnp.int32)[dp_index]

    def take(a, idx):
        return lax.dynamic_index_in_dim(a, order[idx % n], 0, keepdims=False)

    send_c, send_w = take(cw, p + n - 1), take(ccw, p + 1)
    for step in range(n - 1):
        got_c = lax.ppermute(send_c, axes, fwd)
        got_w = lax.ppermute(send_w, axes, bwd)
        acc_c = got_c.astype(F32) + take(cw, p + 2 * n - step - 2).astype(F32)
        acc_w = got_w.astype(F32) + take(ccw, p + step + 2).astype(F32)
        send_c, send_w = bf(acc_c), bf(acc_w)
    return jnp.concatenate([acc_c, acc_w], -1)


def pack_rows(arrays, n, rows):
    pieces = [bf(a).reshape(n, rows, -1) for a in arrays if a.ndim == 2]
    vecs = jnp.concatenate([bf(a).reshape(n, -1) for a in arrays if a.ndim == 1], 1)
    width = -(-vecs.shape[1] // rows)
    vecs = jnp.pad(vecs, ((0, 0), (0, width * rows - vecs.shape[1]))).reshape(n, rows, width)
    pieces.append(vecs)
    cols = sum(x.shape[-1] for x in pieces)
    target = -(-cols // 256) * 256
    pieces.append(jnp.zeros((n, rows, target - cols), BF16))
    return jnp.concatenate(pieces, -1)


def unpack_row(block, arrays, n, rows):
    out, at = [], 0
    mats = {}
    for i, a in enumerate(arrays):
        if a.ndim == 2:
            width = a.size // n // rows
            mats[i] = block[:, at : at + width].reshape((a.shape[0] // n,) + a.shape[1:])
            at += width
    vec_total = sum(a.size // n for a in arrays if a.ndim == 1)
    width = -(-vec_total // rows)
    flat = block[:, at : at + width].reshape(-1)
    vat = 0
    for i, a in enumerate(arrays):
        if a.ndim == 2:
            out.append(mats[i])
        else:
            size = a.size // n
            out.append(flat[vat : vat + size])
            vat += size
    return out


def per_device(
    cycle,
    inputs,
    cotangent,
    images,
    seg_ids,
    row_block,
    seg_image,
    ln1_gain,
    ln1_bias,
    w_qkv,
    w_out,
    ln2_gain,
    ln2_bias,
    w_up,
    b_up,
    w_down,
    b_down,
    lnc_gain,
    lnc_bias,
    wq_cross,
    wkv_cross,
    wo_cross,
):
    up = lax.axis_index("section") == 1
    low = jnp.logical_not(up)
    dp_index = lax.axis_index("dp")
    n_dp = lax.axis_size("dp")
    rows = inputs.shape[0]
    rc = rows // MICRO
    g1, b1, wqkv, wout = ln1_gain[0], ln1_bias[0], w_qkv[0], w_out[0]
    g2, b2, wup, bup, wdown, bdown = ln2_gain[0], ln2_bias[0], w_up[0], b_up[0], w_down[0], b_down[0]
    n_img = n_dp * images.shape[0]

    first_half = lax.ppermute(images[0], "section", [(0, 1)])
    full_image = jnp.concatenate([first_half, images[0]], 0)

    def make_kv(img):
        return bf(mm(img, wkv_cross))

    kv_own = run_on(up, make_kv, full_image)
    ring_up = [(i, (i + 1) % n_dp) for i in range(n_dp)]
    ring_down = [((i + 1) % n_dp, i) for i in range(n_dp)]
    kv_prev = lax.ppermute(kv_own, "dp", ring_up)
    kv_next = lax.ppermute(kv_own, "dp", ring_down)
    pool = jnp.stack([kv_prev, kv_own, kv_next], 0)
    img_tok = pool.shape[1]

    first_img = (row_block[:, None] + seg_image) % n_img
    slot = (first_img - dp_index + 1 + n_img) % n_img
    cut_all = jnp.sum((seg_ids == 0).astype(jnp.int32), 1)

    def chunk(a, m):
        return a[m * rc : (m + 1) * rc]

    x = inputs.astype(F32)

    def lower_fwd(hid, seg):
        h2, s_self = self_fwd(hid, seg, g1, b1, wqkv, wout)
        out, s_ffn = ffn_fwd(h2, g2, b2, wup, bup, wdown, bdown)
        return out, (s_self, s_ffn)

    def upper_fwd(sent, seg, slots, cuts, pool):
        hid = sent.astype(F32)
        h2, s_self = self_fwd(hid, seg, g1, b1, wqkv, wout)
        h3, s_cross = cross_fwd(h2, slots, cuts, pool, lnc_gain, lnc_bias, wq_cross, wo_cross)
        out, s_ffn = ffn_fwd(h3, g2, b2, wup, bup, wdown, bdown)
        return out, (s_self, s_cross, s_ffn)

    low_out, low_saved, sent = [], [], []
    for m in range(MICRO):
        x_m = chunk(x, m)
        if m > 0:
            x_m, low_out[-1] = lax.optimization_barrier((x_m, low_out[-1]))
        out, saved = run_on(low, lower_fwd, x_m, chunk(seg_ids, m))
        low_out.append(out)
        low_saved.append(saved)
        sent.append(lax.ppermute(bf(out), "section", [(0, 1)]))
    up_out, up_saved = [], []
    for m in range(MICRO):
        arriving = sent[m]
        if m > 0:
            arriving, up_out[-1] = lax.optimization_barrier((arriving, up_out[-1]))
        out, saved = run_on(
            up, upper_fwd, arriving, chunk(seg_ids, m), chunk(slot, m), chunk(cut_all, m), pool
        )
        up_out.append(out)
        up_saved.append(saved)

    cot = cotangent[0].astype(F32)

    def upper_bwd(gout, saved, slots, cuts, pool):
        s_self, s_cross, s_ffn = saved
        dh3, ln2g, pf = ffn_bwd(gout, s_ffn, g2, wup, wdown)
        dh2, lncg, pc, dpool = cross_bwd(dh3, s_cross, slots, cuts, pool, lnc_gain, wq_cross, wo_cross)
        dh, ln1g, ps = self_bwd(dh2, s_self, g1, wqkv, wout)
        return dh, (ln1g, ln2g, lncg), (ps, pf, pc), dpool

    up_grad, up_small, up_pairs = [], [], []
    returned = []
    pool_grad = None
    for m in range(MICRO):
        cot_m = chunk(cot, m)
        if m > 0:
            cot_m, up_grad[-1] = lax.optimization_barrier((cot_m, up_grad[-1]))
        dh, small, pairs, dpool = run_on(
            up, upper_bwd, cot_m, up_saved[m], chunk(slot, m), chunk(cut_all, m), pool
        )
        up_grad.append(dh)
        up_small.append(small)
        up_pairs.append(pairs)
        pool_grad = dpool if pool_grad is None else pool_grad + dpool
        returned.append(lax.ppermute(bf(dh), "section", [(1, 0)]))

    def cat(name_path, pairs_list):
        return jnp.concatenate([name_path(p) for p in pairs_list], 0)

    def layer_weight_grads(pairs_list):
        ps = lambda i, k: cat(lambda p: p[i][k], pairs_list)
        d_wqkv = outer(ps(0, "n"), ps(0, "dt"))
        d_wout = outer(ps(0, "o"), ps(0, "g2"))
        d_wup = outer(ps(1, "u"), ps(1, "dz"))
        d_wdown = outer(ps(1, "f"), ps(1, "gb"))
        d_bup = jnp.sum(ps(1, "dz").astype(F32), (0, 1))
        d_bdown = jnp.sum(ps(1, "gb").astype(F32), (0, 1))
        return d_wqkv, d_wout, d_wup, d_bup, d_wdown, d_bdown

    def upper_wgrads(pairs_list):
        layer = layer_weight_grads(pairs_list)
        ps = lambda k: cat(lambda p: p[2][k], pairs_list)
        d_wq = outer(ps("c"), ps("dqc"))
        d_wo = outer(ps("oc"), ps("g3"))
        return layer, (d_wq, d_wo)

    up_w, cross_w = run_on(up, upper_wgrads, up_pairs)

    parts = bf(pool_grad)
    from_next = lax.ppermute(parts[0], "dp", ring_down)
    from_prev = lax.ppermute(parts[2], "dp", ring_up)
    kv_grad = bf(parts[1].astype(F32) + from_next.astype(F32) + from_prev.astype(F32))

    def image_side(kvg, img):
        ig = jnp.einsum("te,de->td", kvg, wkv_cross, preferred_element_type=F32)
        dw = jnp.einsum("td,te->de", img, kvg, preferred_element_type=F32)
        return ig, dw

    image_grad_full, d_wkv = run_on(up, image_side, kv_grad, full_image)
    half = images.shape[1]
    ig_first = lax.ppermute(image_grad_full[:half], "section", [(1, 0)])
    image_grad = jnp.where(up, image_grad_full[half:], ig_first)[None]

    def tree_sum(xs):
        total = xs[0]
        for v in xs[1:]:
            total = jax.tree.map(jnp.add, total, v)
        return total

    def layer_list(lw, sm):
        d_wqkv, d_wout, d_wup, d_bup, d_wdown, d_bdown = lw
        return [d_wqkv, d_wout, d_wup, d_wdown, sm[0][0], sm[0][1], sm[1][0], sm[1][1], d_bup, d_bdown]

    up_sm = tree_sum(up_small)
    a_list = layer_list(up_w, up_sm) + [cross_w[0], cross_w[1], d_wkv, up_sm[2][0], up_sm[2][1]]
    block_rows = wqkv.shape[0] // n_dp
    a_packed = pack_rows(a_list, n_dp, block_rows)

    def lower_bwd(gout, saved):
        s_self, s_ffn = saved
        dh3, ln2g, pf = ffn_bwd(gout, s_ffn, g2, wup, wdown)
        dh, ln1g, ps = self_bwd(dh3, s_self, g1, wqkv, wout)
        return dh, (ln1g, ln2g), (ps, pf)

    low_grad, low_small, low_pairs = [], [], []
    for m in range(MICRO):
        gout = chunk(cot, m) + returned[m].astype(F32)
        if m == 0:
            pass
        else:
            gout, low_grad[-1] = lax.optimization_barrier((gout, low_grad[-1]))
        dh, small, pairs = run_on(low, lower_bwd, gout, low_saved[m])
        low_grad.append(dh)
        low_small.append(small)
        low_pairs.append(pairs)

    low_w = run_on(low, layer_weight_grads, low_pairs)
    low_sm = tree_sum(low_small)
    b_list = layer_list(low_w, low_sm)
    b_packed = pack_rows(b_list, n_dp, block_rows)
    a_packed, b_packed = lax.optimization_barrier((a_packed, b_packed))
    a_row = ring_reduce_scatter(a_packed, 1, cycle, dp_index)
    b_row = ring_reduce_scatter(b_packed, 0, cycle, dp_index)
    a_got = unpack_row(a_row, a_list, n_dp, block_rows)
    b_got = unpack_row(b_row, b_list, n_dp, block_rows)

    cross_out = a_got[10:]
    cross_copy = lax.ppermute(cross_out, "section", [(1, 0)])
    cross_out = [jnp.where(up, a, c) for a, c in zip(cross_out, cross_copy)]

    activations = jnp.where(
        up, jnp.concatenate(up_out, 0), jnp.concatenate(low_out, 0)
    )[None]
    back_grads = jnp.where(
        up, jnp.concatenate(up_grad, 0), jnp.concatenate(low_grad, 0)
    )[None]
    layer = [jnp.where(up, a, b)[None] for a, b in zip(a_got[:10], b_got)]
    big, small = layer[:4], [v.reshape(1, -1) for v in layer[4:]]
    d_wq, d_wo, d_wkv_sh, lnc_g, lnc_b = cross_out

    return (
        activations,
        back_grads,
        image_grad,
        small[0],
        small[1],
        big[0],
        big[1],
        small[2],
        small[3],
        big[2],
        small[4],
        big[3],
        small[5],
        lnc_g,
        lnc_b,
        d_wq,
        d_wkv_sh,
        d_wo,
    )


def solution(mesh):
    placed = (
        P("dp", None, None),
        P("section", "dp", None, None),
        P("dp", "section", None),
        P("dp", None),
        P("dp"),
        P("dp", None),
        P("section", None),
        P("section", None),
        P("section", None, None),
        P("section", None, None),
        P("section", None),
        P("section", None),
        P("section", None, None),
        P("section", None),
        P("section", None, None),
        P("section", None),
        P(),
        P(),
        P(),
        P(),
        P(),
    )
    return jax.shard_map(
        partial(per_device, chip_cycle(mesh)),
        mesh=mesh,
        in_specs=placed,
        out_specs=(
            P("section", "dp", None, None),
            P("section", "dp", None, None),
            P("dp", "section", None),
            P("section", "dp"),
            P("section", "dp"),
            P("section", "dp", None),
            P("section", "dp", None),
            P("section", "dp"),
            P("section", "dp"),
            P("section", "dp", None),
            P("section", "dp"),
            P("section", "dp", None),
            P("section", "dp"),
            P("dp"),
            P("dp"),
            P("dp", None),
            P("dp", None),
            P("dp", None),
        ),
        check_vma=False,
    )
```

```python
from functools import partial

import jax
import jax.numpy as jnp
from jax import lax
from jax.experimental import pallas as pl
from jax.experimental.pallas import tpu as pltpu
from jax.sharding import PartitionSpec as P

H = 12
HD = 64
MICRO = 2

EPS = 1e-05
MASKED = -1e30
SCALE = HD ** (-0.5)
F32 = jnp.float32
BF16 = jnp.bfloat16


def bf(x):
    return x.astype(BF16)


def run_on(flag, fn, *args):
    shapes = jax.eval_shape(fn, *args)

    def idle(*unused):
        return jax.tree.map(lambda s: jnp.zeros(s.shape, s.dtype), shapes)

    return lax.cond(flag, fn, idle, *args)


def norm_fwd(x, gain, bias):
    mean = jnp.mean(x, -1, keepdims=True)
    centred = x - mean
    var = jnp.mean(centred * centred, -1, keepdims=True)
    rstd = lax.rsqrt(var + EPS)
    xhat = centred * rstd
    return xhat * gain + bias, (xhat, rstd)


def norm_bwd(dy, saved, gain):
    xhat, rstd = saved
    lead = tuple(range(dy.ndim - 1))
    d_gain = jnp.sum(dy * xhat, lead)
    d_bias = jnp.sum(dy, lead)
    dxh = dy * gain
    dx = rstd * (
        dxh
        - jnp.mean(dxh, -1, keepdims=True)
        - xhat * jnp.mean(dxh * xhat, -1, keepdims=True)
    )
    return dx, d_gain, d_bias


def mm(a, w):
    return jnp.einsum("...d,de->...e", a, w, preferred_element_type=F32)


def mm_t(g, w):
    return jnp.einsum("...e,de->...d", g, w, preferred_element_type=F32)


def outer(a, b):
    return jnp.einsum("rtd,rte->de", a, b, preferred_element_type=F32)


def softmax_rows(s, axes):
    top = jnp.max(s, axes, keepdims=True)
    e = jnp.exp(s - top)
    return e / jnp.sum(e, axes, keepdims=True)


def self_fwd(h, seg, gain, bias, w_qkv, w_out):
    r, t = seg.shape
    y, nsave = norm_fwd(h, gain, bias)
    n = bf(y)
    trip = bf(mm(n, w_qkv)).reshape(r, t, 3, H, HD)
    q, k, v = trip[:, :, 0], trip[:, :, 1], trip[:, :, 2]
    pos = jnp.arange(t)
    allowed = (seg[:, :, None] == seg[:, None, :]) & (pos[:, None] >= pos[None, :])[None]
    s = jnp.einsum("rqhd,rkhd->rhqk", q, k, preferred_element_type=F32) * SCALE
    s = jnp.where(allowed[:, None], s, MASKED)
    p = softmax_rows(s, -1)
    o = bf(jnp.einsum("rhqk,rkhd->rqhd", bf(p), v, preferred_element_type=F32))
    o = o.reshape(r, t, H * HD)
    h2 = h + mm(o, w_out)
    saved = dict(nsave=nsave, n=n, q=q, k=k, v=v, p=p, o=o)
    return h2, saved


def self_bwd(dh2, sv, gain, w_qkv, w_out):
    r, t = dh2.shape[:2]
    g2 = bf(dh2)
    do = bf(mm_t(g2, w_out)).reshape(r, t, H, HD)
    p, q, k, v = sv["p"], sv["q"], sv["k"], sv["v"]
    dp = jnp.einsum("rqhd,rkhd->rhqk", do, v, preferred_element_type=F32)
    ds = bf(p * (dp - jnp.sum(p * dp, -1, keepdims=True)))
    dq = jnp.einsum("rhqk,rkhd->rqhd", ds, k, preferred_element_type=F32) * SCALE
    dk = jnp.einsum("rhqk,rqhd->rkhd", ds, q, preferred_element_type=F32) * SCALE
    dv = jnp.einsum("rhqk,rqhd->rkhd", bf(p), do, preferred_element_type=F32)
    dt = bf(jnp.stack([dq, dk, dv], 2)).reshape(r, t, 3 * H * HD)
    dn = mm_t(dt, w_qkv)
    dx, d_gain, d_bias = norm_bwd(dn, sv["nsave"], gain)
    pairs = dict(o=sv["o"], g2=g2, n=sv["n"], dt=dt)
    return dh2 + dx, (d_gain, d_bias), pairs


RB = 2


def _dot_nt(a, b):
    return lax.dot_general(a, b, (((1,), (1,)), ((), ())), preferred_element_type=F32)


def _dot_tn(a, b):
    return lax.dot_general(a, b, (((0,), (0,)), ((), ())), preferred_element_type=F32)


def _dot(a, b):
    return lax.dot_general(a, b, (((1,), (0,)), ((), ())), preferred_element_type=F32)


LO = 16
HI = 48


def _join(top, bottom, first):
    t = first.shape[0]
    mid = jnp.where(first[LO:HI], top[LO:HI], bottom[: HI - LO])
    return jnp.concatenate([top[:LO], mid, bottom[HI - LO :]], 0)


def _split(x, first):
    zero = jnp.zeros_like(x)
    return jnp.where(first, x, zero)[:HI], jnp.where(first, zero, x)[LO:]


def _probs(q, ka, kb, first):
    sa = _dot_nt(q[:HI], ka) * SCALE
    sb = _dot_nt(q[LO:], kb) * SCALE
    s = _join(sa, sb, first)
    top = jnp.max(s, -1, keepdims=True)
    e = jnp.exp(s - top)
    return e / jnp.sum(e, -1, keepdims=True)


def _fwd_kernel(slot_ref, cut_ref, q_ref, pool_ref, o_ref):
    i = pl.program_id(0)
    t = q_ref.shape[1]
    d = H * HD
    for j in range(RB):
        r = i * RB + j
        a = slot_ref[2 * r]
        b = slot_ref[2 * r + 1]
        first = lax.broadcasted_iota(jnp.int32, (t, 1), 0) < cut_ref[r]
        for h in range(H):
            cols = pl.ds(h * HD, HD)
            vcols = pl.ds(d + h * HD, HD)
            q = q_ref[j, :, cols]
            p = _probs(q, pool_ref[a, :, cols], pool_ref[b, :, cols], first).astype(BF16)
            pa, pb = _split(p, first)
            oa = _dot(pa, pool_ref[a, :, vcols])
            ob = _dot(pb, pool_ref[b, :, vcols])
            o = jnp.concatenate([oa[:LO], oa[LO:] + ob[: HI - LO], ob[HI - LO :]], 0)
            o_ref[j, :, cols] = o.astype(o_ref.dtype)


def _bwd_kernel(slot_ref, cut_ref, q_ref, do_ref, pool_ref, dq_ref, dpool_ref):
    i = pl.program_id(0)
    t = q_ref.shape[1]
    d = H * HD

    @pl.when(i == 0)
    def _():
        dpool_ref[...] = jnp.zeros_like(dpool_ref)

    for j in range(RB):
        r = i * RB + j
        a = slot_ref[2 * r]
        b = slot_ref[2 * r + 1]
        first = lax.broadcasted_iota(jnp.int32, (t, 1), 0) < cut_ref[r]
        for h in range(H):
            cols = pl.ds(h * HD, HD)
            vcols = pl.ds(d + h * HD, HD)
            q = q_ref[j, :, cols]
            do = do_ref[j, :, cols]
            ka = pool_ref[a, :, cols]
            kb = pool_ref[b, :, cols]
            va = pool_ref[a, :, vcols]
            vb = pool_ref[b, :, vcols]
            p = _probs(q, ka, kb, first)
            dp = _join(_dot_nt(do[:HI], va), _dot_nt(do[LO:], vb), first)
            ds = (p * (dp - jnp.sum(p * dp, -1, keepdims=True))).astype(BF16)
            dsa, dsb = _split(ds, first)
            dqa = _dot(dsa, ka)
            dqb = _dot(dsb, kb)
            dq = jnp.concatenate([dqa[:LO], dqa[LO:] + dqb[: HI - LO], dqb[HI - LO :]], 0) * SCALE
            dq_ref[j, :, cols] = dq.astype(dq_ref.dtype)
            pa, pb = _split(p.astype(BF16), first)
            dpool_ref[a, :, cols] += _dot_tn(dsa, q[:HI]) * SCALE
            dpool_ref[a, :, vcols] += _dot_tn(pa, do[:HI])
            dpool_ref[b, :, cols] += _dot_tn(dsb, q[LO:]) * SCALE
            dpool_ref[b, :, vcols] += _dot_tn(pb, do[LO:])


def cross_attention_fwd(qc, pool, slots, cuts):
    r, t, d = qc.shape
    spec = pltpu.PrefetchScalarGridSpec(
        num_scalar_prefetch=2,
        grid=(r // RB,),
        in_specs=[
            pl.BlockSpec((RB, t, d), lambda i, s, c: (i, 0, 0)),
            pl.BlockSpec(pool.shape, lambda i, s, c: (0, 0, 0)),
        ],
        out_specs=pl.BlockSpec((RB, t, d), lambda i, s, c: (i, 0, 0)),
    )
    flops = r * H * 4 * 2 * t * pool.shape[1] * HD
    return pl.pallas_call(
        _fwd_kernel,
        grid_spec=spec,
        out_shape=jax.ShapeDtypeStruct((r, t, d), BF16),
        compiler_params=pltpu.CompilerParams(
            dimension_semantics=("arbitrary",), vmem_limit_bytes=48 * 1024 * 1024
        ),
        cost_estimate=pl.CostEstimate(
            flops=flops,
            transcendentals=r * H * t * 2 * pool.shape[1],
            bytes_accessed=2 * qc.size * 2 + pool.size * 2,
        ),
    )(slots.reshape(-1), cuts, qc, pool)


def cross_attention_bwd(qc, doc, pool, slots, cuts):
    r, t, d = qc.shape
    spec = pltpu.PrefetchScalarGridSpec(
        num_scalar_prefetch=2,
        grid=(r // RB,),
        in_specs=[
            pl.BlockSpec((RB, t, d), lambda i, s, c: (i, 0, 0)),
            pl.BlockSpec((RB, t, d), lambda i, s, c: (i, 0, 0)),
            pl.BlockSpec(pool.shape, lambda i, s, c: (0, 0, 0)),
        ],
        out_specs=[
            pl.BlockSpec((RB, t, d), lambda i, s, c: (i, 0, 0)),
            pl.BlockSpec(pool.shape, lambda i, s, c: (0, 0, 0)),
        ],
    )
    flops = r * H * 10 * 2 * t * pool.shape[1] * HD
    return pl.pallas_call(
        _bwd_kernel,
        grid_spec=spec,
        out_shape=(
            jax.ShapeDtypeStruct((r, t, d), BF16),
            jax.ShapeDtypeStruct(pool.shape, F32),
        ),
        compiler_params=pltpu.CompilerParams(
            dimension_semantics=("arbitrary",), vmem_limit_bytes=60 * 1024 * 1024
        ),
        cost_estimate=pl.CostEstimate(
            flops=flops,
            transcendentals=r * H * t * 2 * pool.shape[1],
            bytes_accessed=3 * qc.size * 2 + pool.size * 2 + pool.size * 4,
        ),
    )(slots.reshape(-1), cuts, qc, doc, pool)


def cross_fwd(h2, slots, cuts, pool, gain, bias, wq, wo):
    y, csave = norm_fwd(h2, gain, bias)
    c = bf(y)
    qc = bf(mm(c, wq))
    oc = cross_attention_fwd(qc, pool, slots, cuts)
    h3 = h2 + mm(oc, wo)
    return h3, dict(csave=csave, c=c, qc=qc, oc=oc)


def cross_bwd(dh3, sv, slots, cuts, pool, gain, wq, wo):
    g3 = bf(dh3)
    doc = bf(mm_t(g3, wo))
    dqc, dpool = cross_attention_bwd(sv["qc"], doc, pool, slots, cuts)
    dc = mm_t(dqc, wq)
    dx, d_gain, d_bias = norm_bwd(dc, sv["csave"], gain)
    pairs = dict(oc=sv["oc"], g3=g3, c=sv["c"], dqc=dqc)
    return dh3 + dx, (d_gain, d_bias), pairs, dpool


def gelu(z):
    return jax.nn.gelu(z, approximate=False)


def ffn_fwd(h3, gain, bias, w_up, b_up, w_down, b_down):
    y, usave = norm_fwd(h3, gain, bias)
    u = bf(y)
    z = mm(u, w_up) + b_up
    f = bf(gelu(z))
    out = h3 + (mm(f, w_down) + b_down)
    return out, dict(usave=usave, u=u, z=z, f=f)


def ffn_bwd(gout, sv, gain, w_up, w_down):
    gb = bf(gout)
    df = mm_t(gb, w_down)
    _, pull = jax.vjp(gelu, sv["z"])
    dz = bf(pull(df)[0])
    du = mm_t(dz, w_up)
    dx, d_gain, d_bias = norm_bwd(du, sv["usave"], gain)
    pairs = dict(f=sv["f"], gb=gb, u=sv["u"], dz=dz)
    return gout + dx, (d_gain, d_bias), pairs


def chip_cycle(mesh):
    n_dp = mesh.shape["dp"]
    plane = mesh.devices.reshape(-1, n_dp)[0]
    try:
        chips = {}
        for i, dev in enumerate(plane):
            chips.setdefault(tuple(dev.coords), []).append(i)
    except AttributeError:
        return list(range(n_dp))
    keys = sorted(chips)
    if len(keys) < 3:
        return [i for k in keys for i in sorted(chips[k])]
    near = {
        k: [j for j in keys if sum(abs(a - b) for a, b in zip(k, j)) == 1] for k in keys
    }
    path, seen, budget = [keys[0]], {keys[0]}, [200000]

    def walk():
        budget[0] -= 1
        if budget[0] < 0:
            return False
        if len(path) == len(keys):
            return keys[0] in near[path[-1]]
        options = sorted(
            (j for j in near[path[-1]] if j not in seen),
            key=lambda j: sum(1 for n in near[j] if n not in seen),
        )
        for j in options:
            path.append(j)
            seen.add(j)
            if walk():
                return True
            path.pop()
            seen.discard(j)
        return False

    if not walk():
        return list(range(n_dp))
    return [i for k in path for i in sorted(chips[k])]


def ring_reduce_scatter(packed, plane, cycle, dp_index):
    n = len(cycle)
    n_dp = packed.shape[0]
    axes = ("section", "dp")
    fwd = [(plane * n_dp + cycle[i], plane * n_dp + cycle[(i + 1) % n]) for i in range(n)]
    bwd = [(b, a) for a, b in fwd]
    where_in = [0] * n
    for i, d in enumerate(cycle):
        where_in[d] = i
    order = jnp.array(cycle * 2, jnp.int32)
    half = packed.shape[-1] // 2
    cw, ccw = packed[..., :half], packed[..., half:]
    p = jnp.array(where_in, jnp.int32)[dp_index]

    def take(a, idx):
        return lax.dynamic_index_in_dim(a, order[idx % n], 0, keepdims=False)

    send_c, send_w = take(cw, p + n - 1), take(ccw, p + 1)
    for step in range(n - 1):
        got_c = lax.ppermute(send_c, axes, fwd)
        got_w = lax.ppermute(send_w, axes, bwd)
        acc_c = got_c.astype(F32) + take(cw, p + 2 * n - step - 2).astype(F32)
        acc_w = got_w.astype(F32) + take(ccw, p + step + 2).astype(F32)
        send_c, send_w = bf(acc_c), bf(acc_w)
    return jnp.concatenate([acc_c, acc_w], -1)


def pack_rows(arrays, n, rows):
    pieces = [bf(a).reshape(n, rows, -1) for a in arrays if a.ndim == 2]
    vecs = jnp.concatenate([bf(a).reshape(n, -1) for a in arrays if a.ndim == 1], 1)
    width = -(-vecs.shape[1] // rows)
    vecs = jnp.pad(vecs, ((0, 0), (0, width * rows - vecs.shape[1]))).reshape(n, rows, width)
    pieces.append(vecs)
    cols = sum(x.shape[-1] for x in pieces)
    target = -(-cols // 256) * 256
    pieces.append(jnp.zeros((n, rows, target - cols), BF16))
    return jnp.concatenate(pieces, -1)


def unpack_row(block, arrays, n, rows):
    out, at = [], 0
    mats = {}
    for i, a in enumerate(arrays):
        if a.ndim == 2:
            width = a.size // n // rows
            mats[i] = block[:, at : at + width].reshape((a.shape[0] // n,) + a.shape[1:])
            at += width
    vec_total = sum(a.size // n for a in arrays if a.ndim == 1)
    width = -(-vec_total // rows)
    flat = block[:, at : at + width].reshape(-1)
    vat = 0
    for i, a in enumerate(arrays):
        if a.ndim == 2:
            out.append(mats[i])
        else:
            size = a.size // n
            out.append(flat[vat : vat + size])
            vat += size
    return out


def per_device(
    cycle,
    inputs,
    cotangent,
    images,
    seg_ids,
    row_block,
    seg_image,
    ln1_gain,
    ln1_bias,
    w_qkv,
    w_out,
    ln2_gain,
    ln2_bias,
    w_up,
    b_up,
    w_down,
    b_down,
    lnc_gain,
    lnc_bias,
    wq_cross,
    wkv_cross,
    wo_cross,
):
    up = lax.axis_index("section") == 1
    low = jnp.logical_not(up)
    dp_index = lax.axis_index("dp")
    n_dp = lax.axis_size("dp")
    rows = inputs.shape[0]
    rc = rows // MICRO
    g1, b1, wqkv, wout = ln1_gain[0], ln1_bias[0], w_qkv[0], w_out[0]
    g2, b2, wup, bup, wdown, bdown = ln2_gain[0], ln2_bias[0], w_up[0], b_up[0], w_down[0], b_down[0]
    n_img = n_dp * images.shape[0]

    first_half = lax.ppermute(images[0], "section", [(0, 1)])
    full_image = jnp.concatenate([first_half, images[0]], 0)

    def make_kv(img):
        return bf(mm(img, wkv_cross))

    kv_own = run_on(up, make_kv, full_image)
    ring_up = [(i, (i + 1) % n_dp) for i in range(n_dp)]
    ring_down = [((i + 1) % n_dp, i) for i in range(n_dp)]
    kv_prev = lax.ppermute(kv_own, "dp", ring_up)
    kv_next = lax.ppermute(kv_own, "dp", ring_down)
    pool = jnp.stack([kv_prev, kv_own, kv_next], 0)
    img_tok = pool.shape[1]

    first_img = (row_block[:, None] + seg_image) % n_img
    slot = (first_img - dp_index + 1 + n_img) % n_img
    cut_all = jnp.sum((seg_ids == 0).astype(jnp.int32), 1)

    def chunk(a, m):
        return a[m * rc : (m + 1) * rc]

    x = inputs.astype(F32)

    def lower_fwd(hid, seg):
        h2, s_self = self_fwd(hid, seg, g1, b1, wqkv, wout)
        out, s_ffn = ffn_fwd(h2, g2, b2, wup, bup, wdown, bdown)
        return out, (s_self, s_ffn)

    def upper_fwd(sent, seg, slots, cuts, pool):
        hid = sent.astype(F32)
        h2, s_self = self_fwd(hid, seg, g1, b1, wqkv, wout)
        h3, s_cross = cross_fwd(h2, slots, cuts, pool, lnc_gain, lnc_bias, wq_cross, wo_cross)
        out, s_ffn = ffn_fwd(h3, g2, b2, wup, bup, wdown, bdown)
        return out, (s_self, s_cross, s_ffn)

    low_out, low_saved, sent = [], [], []
    for m in range(MICRO):
        x_m = chunk(x, m)
        if m > 0:
            x_m, low_out[-1] = lax.optimization_barrier((x_m, low_out[-1]))
        out, saved = run_on(low, lower_fwd, x_m, chunk(seg_ids, m))
        low_out.append(out)
        low_saved.append(saved)
        sent.append(lax.ppermute(bf(out), "section", [(0, 1)]))
    up_out, up_saved = [], []
    for m in range(MICRO):
        arriving = sent[m]
        if m > 0:
            arriving, up_out[-1] = lax.optimization_barrier((arriving, up_out[-1]))
        out, saved = run_on(
            up, upper_fwd, arriving, chunk(seg_ids, m), chunk(slot, m), chunk(cut_all, m), pool
        )
        up_out.append(out)
        up_saved.append(saved)

    cot = cotangent[0].astype(F32)

    def upper_bwd(gout, saved, slots, cuts, pool):
        s_self, s_cross, s_ffn = saved
        dh3, ln2g, pf = ffn_bwd(gout, s_ffn, g2, wup, wdown)
        dh2, lncg, pc, dpool = cross_bwd(dh3, s_cross, slots, cuts, pool, lnc_gain, wq_cross, wo_cross)
        dh, ln1g, ps = self_bwd(dh2, s_self, g1, wqkv, wout)
        return dh, (ln1g, ln2g, lncg), (ps, pf, pc), dpool

    up_grad, up_small, up_pairs = [], [], []
    returned = []
    pool_grad = None
    for m in range(MICRO):
        cot_m = chunk(cot, m)
        if m > 0:
            cot_m, up_grad[-1] = lax.optimization_barrier((cot_m, up_grad[-1]))
        dh, small, pairs, dpool = run_on(
            up, upper_bwd, cot_m, up_saved[m], chunk(slot, m), chunk(cut_all, m), pool
        )
        up_grad.append(dh)
        up_small.append(small)
        up_pairs.append(pairs)
        pool_grad = dpool if pool_grad is None else pool_grad + dpool
        returned.append(lax.ppermute(bf(dh), "section", [(1, 0)]))

    def cat(name_path, pairs_list):
        return jnp.concatenate([name_path(p) for p in pairs_list], 0)

    def layer_weight_grads(pairs_list):
        ps = lambda i, k: cat(lambda p: p[i][k], pairs_list)
        d_wqkv = outer(ps(0, "n"), ps(0, "dt"))
        d_wout = outer(ps(0, "o"), ps(0, "g2"))
        d_wup = outer(ps(1, "u"), ps(1, "dz"))
        d_wdown = outer(ps(1, "f"), ps(1, "gb"))
        d_bup = jnp.sum(ps(1, "dz").astype(F32), (0, 1))
        d_bdown = jnp.sum(ps(1, "gb").astype(F32), (0, 1))
        return d_wqkv, d_wout, d_wup, d_bup, d_wdown, d_bdown

    def upper_wgrads(pairs_list):
        layer = layer_weight_grads(pairs_list)
        ps = lambda k: cat(lambda p: p[2][k], pairs_list)
        d_wq = outer(ps("c"), ps("dqc"))
        d_wo = outer(ps("oc"), ps("g3"))
        return layer, (d_wq, d_wo)

    up_w, cross_w = run_on(up, upper_wgrads, up_pairs)

    parts = bf(pool_grad)
    from_next = lax.ppermute(parts[0], "dp", ring_down)
    from_prev = lax.ppermute(parts[2], "dp", ring_up)
    kv_grad = bf(parts[1].astype(F32) + from_next.astype(F32) + from_prev.astype(F32))

    def image_side(kvg, img):
        ig = jnp.einsum("te,de->td", kvg, wkv_cross, preferred_element_type=F32)
        dw = jnp.einsum("td,te->de", img, kvg, preferred_element_type=F32)
        return ig, dw

    image_grad_full, d_wkv = run_on(up, image_side, kv_grad, full_image)
    half = images.shape[1]
    ig_first = lax.ppermute(image_grad_full[:half], "section", [(1, 0)])
    image_grad = jnp.where(up, image_grad_full[half:], ig_first)[None]

    def tree_sum(xs):
        total = xs[0]
        for v in xs[1:]:
            total = jax.tree.map(jnp.add, total, v)
        return total

    def layer_list(lw, sm):
        d_wqkv, d_wout, d_wup, d_bup, d_wdown, d_bdown = lw
        return [d_wqkv, d_wout, d_wup, d_wdown, sm[0][0], sm[0][1], sm[1][0], sm[1][1], d_bup, d_bdown]

    up_sm = tree_sum(up_small)
    a_list = layer_list(up_w, up_sm) + [cross_w[0], cross_w[1], d_wkv, up_sm[2][0], up_sm[2][1]]
    block_rows = wqkv.shape[0] // n_dp
    a_packed = pack_rows(a_list, n_dp, block_rows)

    def lower_bwd(gout, saved):
        s_self, s_ffn = saved
        dh3, ln2g, pf = ffn_bwd(gout, s_ffn, g2, wup, wdown)
        dh, ln1g, ps = self_bwd(dh3, s_self, g1, wqkv, wout)
        return dh, (ln1g, ln2g), (ps, pf)

    low_grad, low_small, low_pairs = [], [], []
    for m in range(MICRO):
        gout = chunk(cot, m) + returned[m].astype(F32)
        if m == 0:
            pass
        else:
            gout, low_grad[-1] = lax.optimization_barrier((gout, low_grad[-1]))
        dh, small, pairs = run_on(low, lower_bwd, gout, low_saved[m])
        low_grad.append(dh)
        low_small.append(small)
        low_pairs.append(pairs)

    low_w = run_on(low, layer_weight_grads, low_pairs)
    low_sm = tree_sum(low_small)
    b_list = layer_list(low_w, low_sm)
    b_packed = pack_rows(b_list, n_dp, block_rows)
    a_packed, b_packed = lax.optimization_barrier((a_packed, b_packed))
    a_row = ring_reduce_scatter(a_packed, 1, cycle, dp_index)
    b_row = ring_reduce_scatter(b_packed, 0, cycle, dp_index)
    a_got = unpack_row(a_row, a_list, n_dp, block_rows)
    b_got = unpack_row(b_row, b_list, n_dp, block_rows)

    cross_out = a_got[10:]
    cross_copy = lax.ppermute(cross_out, "section", [(1, 0)])
    cross_out = [jnp.where(up, a, c) for a, c in zip(cross_out, cross_copy)]

    activations = jnp.where(
        up, jnp.concatenate(up_out, 0), jnp.concatenate(low_out, 0)
    )[None]
    back_grads = jnp.where(
        up, jnp.concatenate(up_grad, 0), jnp.concatenate(low_grad, 0)
    )[None]
    layer = [jnp.where(up, a, b)[None] for a, b in zip(a_got[:10], b_got)]
    big, small = layer[:4], [v.reshape(1, -1) for v in layer[4:]]
    d_wq, d_wo, d_wkv_sh, lnc_g, lnc_b = cross_out

    return (
        activations,
        back_grads,
        image_grad,
        small[0],
        small[1],
        big[0],
        big[1],
        small[2],
        small[3],
        big[2],
        small[4],
        big[3],
        small[5],
        lnc_g,
        lnc_b,
        d_wq,
        d_wkv_sh,
        d_wo,
    )


def solution(mesh):
    placed = (
        P("dp", None, None),
        P("section", "dp", None, None),
        P("dp", "section", None),
        P("dp", None),
        P("dp"),
        P("dp", None),
        P("section", None),
        P("section", None),
        P("section", None, None),
        P("section", None, None),
        P("section", None),
        P("section", None),
        P("section", None, None),
        P("section", None),
        P("section", None, None),
        P("section", None),
        P(),
        P(),
        P(),
        P(),
        P(),
    )
    return jax.shard_map(
        partial(per_device, chip_cycle(mesh)),
        mesh=mesh,
        in_specs=placed,
        out_specs=(
            P("section", "dp", None, None),
            P("section", "dp", None, None),
            P("dp", "section", None),
            P("section", "dp"),
            P("section", "dp"),
            P("section", "dp", None),
            P("section", "dp", None),
            P("section", "dp"),
            P("section", "dp"),
            P("section", "dp", None),
            P("section", "dp"),
            P("section", "dp", None),
            P("section", "dp"),
            P("dp"),
            P("dp"),
            P("dp", None),
            P("dp", None),
            P("dp", None),
        ),
        check_vma=False,
    )
```

```python
from functools import partial

import jax
import jax.numpy as jnp
from jax import lax
from jax.experimental import pallas as pl
from jax.experimental.pallas import tpu as pltpu
from jax.sharding import PartitionSpec as P

H = 12
HD = 64
MICRO = 2

EPS = 1e-05
MASKED = -1e30
SCALE = HD ** (-0.5)
F32 = jnp.float32
BF16 = jnp.bfloat16


def bf(x):
    return x.astype(BF16)


def run_on(flag, fn, *args):
    shapes = jax.eval_shape(fn, *args)

    def idle(*unused):
        return jax.tree.map(lambda s: jnp.zeros(s.shape, s.dtype), shapes)

    return lax.cond(flag, fn, idle, *args)


def norm_fwd(x, gain, bias):
    mean = jnp.mean(x, -1, keepdims=True)
    centred = x - mean
    var = jnp.mean(centred * centred, -1, keepdims=True)
    rstd = lax.rsqrt(var + EPS)
    xhat = centred * rstd
    return xhat * gain + bias, (xhat, rstd)


def norm_bwd(dy, saved, gain):
    xhat, rstd = saved
    lead = tuple(range(dy.ndim - 1))
    d_gain = jnp.sum(dy * xhat, lead)
    d_bias = jnp.sum(dy, lead)
    dxh = dy * gain
    dx = rstd * (
        dxh
        - jnp.mean(dxh, -1, keepdims=True)
        - xhat * jnp.mean(dxh * xhat, -1, keepdims=True)
    )
    return dx, d_gain, d_bias


def mm(a, w):
    return jnp.einsum("...d,de->...e", a, w, preferred_element_type=F32)


def mm_t(g, w):
    return jnp.einsum("...e,de->...d", g, w, preferred_element_type=F32)


def outer(a, b):
    return jnp.einsum("rtd,rte->de", a, b, preferred_element_type=F32)


def softmax_rows(s, axes):
    top = jnp.max(s, axes, keepdims=True)
    e = jnp.exp(s - top)
    return e / jnp.sum(e, axes, keepdims=True)


def self_fwd(h, seg, gain, bias, w_qkv, w_out):
    r, t = seg.shape
    y, nsave = norm_fwd(h, gain, bias)
    n = bf(y)
    trip = bf(mm(n, w_qkv)).reshape(r, t, 3, H, HD)
    q, k, v = trip[:, :, 0], trip[:, :, 1], trip[:, :, 2]
    pos = jnp.arange(t)
    allowed = (seg[:, :, None] == seg[:, None, :]) & (pos[:, None] >= pos[None, :])[None]
    s = jnp.einsum("rqhd,rkhd->rhqk", q, k, preferred_element_type=F32) * SCALE
    s = jnp.where(allowed[:, None], s, MASKED)
    p = softmax_rows(s, -1)
    o = bf(jnp.einsum("rhqk,rkhd->rqhd", bf(p), v, preferred_element_type=F32))
    o = o.reshape(r, t, H * HD)
    h2 = h + mm(o, w_out)
    saved = dict(nsave=nsave, n=n, q=q, k=k, v=v, p=p, o=o)
    return h2, saved


def self_bwd(dh2, sv, gain, w_qkv, w_out):
    r, t = dh2.shape[:2]
    g2 = bf(dh2)
    do = bf(mm_t(g2, w_out)).reshape(r, t, H, HD)
    p, q, k, v = sv["p"], sv["q"], sv["k"], sv["v"]
    dp = jnp.einsum("rqhd,rkhd->rhqk", do, v, preferred_element_type=F32)
    ds = bf(p * (dp - jnp.sum(p * dp, -1, keepdims=True)))
    dq = jnp.einsum("rhqk,rkhd->rqhd", ds, k, preferred_element_type=F32) * SCALE
    dk = jnp.einsum("rhqk,rqhd->rkhd", ds, q, preferred_element_type=F32) * SCALE
    dv = jnp.einsum("rhqk,rqhd->rkhd", bf(p), do, preferred_element_type=F32)
    dt = bf(jnp.stack([dq, dk, dv], 2)).reshape(r, t, 3 * H * HD)
    dn = mm_t(dt, w_qkv)
    dx, d_gain, d_bias = norm_bwd(dn, sv["nsave"], gain)
    pairs = dict(o=sv["o"], g2=g2, n=sv["n"], dt=dt)
    return dh2 + dx, (d_gain, d_bias), pairs


RB = 2


def _dot_nt(a, b):
    return lax.dot_general(a, b, (((1,), (1,)), ((), ())), preferred_element_type=F32)


def _dot_tn(a, b):
    return lax.dot_general(a, b, (((0,), (0,)), ((), ())), preferred_element_type=F32)


def _dot(a, b):
    return lax.dot_general(a, b, (((1,), (0,)), ((), ())), preferred_element_type=F32)


LO = 16
HI = 48


def _join(top, bottom, first):
    t = first.shape[0]
    mid = jnp.where(first[LO:HI], top[LO:HI], bottom[: HI - LO])
    return jnp.concatenate([top[:LO], mid, bottom[HI - LO :]], 0)


def _split(x, first):
    zero = jnp.zeros_like(x)
    return jnp.where(first, x, zero)[:HI], jnp.where(first, zero, x)[LO:]


def _probs(q, ka, kb, first):
    sa = _dot_nt(q[:HI], ka) * SCALE
    sb = _dot_nt(q[LO:], kb) * SCALE
    s = _join(sa, sb, first)
    top = jnp.max(s, -1, keepdims=True)
    e = jnp.exp(s - top)
    return e / jnp.sum(e, -1, keepdims=True)


def _fwd_kernel(slot_ref, cut_ref, q_ref, pool_ref, o_ref):
    i = pl.program_id(0)
    t = q_ref.shape[1]
    d = H * HD
    for j in range(RB):
        r = i * RB + j
        a = slot_ref[2 * r]
        b = slot_ref[2 * r + 1]
        first = lax.broadcasted_iota(jnp.int32, (t, 1), 0) < cut_ref[r]
        for h in range(H):
            cols = pl.ds(h * HD, HD)
            vcols = pl.ds(d + h * HD, HD)
            q = q_ref[j, :, cols]
            p = _probs(q, pool_ref[a, :, cols], pool_ref[b, :, cols], first).astype(BF16)
            pa, pb = _split(p, first)
            oa = _dot(pa, pool_ref[a, :, vcols])
            ob = _dot(pb, pool_ref[b, :, vcols])
            o = jnp.concatenate([oa[:LO], oa[LO:] + ob[: HI - LO], ob[HI - LO :]], 0)
            o_ref[j, :, cols] = o.astype(o_ref.dtype)


def _bwd_kernel(slot_ref, cut_ref, q_ref, do_ref, pool_ref, dq_ref, dpool_ref):
    i = pl.program_id(0)
    t = q_ref.shape[1]
    d = H * HD

    @pl.when(i == 0)
    def _():
        dpool_ref[...] = jnp.zeros_like(dpool_ref)

    for j in range(RB):
        r = i * RB + j
        a = slot_ref[2 * r]
        b = slot_ref[2 * r + 1]
        first = lax.broadcasted_iota(jnp.int32, (t, 1), 0) < cut_ref[r]
        for h in range(H):
            cols = pl.ds(h * HD, HD)
            vcols = pl.ds(d + h * HD, HD)
            q = q_ref[j, :, cols]
            do = do_ref[j, :, cols]
            ka = pool_ref[a, :, cols]
            kb = pool_ref[b, :, cols]
            va = pool_ref[a, :, vcols]
            vb = pool_ref[b, :, vcols]
            p = _probs(q, ka, kb, first)
            dp = _join(_dot_nt(do[:HI], va), _dot_nt(do[LO:], vb), first)
            ds = (p * (dp - jnp.sum(p * dp, -1, keepdims=True))).astype(BF16)
            dsa, dsb = _split(ds, first)
            dqa = _dot(dsa, ka)
            dqb = _dot(dsb, kb)
            dq = jnp.concatenate([dqa[:LO], dqa[LO:] + dqb[: HI - LO], dqb[HI - LO :]], 0) * SCALE
            dq_ref[j, :, cols] = dq.astype(dq_ref.dtype)
            pa, pb = _split(p.astype(BF16), first)
            dpool_ref[a, :, cols] += _dot_tn(dsa, q[:HI]) * SCALE
            dpool_ref[a, :, vcols] += _dot_tn(pa, do[:HI])
            dpool_ref[b, :, cols] += _dot_tn(dsb, q[LO:]) * SCALE
            dpool_ref[b, :, vcols] += _dot_tn(pb, do[LO:])


def cross_attention_fwd(qc, pool, slots, cuts):
    r, t, d = qc.shape
    spec = pltpu.PrefetchScalarGridSpec(
        num_scalar_prefetch=2,
        grid=(r // RB,),
        in_specs=[
            pl.BlockSpec((RB, t, d), lambda i, s, c: (i, 0, 0)),
            pl.BlockSpec(pool.shape, lambda i, s, c: (0, 0, 0)),
        ],
        out_specs=pl.BlockSpec((RB, t, d), lambda i, s, c: (i, 0, 0)),
    )
    flops = r * H * 4 * 2 * t * pool.shape[1] * HD
    return pl.pallas_call(
        _fwd_kernel,
        grid_spec=spec,
        out_shape=jax.ShapeDtypeStruct((r, t, d), BF16),
        compiler_params=pltpu.CompilerParams(
            dimension_semantics=("arbitrary",), vmem_limit_bytes=48 * 1024 * 1024
        ),
        cost_estimate=pl.CostEstimate(
            flops=flops,
            transcendentals=r * H * t * 2 * pool.shape[1],
            bytes_accessed=2 * qc.size * 2 + pool.size * 2,
        ),
    )(slots.reshape(-1), cuts, qc, pool)


def cross_attention_bwd(qc, doc, pool, slots, cuts):
    r, t, d = qc.shape
    spec = pltpu.PrefetchScalarGridSpec(
        num_scalar_prefetch=2,
        grid=(r // RB,),
        in_specs=[
            pl.BlockSpec((RB, t, d), lambda i, s, c: (i, 0, 0)),
            pl.BlockSpec((RB, t, d), lambda i, s, c: (i, 0, 0)),
            pl.BlockSpec(pool.shape, lambda i, s, c: (0, 0, 0)),
        ],
        out_specs=[
            pl.BlockSpec((RB, t, d), lambda i, s, c: (i, 0, 0)),
            pl.BlockSpec(pool.shape, lambda i, s, c: (0, 0, 0)),
        ],
    )
    flops = r * H * 10 * 2 * t * pool.shape[1] * HD
    return pl.pallas_call(
        _bwd_kernel,
        grid_spec=spec,
        out_shape=(
            jax.ShapeDtypeStruct((r, t, d), BF16),
            jax.ShapeDtypeStruct(pool.shape, F32),
        ),
        compiler_params=pltpu.CompilerParams(
            dimension_semantics=("arbitrary",), vmem_limit_bytes=60 * 1024 * 1024
        ),
        cost_estimate=pl.CostEstimate(
            flops=flops,
            transcendentals=r * H * t * 2 * pool.shape[1],
            bytes_accessed=3 * qc.size * 2 + pool.size * 2 + pool.size * 4,
        ),
    )(slots.reshape(-1), cuts, qc, doc, pool)


def cross_fwd(h2, slots, cuts, pool, gain, bias, wq, wo):
    y, csave = norm_fwd(h2, gain, bias)
    c = bf(y)
    qc = bf(mm(c, wq))
    oc = cross_attention_fwd(qc, pool, slots, cuts)
    h3 = h2 + mm(oc, wo)
    return h3, dict(csave=csave, c=c, qc=qc, oc=oc)


def cross_bwd(dh3, sv, slots, cuts, pool, gain, wq, wo):
    g3 = bf(dh3)
    doc = bf(mm_t(g3, wo))
    dqc, dpool = cross_attention_bwd(sv["qc"], doc, pool, slots, cuts)
    dc = mm_t(dqc, wq)
    dx, d_gain, d_bias = norm_bwd(dc, sv["csave"], gain)
    pairs = dict(oc=sv["oc"], g3=g3, c=sv["c"], dqc=dqc)
    return dh3 + dx, (d_gain, d_bias), pairs, dpool


def gelu(z):
    return jax.nn.gelu(z, approximate=False)


def ffn_fwd(h3, gain, bias, w_up, b_up, w_down, b_down):
    y, usave = norm_fwd(h3, gain, bias)
    u = bf(y)
    z = mm(u, w_up) + b_up
    f = bf(gelu(z))
    out = h3 + (mm(f, w_down) + b_down)
    return out, dict(usave=usave, u=u, z=z, f=f)


def ffn_bwd(gout, sv, gain, w_up, w_down):
    gb = bf(gout)
    df = mm_t(gb, w_down)
    _, pull = jax.vjp(gelu, sv["z"])
    dz = bf(pull(df)[0])
    du = mm_t(dz, w_up)
    dx, d_gain, d_bias = norm_bwd(du, sv["usave"], gain)
    pairs = dict(f=sv["f"], gb=gb, u=sv["u"], dz=dz)
    return gout + dx, (d_gain, d_bias), pairs


def chip_cycle(mesh):
    n_dp = mesh.shape["dp"]
    plane = mesh.devices.reshape(-1, n_dp)[0]
    try:
        chips = {}
        for i, dev in enumerate(plane):
            chips.setdefault(tuple(dev.coords), []).append(i)
    except AttributeError:
        return list(range(n_dp))
    keys = sorted(chips)
    if len(keys) < 3:
        return [i for k in keys for i in sorted(chips[k])]
    near = {
        k: [j for j in keys if sum(abs(a - b) for a, b in zip(k, j)) == 1] for k in keys
    }
    path, seen, budget = [keys[0]], {keys[0]}, [200000]

    def walk():
        budget[0] -= 1
        if budget[0] < 0:
            return False
        if len(path) == len(keys):
            return keys[0] in near[path[-1]]
        options = sorted(
            (j for j in near[path[-1]] if j not in seen),
            key=lambda j: sum(1 for n in near[j] if n not in seen),
        )
        for j in options:
            path.append(j)
            seen.add(j)
            if walk():
                return True
            path.pop()
            seen.discard(j)
        return False

    if not walk():
        return list(range(n_dp))
    return [i for k in path for i in sorted(chips[k])]


def ring_reduce_scatter(packed, plane, cycle, dp_index):
    n = len(cycle)
    n_dp = packed.shape[0]
    axes = ("section", "dp")
    fwd = [(plane * n_dp + cycle[i], plane * n_dp + cycle[(i + 1) % n]) for i in range(n)]
    bwd = [(b, a) for a, b in fwd]
    where_in = [0] * n
    for i, d in enumerate(cycle):
        where_in[d] = i
    order = jnp.array(cycle * 2, jnp.int32)
    half = packed.shape[-1] // 2
    cw, ccw = packed[..., :half], packed[..., half:]
    p = jnp.array(where_in, jnp.int32)[dp_index]

    def take(a, idx):
        return lax.dynamic_index_in_dim(a, order[idx % n], 0, keepdims=False)

    send_c, send_w = take(cw, p + n - 1), take(ccw, p + 1)
    for step in range(n - 1):
        got_c = lax.ppermute(send_c, axes, fwd)
        got_w = lax.ppermute(send_w, axes, bwd)
        acc_c = got_c.astype(F32) + take(cw, p + 2 * n - step - 2).astype(F32)
        acc_w = got_w.astype(F32) + take(ccw, p + step + 2).astype(F32)
        send_c, send_w = bf(acc_c), bf(acc_w)
    return jnp.concatenate([acc_c, acc_w], -1)


def pack_rows(arrays, n, rows):
    pieces = [bf(a).reshape(n, rows, -1) for a in arrays if a.ndim == 2]
    vecs = jnp.concatenate([bf(a).reshape(n, -1) for a in arrays if a.ndim == 1], 1)
    width = -(-vecs.shape[1] // rows)
    vecs = jnp.pad(vecs, ((0, 0), (0, width * rows - vecs.shape[1]))).reshape(n, rows, width)
    pieces.append(vecs)
    cols = sum(x.shape[-1] for x in pieces)
    target = -(-cols // 256) * 256
    pieces.append(jnp.zeros((n, rows, target - cols), BF16))
    return jnp.concatenate(pieces, -1)


def unpack_row(block, arrays, n, rows):
    out, at = [], 0
    mats = {}
    for i, a in enumerate(arrays):
        if a.ndim == 2:
            width = a.size // n // rows
            mats[i] = block[:, at : at + width].reshape((a.shape[0] // n,) + a.shape[1:])
            at += width
    vec_total = sum(a.size // n for a in arrays if a.ndim == 1)
    width = -(-vec_total // rows)
    flat = block[:, at : at + width].reshape(-1)
    vat = 0
    for i, a in enumerate(arrays):
        if a.ndim == 2:
            out.append(mats[i])
        else:
            size = a.size // n
            out.append(flat[vat : vat + size])
            vat += size
    return out


def per_device(
    cycle,
    inputs,
    cotangent,
    images,
    seg_ids,
    row_block,
    seg_image,
    ln1_gain,
    ln1_bias,
    w_qkv,
    w_out,
    ln2_gain,
    ln2_bias,
    w_up,
    b_up,
    w_down,
    b_down,
    lnc_gain,
    lnc_bias,
    wq_cross,
    wkv_cross,
    wo_cross,
):
    up = lax.axis_index("section") == 1
    low = jnp.logical_not(up)
    dp_index = lax.axis_index("dp")
    n_dp = lax.axis_size("dp")
    rows = inputs.shape[0]
    rc = rows // MICRO
    g1, b1, wqkv, wout = ln1_gain[0], ln1_bias[0], w_qkv[0], w_out[0]
    g2, b2, wup, bup, wdown, bdown = ln2_gain[0], ln2_bias[0], w_up[0], b_up[0], w_down[0], b_down[0]
    n_img = n_dp * images.shape[0]

    first_half = lax.ppermute(images[0], "section", [(0, 1)])
    full_image = jnp.concatenate([first_half, images[0]], 0)

    def make_kv(img):
        return bf(mm(img, wkv_cross))

    kv_own = run_on(up, make_kv, full_image)
    ring_up = [(i, (i + 1) % n_dp) for i in range(n_dp)]
    ring_down = [((i + 1) % n_dp, i) for i in range(n_dp)]
    kv_prev = lax.ppermute(kv_own, "dp", ring_up)
    kv_next = lax.ppermute(kv_own, "dp", ring_down)
    pool = jnp.stack([kv_prev, kv_own, kv_next], 0)
    img_tok = pool.shape[1]

    first_img = (row_block[:, None] + seg_image) % n_img
    slot = (first_img - dp_index + 1 + n_img) % n_img
    cut_all = jnp.sum((seg_ids == 0).astype(jnp.int32), 1)

    def chunk(a, m):
        return a[m * rc : (m + 1) * rc]

    x = inputs.astype(F32)

    def lower_fwd(hid, seg):
        h2, s_self = self_fwd(hid, seg, g1, b1, wqkv, wout)
        out, s_ffn = ffn_fwd(h2, g2, b2, wup, bup, wdown, bdown)
        return out, (s_self, s_ffn)

    def upper_fwd(sent, seg, slots, cuts, pool):
        hid = sent.astype(F32)
        h2, s_self = self_fwd(hid, seg, g1, b1, wqkv, wout)
        h3, s_cross = cross_fwd(h2, slots, cuts, pool, lnc_gain, lnc_bias, wq_cross, wo_cross)
        out, s_ffn = ffn_fwd(h3, g2, b2, wup, bup, wdown, bdown)
        return out, (s_self, s_cross, s_ffn)

    low_out, low_saved, sent = [], [], []
    for m in range(MICRO):
        x_m = chunk(x, m)
        if m > 0:
            x_m, low_out[-1] = lax.optimization_barrier((x_m, low_out[-1]))
        out, saved = run_on(low, lower_fwd, x_m, chunk(seg_ids, m))
        low_out.append(out)
        low_saved.append(saved)
        sent.append(lax.ppermute(bf(out), "section", [(0, 1)]))
    up_out, up_saved = [], []
    for m in range(MICRO):
        arriving = sent[m]
        if m > 0:
            arriving, up_out[-1] = lax.optimization_barrier((arriving, up_out[-1]))
        out, saved = run_on(
            up, upper_fwd, arriving, chunk(seg_ids, m), chunk(slot, m), chunk(cut_all, m), pool
        )
        up_out.append(out)
        up_saved.append(saved)

    cot = cotangent[0].astype(F32)

    def upper_bwd(gout, saved, slots, cuts, pool):
        s_self, s_cross, s_ffn = saved
        dh3, ln2g, pf = ffn_bwd(gout, s_ffn, g2, wup, wdown)
        dh2, lncg, pc, dpool = cross_bwd(dh3, s_cross, slots, cuts, pool, lnc_gain, wq_cross, wo_cross)
        dh, ln1g, ps = self_bwd(dh2, s_self, g1, wqkv, wout)
        return dh, (ln1g, ln2g, lncg), (ps, pf, pc), dpool

    up_grad, up_small, up_pairs = [], [], []
    returned = []
    pool_grad = None
    for m in range(MICRO):
        cot_m = chunk(cot, m)
        if m > 0:
            cot_m, up_grad[-1] = lax.optimization_barrier((cot_m, up_grad[-1]))
        dh, small, pairs, dpool = run_on(
            up, upper_bwd, cot_m, up_saved[m], chunk(slot, m), chunk(cut_all, m), pool
        )
        up_grad.append(dh)
        up_small.append(small)
        up_pairs.append(pairs)
        pool_grad = dpool if pool_grad is None else pool_grad + dpool
        returned.append(lax.ppermute(bf(dh), "section", [(1, 0)]))

    def cat(name_path, pairs_list):
        return jnp.concatenate([name_path(p) for p in pairs_list], 0)

    def layer_weight_grads(pairs_list):
        ps = lambda i, k: cat(lambda p: p[i][k], pairs_list)
        d_wqkv = outer(ps(0, "n"), ps(0, "dt"))
        d_wout = outer(ps(0, "o"), ps(0, "g2"))
        d_wup = outer(ps(1, "u"), ps(1, "dz"))
        d_wdown = outer(ps(1, "f"), ps(1, "gb"))
        d_bup = jnp.sum(ps(1, "dz").astype(F32), (0, 1))
        d_bdown = jnp.sum(ps(1, "gb").astype(F32), (0, 1))
        return d_wqkv, d_wout, d_wup, d_bup, d_wdown, d_bdown

    def upper_wgrads(pairs_list):
        layer = layer_weight_grads(pairs_list)
        ps = lambda k: cat(lambda p: p[2][k], pairs_list)
        d_wq = outer(ps("c"), ps("dqc"))
        d_wo = outer(ps("oc"), ps("g3"))
        return layer, (d_wq, d_wo)

    up_w, cross_w = run_on(up, upper_wgrads, up_pairs)

    parts = bf(pool_grad)
    from_next = lax.ppermute(parts[0], "dp", ring_down)
    from_prev = lax.ppermute(parts[2], "dp", ring_up)
    kv_grad = bf(parts[1].astype(F32) + from_next.astype(F32) + from_prev.astype(F32))

    def image_side(kvg, img):
        ig = jnp.einsum("te,de->td", kvg, wkv_cross, preferred_element_type=F32)
        dw = jnp.einsum("td,te->de", img, kvg, preferred_element_type=F32)
        return ig, dw

    image_grad_full, d_wkv = run_on(up, image_side, kv_grad, full_image)
    half = images.shape[1]
    ig_first = lax.ppermute(image_grad_full[:half], "section", [(1, 0)])
    image_grad = jnp.where(up, image_grad_full[half:], ig_first)[None]

    def tree_sum(xs):
        total = xs[0]
        for v in xs[1:]:
            total = jax.tree.map(jnp.add, total, v)
        return total

    def layer_list(lw, sm):
        d_wqkv, d_wout, d_wup, d_bup, d_wdown, d_bdown = lw
        return [d_wqkv, d_wout, d_wup, d_wdown, sm[0][0], sm[0][1], sm[1][0], sm[1][1], d_bup, d_bdown]

    up_sm = tree_sum(up_small)
    a_list = layer_list(up_w, up_sm) + [cross_w[0], cross_w[1], d_wkv, up_sm[2][0], up_sm[2][1]]
    block_rows = wqkv.shape[0] // n_dp
    a_packed = pack_rows(a_list, n_dp, block_rows)

    def lower_bwd(gout, saved):
        s_self, s_ffn = saved
        dh3, ln2g, pf = ffn_bwd(gout, s_ffn, g2, wup, wdown)
        dh, ln1g, ps = self_bwd(dh3, s_self, g1, wqkv, wout)
        return dh, (ln1g, ln2g), (ps, pf)

    low_grad, low_small, low_pairs = [], [], []
    for m in range(MICRO):
        gout = chunk(cot, m) + returned[m].astype(F32)
        if m == 0:
            pass
        else:
            gout, low_grad[-1] = lax.optimization_barrier((gout, low_grad[-1]))
        dh, small, pairs = run_on(low, lower_bwd, gout, low_saved[m])
        low_grad.append(dh)
        low_small.append(small)
        low_pairs.append(pairs)

    low_w = run_on(low, layer_weight_grads, low_pairs)
    a_packed, low_w = lax.optimization_barrier((a_packed, low_w))
    low_sm = tree_sum(low_small)
    b_list = layer_list(low_w, low_sm)
    b_packed = pack_rows(b_list, n_dp, block_rows)
    a_row = ring_reduce_scatter(a_packed, 1, cycle, dp_index)
    b_row = ring_reduce_scatter(b_packed, 0, cycle, dp_index)
    a_got = unpack_row(a_row, a_list, n_dp, block_rows)
    b_got = unpack_row(b_row, b_list, n_dp, block_rows)

    cross_out = a_got[10:]
    cross_copy = lax.ppermute(cross_out, "section", [(1, 0)])
    cross_out = [jnp.where(up, a, c) for a, c in zip(cross_out, cross_copy)]

    activations = jnp.where(
        up, jnp.concatenate(up_out, 0), jnp.concatenate(low_out, 0)
    )[None]
    back_grads = jnp.where(
        up, jnp.concatenate(up_grad, 0), jnp.concatenate(low_grad, 0)
    )[None]
    layer = [jnp.where(up, a, b)[None] for a, b in zip(a_got[:10], b_got)]
    big, small = layer[:4], [v.reshape(1, -1) for v in layer[4:]]
    d_wq, d_wo, d_wkv_sh, lnc_g, lnc_b = cross_out

    return (
        activations,
        back_grads,
        image_grad,
        small[0],
        small[1],
        big[0],
        big[1],
        small[2],
        small[3],
        big[2],
        small[4],
        big[3],
        small[5],
        lnc_g,
        lnc_b,
        d_wq,
        d_wkv_sh,
        d_wo,
    )


def solution(mesh):
    placed = (
        P("dp", None, None),
        P("section", "dp", None, None),
        P("dp", "section", None),
        P("dp", None),
        P("dp"),
        P("dp", None),
        P("section", None),
        P("section", None),
        P("section", None, None),
        P("section", None, None),
        P("section", None),
        P("section", None),
        P("section", None, None),
        P("section", None),
        P("section", None, None),
        P("section", None),
        P(),
        P(),
        P(),
        P(),
        P(),
    )
    return jax.shard_map(
        partial(per_device, chip_cycle(mesh)),
        mesh=mesh,
        in_specs=placed,
        out_specs=(
            P("section", "dp", None, None),
            P("section", "dp", None, None),
            P("dp", "section", None),
            P("section", "dp"),
            P("section", "dp"),
            P("section", "dp", None),
            P("section", "dp", None),
            P("section", "dp"),
            P("section", "dp"),
            P("section", "dp", None),
            P("section", "dp"),
            P("section", "dp", None),
            P("section", "dp"),
            P("dp"),
            P("dp"),
            P("dp", None),
            P("dp", None),
            P("dp", None),
        ),
        check_vma=False,
    )
```
